256 devices in a mesh: mom: 32 (over x, z), tm: 8 (over y, core).
Axes of the slice: x: 4, y: 4, z: 8, core: 2. Of those that a mesh axis runs over, the one named last changes fastest.
Arguments:
- source: float32 [2, 32, 2048, 512], P(None, 'mom', 'tm'), may hold values from -6 to 6
- inverse_diag: float32 [2, 32, 8, 256, 256], P(None, 'mom', 'tm'), may hold values from -0.25 to 0.25
- coupling: float32 [2, 32, 8, 256, 256], P(None, 'mom', 'tm'), may hold values from -0.21875 to 0.21875
- pair_moms: int32 [32, 8, 3], replicated, may hold values from 0 to 31, as said below
- pair_count: int32 [32], replicated, may hold values from 1 to 8
- pair_weight: int32 [32, 8], replicated, may hold values from 0 to 15
- vertex: float32 [16], replicated, may hold values from 0.02 to 0.2
Outputs:
- solved: bfloat16 [2, 32, 2048, 512], P(None, 'mom', 'tm')
- sigma: float32 [2, 32, 2048, 512], P(None, 'mom', 'tm')
The draws below stay inside these ranges and needn't reach their ends.
Inputs may be any that keep to these rules, and one draw needn't show every extreme that they name: `pair_moms`: entry (k, s) is ((k - q) mod 32, p, (p + q) mod 32) for some q and p.
All inputs are finite; a program needn't handle non-finite values.
Results may differ from the reference program's by a relative error of at most 0.0059.
Values may be sent and summed in bfloat16 or wider, within the bound.
A program may use at most 64 MiB of HBM per device.

```python
import math
import jax
import jax.numpy as jnp
from jax import lax

TB = 256
COLS = 512
PAIRS = 8
NW = 16
K = 32
NB = 8
TIMES = 2048


def draw_pair_moms(key, part):
    base = jax.random.fold_in(key, 11)
    key_transfer, key_inner = jax.random.split(base)
    transfer = jax.random.randint(key_transfer, (K, PAIRS), 0, K)
    inner = jax.random.randint(key_inner, (K, PAIRS), 0, K)
    inner = inner.at[0, 0].set(0).at[1, 0].set(K - 1)
    owner = jnp.arange(K, dtype=jnp.int32)[:, None]
    return jnp.stack([(owner - transfer) % K, inner, (inner + transfer) % K], -1).astype(jnp.int32)


def draw_pair_count(key, part):
    base = jax.random.fold_in(key, 23)
    key_raw, key_hot = jax.random.split(base)
    raw = jax.random.randint(key_raw, (K,), 1, PAIRS + 1)
    hot_index = jax.random.randint(key_hot, (), 0, K)
    raw = raw.at[hot_index].set(PAIRS).at[(hot_index + 1) % K].set(1)
    return raw.astype(jnp.int32)


def with_ends(drawn, stream_key, low, top_value):
    extent = drawn.shape
    spot = [jax.random.randint(jax.random.fold_in(stream_key, axis), (), 0, extent[axis]) for axis in range(len(extent))]
    drawn = drawn.at[tuple(spot)].set(low)
    longest = extent.index(max(extent))
    spot[longest] = (spot[longest] + 1) % extent[longest]
    return drawn.at[tuple(spot)].set(top_value)


def block_levels(rng, extent, cuts, smallest, largest):
    factor_of = 1.0
    for axis_at, blocks in cuts:
        draws = jax.random.uniform(jax.random.fold_in(jax.random.fold_in(rng, 6), axis_at), (blocks,), jnp.float32, smallest / len(cuts), largest / len(cuts))
        factor_of = factor_of * jnp.repeat(jnp.exp(draws), extent[axis_at] // blocks).reshape((-1,) + (1,) * (len(extent) - 1 - axis_at))
    return factor_of


def centred(stream_key, extent, spread, bound, shards=(), held_as=jnp.bfloat16):
    array = spread * jax.random.normal(stream_key, extent, jnp.float32)
    if shards:
        array = array * block_levels(stream_key, extent, shards, -0.22, 0.18)
    return jnp.clip(array, -bound, bound).astype(held_as)


def setup_inputs(seed: int = 0) -> dict:
    splits = jax.random.split(jax.random.key(seed), 8)
    return {
        "source": centred(splits[0], (2, K, TIMES, COLS), 1.0, 6.0, ((1, 32), (2, 8)), jnp.float32),
        "inverse_diag": centred(splits[1], (2, K, NB, TB, TB), (2 * TB) ** -0.5, 0.25, ((1, 32), (2, 8)), jnp.float32),
        "coupling": centred(splits[2], (2, K, NB, TB, TB), (3 * TB) ** -0.5, 0.21875, ((1, 32), (2, 8)), jnp.float32),
        "pair_moms": draw_pair_moms(jax.random.fold_in(splits[7], 71), 0),
        "pair_count": draw_pair_count(jax.random.fold_in(splits[7], 71), 0),
        "pair_weight": with_ends(jax.random.randint(splits[5], (K, PAIRS), 0, NW), jax.random.fold_in(splits[5], 1), 0, NW - 1).astype(jnp.int32),
        "vertex": jnp.clip(jnp.exp(jax.random.uniform(splits[6], (NW,), jnp.float32, math.log(0.02), math.log(0.2))), 0.02, 0.2),
    }


def complex_mat(left, right):
    def real_mat(first, second):
        return jnp.einsum("kij,kjc->kic", first, second, precision=lax.Precision.HIGHEST)
    real_part = real_mat(left[0], right[0]) - real_mat(left[1], right[1])
    imag_part = real_mat(left[0], right[1]) + real_mat(left[1], right[0])
    return jnp.stack([real_part, imag_part])


def self_energy(greens, triples, live_count, weight_index, vertex):
    slots = triples.shape[1]
    entries = vertex.shape[0]
    table = jnp.sum(jnp.where(weight_index[..., None] == jnp.arange(entries, dtype=jnp.int32), vertex, 0.0), -1)
    live_mask = jnp.arange(slots, dtype=jnp.int32)[None, :] < live_count[:, None]
    scaled = jnp.where(live_mask, table, 0.0)
    total = jnp.zeros((2, triples.shape[0], greens.shape[2], greens.shape[3]), jnp.float32)
    for pair_slot in range(slots):
        first = jnp.take(greens, triples[:, pair_slot, 0], axis=1).astype(jnp.float32)
        second = jnp.take(greens, triples[:, pair_slot, 1], axis=1).astype(jnp.float32)
        third = jnp.take(greens, triples[:, pair_slot, 2], axis=1).astype(jnp.float32)
        prod_re = first[0] * second[0] - first[1] * second[1]
        prod_im = first[0] * second[1] + first[1] * second[0]
        term_re = prod_re * third[0] + prod_im * third[1]
        term_im = prod_im * third[0] - prod_re * third[1]
        factor = scaled[:, pair_slot][:, None, None]
        total = total + factor * jnp.stack([term_re, term_im])
    return total


def reference(source, inverse_diag, coupling, pair_moms, pair_count, pair_weight, vertex):
    driving = jnp.moveaxis(source.reshape(2, K, NB, TB, COLS), 2, 0)
    inverses = jnp.moveaxis(inverse_diag, 2, 0)
    couplings = jnp.moveaxis(coupling, 2, 0)

    def advance(previous, blocks):
        inverse, coupled, forcing = blocks
        current = complex_mat(inverse, forcing + complex_mat(coupled, previous))
        return current, current

    start_state = jnp.zeros((2, K, TB, COLS), jnp.float32)
    _, solved_blocks = lax.scan(advance, start_state, (inverses, couplings, driving))
    greens = jnp.moveaxis(solved_blocks, 0, 2).reshape(2, K, TIMES, COLS)
    solved = greens.astype(jnp.bfloat16)
    sigma = self_energy(solved, pair_moms, pair_count, pair_weight, vertex)
    return solved, sigma
```

```python
import jax
import jax.numpy as jnp
from jax import lax
from jax.experimental import pallas as pl
from jax.experimental.pallas import tpu as pltpu
from jax.sharding import PartitionSpec as P

MESH = pl.DeviceIdType.MESH
LANES = 128


def split(value):
    high = value.astype(jnp.bfloat16)
    return high, (value - high.astype(jnp.float32)).astype(jnp.bfloat16)


def dot(left, right):
    return jnp.dot(left, right, preferred_element_type=jnp.float32)


def complex_times(high, low, value):
    rows, width = high.shape[1], value.shape[1] // 2
    value_high, value_low = split(value)
    both = dot(high, value_high) + (dot(high, value_low) + dot(low, value_high))
    real = both[:rows, :width] - both[rows:, width:]
    imag = both[:rows, width:] + both[rows:, :width]
    return real, imag


def kernel(
    moms, counts, weights, vertex, source_hbm, inverse_hbm, coupling_hbm,
    solved, sigma,
    source, inverse, coupling, left_high, left_low, step_high, step_low, driven, entering, greens,
    outbox, inbox, wide, formed, returned,
    load_sem, hop_send, hop_recv, in_send, in_recv, out_send, out_recv,
):
    n_mom, n_tm = lax.axis_size("mom"), lax.axis_size("tm")
    me, turn = lax.axis_index("mom"), lax.axis_index("tm")
    rows, chunks = driven.shape[1], driven.shape[0]
    share = rows // n_mom
    slots = moms.shape[1]

    loads = [
        pltpu.make_async_copy(inverse_hbm.at[:, 0, 0], inverse, load_sem.at[0]),
        pltpu.make_async_copy(coupling_hbm.at[:, 0, 0], coupling, load_sem.at[1]),
        pltpu.make_async_copy(source_hbm.at[:, 0], source, load_sem.at[2]),
    ]
    for load in loads:
        load.start()

    barrier = pltpu.get_barrier_semaphore()

    def greet(step, carry):
        other = lax.rem(me + step, n_mom)
        pl.semaphore_signal(barrier, inc=1, device_id={"mom": other, "tm": turn}, device_id_type=MESH)
        return carry

    lax.fori_loop(1, n_mom, greet, 0)

    for other in (lax.rem(turn + 1, n_tm), lax.rem(turn + n_tm - 1, n_tm)):
        pl.semaphore_signal(barrier, inc=1, device_id={"mom": me, "tm": other}, device_id_type=MESH)

    for load in loads:
        load.wait()

    for part in range(2):
        high, low = split(inverse[part])
        left_high[part * rows:(part + 1) * rows, :] = high
        left_low[part * rows:(part + 1) * rows, :] = low
    step = complex_times(
        left_high[...], left_low[...], jnp.concatenate([coupling[0], coupling[1]], axis=1)
    )
    for part in range(2):
        high, low = split(step[part])
        step_high[part * rows:(part + 1) * rows, :] = high
        step_low[part * rows:(part + 1) * rows, :] = low

    def drive(chunk, carry):
        columns = pl.ds(pl.multiple_of(chunk * LANES, LANES), LANES)
        forcing = jnp.concatenate([source[0, :, columns], source[1, :, columns]], axis=1)
        real, imag = complex_times(left_high[...], left_low[...], forcing)
        driven[chunk] = jnp.concatenate([real, imag], axis=1)
        return carry

    lax.fori_loop(0, chunks, drive, 0)

    pl.semaphore_wait(barrier, n_mom + 1)

    def hop(chunk):
        return pltpu.make_async_remote_copy(
            src_ref=greens.at[chunk], dst_ref=entering.at[chunk],
            send_sem=hop_send.at[chunk], recv_sem=hop_recv.at[chunk],
            device_id={"mom": me, "tm": lax.rem(turn + 1, n_tm)}, device_id_type=MESH,
        )

    def scatter(chunk, other):
        return pltpu.make_async_remote_copy(
            src_ref=outbox.at[chunk, other], dst_ref=inbox.at[chunk, me],
            send_sem=in_send.at[chunk], recv_sem=in_recv.at[chunk],
            device_id={"mom": other, "tm": turn}, device_id_type=MESH,
        )

    def collect(chunk, other):
        return pltpu.make_async_remote_copy(
            src_ref=formed.at[chunk, other], dst_ref=returned.at[chunk, me],
            send_sem=out_send.at[chunk], recv_sem=out_recv.at[chunk],
            device_id={"mom": other, "tm": turn}, device_id_type=MESH,
        )

    def settle(buffer, chunk, sem):
        block = buffer.at[chunk, pl.ds(0, n_mom - 1)]
        pltpu.make_async_copy(block, block, sem.at[chunk]).wait()

    def advance(chunk):
        @pl.when(turn == 0)
        def _():
            greens[chunk] = driven[chunk]

        @pl.when(turn > 0)
        def _():
            hop(chunk).wait_recv()
            real, imag = complex_times(step_high[...], step_low[...], entering[chunk])
            greens[chunk] = driven[chunk] + jnp.concatenate([real, imag], axis=1)

        @pl.when(turn < n_tm - 1)
        def _():
            hop(chunk).start()

        value = greens[chunk]
        real, imag = value[:, :LANES], value[:, LANES:]
        packed = jnp.concatenate(
            [real.reshape(n_mom, share, LANES), imag.reshape(n_mom, share, LANES)], axis=1
        )
        outbox[chunk] = packed.astype(jnp.bfloat16)
        inbox[chunk, me] = outbox[chunk, me]

        def send(step, carry):
            scatter(chunk, lax.rem(me + step, n_mom)).start()
            return carry

        lax.fori_loop(1, n_mom, send, 0)
        columns = pl.ds(pl.multiple_of(chunk * LANES, LANES), LANES)
        solved[0, 0, :, columns] = real.astype(jnp.bfloat16)
        solved[1, 0, :, columns] = imag.astype(jnp.bfloat16)

    def form(chunk):
        settle(inbox, chunk, in_recv)
        wide[...] = inbox[chunk].astype(jnp.float32)

        def one(step, carry):
            mom = lax.rem(me + step, n_mom)
            live = counts[mom]
            total_real = jnp.zeros((share, LANES), jnp.float32)
            total_imag = jnp.zeros((share, LANES), jnp.float32)
            for slot in range(slots):
                first, second, third = (wide[moms[place, slot, mom]] for place in range(3))
                factor = jnp.where(slot < live, vertex[weights[slot, mom]], 0.0)
                ar, ai = first[:share], first[share:]
                br, bi = second[:share], second[share:]
                cr, ci = third[:share], third[share:]
                prod_real = ar * br - ai * bi
                prod_imag = ar * bi + ai * br
                total_real = total_real + factor * (prod_real * cr + prod_imag * ci)
                total_imag = total_imag + factor * (prod_imag * cr - prod_real * ci)
            formed[chunk, mom] = jnp.concatenate([total_real, total_imag], axis=0).astype(jnp.bfloat16)

            @pl.when(step < n_mom)
            def _():
                collect(chunk, mom).start()

            return carry

        lax.fori_loop(1, n_mom + 1, one, 0)
        returned[chunk, me] = formed[chunk, me]

    def finish(chunk):
        settle(returned, chunk, out_recv)
        value = returned[chunk].astype(jnp.float32)
        columns = pl.ds(pl.multiple_of(chunk * LANES, LANES), LANES)
        sigma[0, 0, :, columns] = value[:, :share].reshape(rows, LANES)
        sigma[1, 0, :, columns] = value[:, share:].reshape(rows, LANES)

    def stage(step, carry):
        @pl.when(step < chunks)
        def _():
            advance(step)

        @pl.when((step >= 1) & (step < chunks + 1))
        def _():
            form(step - 1)

        @pl.when(step >= 2)
        def _():
            finish(step - 2)

        return carry

    lax.fori_loop(0, chunks + 2, stage, 0)

    def close(chunk, carry):
        @pl.when(turn < n_tm - 1)
        def _():
            hop(chunk).wait_send()

        settle(outbox, chunk, in_send)
        settle(formed, chunk, out_send)
        return carry

    lax.fori_loop(0, chunks, close, 0)


def local(source, inverse_diag, coupling, pair_moms, pair_count, pair_weight, vertex):
    rows, columns = source.shape[2], source.shape[3]
    n_mom = lax.axis_size("mom")
    chunks, share = columns // LANES, rows // n_mom
    f32, bf16 = jnp.float32, jnp.bfloat16
    smem = pl.BlockSpec(memory_space=pltpu.SMEM)
    vmem = pl.BlockSpec(memory_space=pltpu.VMEM)
    hbm = pl.BlockSpec(memory_space=pl.ANY)
    piece = (chunks, n_mom, 2 * share, LANES)
    sems = pltpu.SemaphoreType.DMA((chunks,))
    return pl.pallas_call(
        kernel,
        out_shape=(
            jax.ShapeDtypeStruct(source.shape, bf16),
            jax.ShapeDtypeStruct(source.shape, f32),
        ),
        in_specs=[smem] * 4 + [hbm] * 3,
        out_specs=(vmem, vmem),
        scratch_shapes=[
            pltpu.VMEM((2, rows, columns), f32),
            pltpu.VMEM((2, rows, rows), f32),
            pltpu.VMEM((2, rows, rows), f32),
            pltpu.VMEM((2 * rows, rows), bf16),
            pltpu.VMEM((2 * rows, rows), bf16),
            pltpu.VMEM((2 * rows, rows), bf16),
            pltpu.VMEM((2 * rows, rows), bf16),
            pltpu.VMEM((chunks, rows, 2 * LANES), f32),
            pltpu.VMEM((chunks, rows, 2 * LANES), f32),
            pltpu.VMEM((chunks, rows, 2 * LANES), f32),
            pltpu.VMEM(piece, bf16),
            pltpu.VMEM(piece, bf16),
            pltpu.VMEM(piece[1:], f32),
            pltpu.VMEM(piece, bf16),
            pltpu.VMEM(piece, bf16),
            pltpu.SemaphoreType.DMA((3,)),
            sems, sems, sems, sems, sems, sems,
        ],
        compiler_params=pltpu.CompilerParams(
            collective_id=0, has_side_effects=True, vmem_limit_bytes=32 << 20
        ),
    )(
        jnp.transpose(pair_moms, (2, 1, 0)), pair_count, jnp.transpose(pair_weight, (1, 0)), vertex,
        source, inverse_diag, coupling,
    )


def solution(mesh):
    return jax.shard_map(
        local,
        mesh=mesh,
        in_specs=(
            P(None, "mom", "tm", None),
            P(None, "mom", "tm", None, None),
            P(None, "mom", "tm", None, None),
            P(),
            P(),
            P(),
            P(),
        ),
        out_specs=(P(None, "mom", "tm", None), P(None, "mom", "tm", None)),
        check_vma=False,
    )
```

```python
import jax
import jax.numpy as jnp
from jax import lax
from jax.experimental import pallas as pl
from jax.experimental.pallas import tpu as pltpu
from jax.sharding import PartitionSpec as P

MESH = pl.DeviceIdType.MESH
LANES = 128


def split(value):
    high = value.astype(jnp.bfloat16)
    return high, (value - high.astype(jnp.float32)).astype(jnp.bfloat16)


def dot(left, right):
    return jnp.dot(left, right, preferred_element_type=jnp.float32)


def complex_times(high, low, value):
    rows, width = high.shape[1], value.shape[1] // 2
    value_high, value_low = split(value)
    both = dot(high, value_high) + (dot(high, value_low) + dot(low, value_high))
    real = both[:rows, :width] - both[rows:, width:]
    imag = both[:rows, width:] + both[rows:, :width]
    return real, imag


def kernel(
    moms_hbm, counts_hbm, weights_hbm, vertex_hbm, source_hbm, inverse_hbm, coupling_hbm,
    solved_hbm, sigma_hbm,
    moms, counts, weights, vertex, source, inverse, coupling, left_high, left_low, step_high, step_low, driven, entering, greens,
    outbox, inbox, wide, formed, returned, solved, sigma,
    load_sem, store_sem, hop_send, hop_recv, in_send, in_recv, out_send, out_recv,
):
    n_mom, n_tm = lax.axis_size("mom"), lax.axis_size("tm")
    me, turn = lax.axis_index("mom"), lax.axis_index("tm")
    rows, chunks = driven.shape[1], driven.shape[0]
    share = rows // n_mom
    slots = moms.shape[1]

    loads = [
        pltpu.make_async_copy(here, there, load_sem.at[place])
        for place, (here, there) in enumerate((
            (inverse_hbm.at[:, 0, 0], inverse),
            (source_hbm.at[:, 0], source),
            (coupling_hbm.at[:, 0, 0], coupling),
            (moms_hbm, moms),
            (counts_hbm, counts),
            (weights_hbm, weights),
            (vertex_hbm, vertex),
        ))
    ]
    for load in loads:
        load.start()

    barrier = pltpu.get_barrier_semaphore()

    def greet(step, carry):
        other = lax.rem(me + step, n_mom)
        pl.semaphore_signal(barrier, inc=1, device_id={"mom": other, "tm": turn}, device_id_type=MESH)
        return carry

    lax.fori_loop(1, n_mom, greet, 0)

    for other in (lax.rem(turn + 1, n_tm), lax.rem(turn + n_tm - 1, n_tm)):
        pl.semaphore_signal(barrier, inc=1, device_id={"mom": me, "tm": other}, device_id_type=MESH)

    def drive(chunk):
        columns = pl.ds(pl.multiple_of(chunk * LANES, LANES), LANES)
        forcing = jnp.concatenate([source[0, :, columns], source[1, :, columns]], axis=1)
        real, imag = complex_times(left_high[...], left_low[...], forcing)
        driven[chunk] = jnp.concatenate([real, imag], axis=1)

    loads[0].wait()
    for part in range(2):
        high, low = split(inverse[part])
        left_high[part * rows:(part + 1) * rows, :] = high
        left_low[part * rows:(part + 1) * rows, :] = low
    loads[1].wait()
    drive(0)
    loads[2].wait()

    @pl.when(turn > 0)
    def _():
        step = complex_times(
            left_high[...], left_low[...], jnp.concatenate([coupling[0], coupling[1]], axis=1)
        )
        for part in range(2):
            high, low = split(step[part])
            step_high[part * rows:(part + 1) * rows, :] = high
            step_low[part * rows:(part + 1) * rows, :] = low

    for load in loads[3:]:
        load.wait()
    pl.semaphore_wait(barrier, n_mom + 1)

    def hop(chunk):
        return pltpu.make_async_remote_copy(
            src_ref=greens.at[chunk], dst_ref=entering.at[chunk],
            send_sem=hop_send.at[chunk], recv_sem=hop_recv.at[chunk],
            device_id={"mom": me, "tm": lax.rem(turn + 1, n_tm)}, device_id_type=MESH,
        )

    def scatter(chunk, other):
        return pltpu.make_async_remote_copy(
            src_ref=outbox.at[chunk, other], dst_ref=inbox.at[chunk, me],
            send_sem=in_send.at[chunk], recv_sem=in_recv.at[chunk],
            device_id={"mom": other, "tm": turn}, device_id_type=MESH,
        )

    def collect(chunk, other):
        return pltpu.make_async_remote_copy(
            src_ref=formed.at[chunk, other], dst_ref=returned.at[chunk, me],
            send_sem=out_send.at[chunk], recv_sem=out_recv.at[chunk],
            device_id={"mom": other, "tm": turn}, device_id_type=MESH,
        )

    def settle(buffer, chunk, sem):
        block = buffer.at[chunk, pl.ds(0, n_mom - 1)]
        pltpu.make_async_copy(block, block, sem.at[chunk]).wait()

    def store(which, chunk):
        here, there = ((solved, solved_hbm), (sigma, sigma_hbm))[which]
        columns = pl.ds(pl.multiple_of(chunk * LANES, LANES), LANES)
        return pltpu.make_async_copy(here.at[chunk], there.at[:, 0, :, columns], store_sem.at[which, chunk])

    def advance(chunk):
        @pl.when(chunk > 0)
        def _():
            drive(chunk)

        @pl.when(turn == 0)
        def _():
            greens[chunk] = driven[chunk]

        @pl.when(turn > 0)
        def _():
            hop(chunk).wait_recv()
            real, imag = complex_times(step_high[...], step_low[...], entering[chunk])
            greens[chunk] = driven[chunk] + jnp.concatenate([real, imag], axis=1)

        @pl.when(turn < n_tm - 1)
        def _():
            hop(chunk).start()

        value = greens[chunk]
        real, imag = value[:, :LANES], value[:, LANES:]
        packed = jnp.concatenate(
            [real.reshape(n_mom, share, LANES), imag.reshape(n_mom, share, LANES)], axis=1
        )
        outbox[chunk] = packed.astype(jnp.bfloat16)
        inbox[chunk, me] = outbox[chunk, me]

        def send(step, carry):
            scatter(chunk, lax.rem(me + step, n_mom)).start()
            return carry

        lax.fori_loop(1, n_mom, send, 0)
        solved[chunk, 0] = real.astype(jnp.bfloat16)
        solved[chunk, 1] = imag.astype(jnp.bfloat16)
        store(0, chunk).start()

    def form(chunk):
        settle(inbox, chunk, in_recv)
        wide[...] = inbox[chunk].astype(jnp.float32)

        def one(step, carry):
            mom = lax.rem(me + step, n_mom)
            live = counts[mom]
            total_real = jnp.zeros((share, LANES), jnp.float32)
            total_imag = jnp.zeros((share, LANES), jnp.float32)
            for slot in range(slots):
                first, second, third = (wide[moms[place, slot, mom]] for place in range(3))
                factor = jnp.where(slot < live, vertex[weights[slot, mom]], 0.0)
                ar, ai = first[:share], first[share:]
                br, bi = second[:share], second[share:]
                cr, ci = third[:share], third[share:]
                prod_real = ar * br - ai * bi
                prod_imag = ar * bi + ai * br
                total_real = total_real + factor * (prod_real * cr + prod_imag * ci)
                total_imag = total_imag + factor * (prod_imag * cr - prod_real * ci)
            formed[chunk, mom] = jnp.concatenate([total_real, total_imag], axis=0).astype(jnp.bfloat16)

            @pl.when(step < n_mom)
            def _():
                collect(chunk, mom).start()

            return carry

        lax.fori_loop(1, n_mom + 1, one, 0)
        returned[chunk, me] = formed[chunk, me]

    def finish(chunk):
        settle(returned, chunk, out_recv)
        value = returned[chunk].astype(jnp.float32)
        sigma[chunk, 0] = value[:, :share].reshape(rows, LANES)
        sigma[chunk, 1] = value[:, share:].reshape(rows, LANES)
        store(1, chunk).start()

    def stage(step, carry):
        @pl.when(step < chunks)
        def _():
            advance(step)

        @pl.when((step >= 1) & (step < chunks + 1))
        def _():
            form(step - 1)

        @pl.when(step >= 2)
        def _():
            finish(step - 2)

        return carry

    lax.fori_loop(0, chunks + 2, stage, 0)

    def close(chunk, carry):
        @pl.when(turn < n_tm - 1)
        def _():
            hop(chunk).wait_send()

        settle(outbox, chunk, in_send)
        settle(formed, chunk, out_send)
        store(0, chunk).wait()
        store(1, chunk).wait()
        return carry

    lax.fori_loop(0, chunks, close, 0)


def write_out(solved, sigma, solved_out, sigma_out, sem):
    copies = [
        pltpu.make_async_copy(here.at[part], there.at[part], sem.at[place, part])
        for place, (here, there) in enumerate(((sigma, sigma_out), (solved, solved_out)))
        for part in range(2)
    ]
    for copy in copies:
        copy.start()
    for copy in copies:
        copy.wait()


def local(source, inverse_diag, coupling, pair_moms, pair_count, pair_weight, vertex):
    rows, columns = source.shape[2], source.shape[3]
    n_mom = lax.axis_size("mom")
    chunks, share = columns // LANES, rows // n_mom
    f32, bf16 = jnp.float32, jnp.bfloat16
    hbm = pl.BlockSpec(memory_space=pltpu.HBM)
    piece = (chunks, n_mom, 2 * share, LANES)
    sems = pltpu.SemaphoreType.DMA((chunks,))
    results = pl.pallas_call(
        kernel,
        out_shape=(
            jax.ShapeDtypeStruct(source.shape, bf16),
            jax.ShapeDtypeStruct(source.shape, f32),
        ),
        in_specs=[hbm] * 7,
        out_specs=(hbm, hbm),
        scratch_shapes=[
            pltpu.SMEM(pair_moms.shape[::-1], jnp.int32),
            pltpu.SMEM(pair_count.shape, jnp.int32),
            pltpu.SMEM(pair_weight.shape[::-1], jnp.int32),
            pltpu.SMEM(vertex.shape, f32),
            pltpu.VMEM((2, rows, columns), f32),
            pltpu.VMEM((2, rows, rows), f32),
            pltpu.VMEM((2, rows, rows), f32),
            pltpu.VMEM((2 * rows, rows), bf16),
            pltpu.VMEM((2 * rows, rows), bf16),
            pltpu.VMEM((2 * rows, rows), bf16),
            pltpu.VMEM((2 * rows, rows), bf16),
            pltpu.VMEM((chunks, rows, 2 * LANES), f32),
            pltpu.VMEM((chunks, rows, 2 * LANES), f32),
            pltpu.VMEM((chunks, rows, 2 * LANES), f32),
            pltpu.VMEM(piece, bf16),
            pltpu.VMEM(piece, bf16),
            pltpu.VMEM(piece[1:], f32),
            pltpu.VMEM(piece, bf16),
            pltpu.VMEM(piece, bf16),
            pltpu.VMEM((chunks, 2, rows, LANES), bf16),
            pltpu.VMEM((chunks, 2, rows, LANES), f32),
            pltpu.SemaphoreType.DMA((7,)),
            pltpu.SemaphoreType.DMA((2, chunks)),
            sems, sems, sems, sems, sems, sems,
        ],
        compiler_params=pltpu.CompilerParams(
            collective_id=0, has_side_effects=True, vmem_limit_bytes=58 << 20
        ),
    )(
        jnp.transpose(pair_moms, (2, 1, 0)), pair_count, jnp.transpose(pair_weight, (1, 0)), vertex,
        source, inverse_diag, coupling,
    )
    return pl.pallas_call(
        write_out,
        out_shape=(
            jax.ShapeDtypeStruct(source.shape, bf16),
            jax.ShapeDtypeStruct(source.shape, f32),
        ),
        in_specs=[pl.BlockSpec(memory_space=pl.ANY)] * 2,
        out_specs=(hbm, hbm),
        scratch_shapes=[pltpu.SemaphoreType.DMA((2, 2))],
    )(*results)


def solution(mesh):
    return jax.shard_map(
        local,
        mesh=mesh,
        in_specs=(
            P(None, "mom", "tm", None),
            P(None, "mom", "tm", None, None),
            P(None, "mom", "tm", None, None),
            P(),
            P(),
            P(),
            P(),
        ),
        out_specs=(P(None, "mom", "tm", None), P(None, "mom", "tm", None)),
        check_vma=False,
    )
```

```python
import jax
import jax.numpy as jnp
from jax import lax
from jax.experimental import pallas as pl
from jax.experimental.pallas import tpu as pltpu
from jax.sharding import PartitionSpec as P

MESH = pl.DeviceIdType.MESH
LANES = 128


def split(value):
    high = value.astype(jnp.bfloat16)
    return high, (value - high.astype(jnp.float32)).astype(jnp.bfloat16)


def dot(left, right):
    return jnp.dot(left, right, preferred_element_type=jnp.float32)


def complex_times(high, low, value):
    rows, width = high.shape[1], value.shape[1] // 2
    value_high, value_low = split(value)
    both = dot(high, value_high) + (dot(high, value_low) + dot(low, value_high))
    real = both[:rows, :width] - both[rows:, width:]
    imag = both[:rows, width:] + both[rows:, :width]
    return real, imag


def kernel(
    moms_hbm, counts_hbm, weights_hbm, vertex_hbm, source_hbm, inverse_hbm, coupling_hbm,
    solved_hbm, sigma_hbm,
    moms, counts, weights, vertex, source, inverse, coupling, left_high, left_low, step_high, step_low, driven, entering, greens,
    outbox, inbox, wide, formed, returned, solved, sigma,
    load_sem, store_sem, hop_send, hop_recv, in_send, in_recv, out_send, out_recv,
):
    n_mom, n_tm = lax.axis_size("mom"), lax.axis_size("tm")
    me, turn = lax.axis_index("mom"), lax.axis_index("tm")
    rows, chunks = driven.shape[1], driven.shape[0]
    share = rows // n_mom
    slots = moms.shape[1]

    loads = [
        pltpu.make_async_copy(here, there, load_sem.at[place])
        for place, (here, there) in enumerate((
            (inverse_hbm.at[:, 0, 0], inverse),
            (source_hbm.at[:, 0], source),
            (coupling_hbm.at[:, 0, 0], coupling),
            (moms_hbm, moms),
            (counts_hbm, counts),
            (weights_hbm, weights),
            (vertex_hbm, vertex),
        ))
    ]
    for load in loads:
        load.start()

    barrier = pltpu.get_barrier_semaphore()

    def greet(step, carry):
        other = lax.rem(me + step, n_mom)
        pl.semaphore_signal(barrier, inc=1, device_id={"mom": other, "tm": turn}, device_id_type=MESH)
        return carry

    lax.fori_loop(1, n_mom, greet, 0)

    for other in (lax.rem(turn + 1, n_tm), lax.rem(turn + n_tm - 1, n_tm)):
        pl.semaphore_signal(barrier, inc=1, device_id={"mom": me, "tm": other}, device_id_type=MESH)

    def drive(chunk):
        columns = pl.ds(pl.multiple_of(chunk * LANES, LANES), LANES)
        forcing = jnp.concatenate([source[0, :, columns], source[1, :, columns]], axis=1)
        real, imag = complex_times(left_high[...], left_low[...], forcing)
        driven[chunk] = jnp.concatenate([real, imag], axis=1)

    loads[0].wait()
    for part in range(2):
        high, low = split(inverse[part])
        left_high[part * rows:(part + 1) * rows, :] = high
        left_low[part * rows:(part + 1) * rows, :] = low
    loads[1].wait()
    drive(0)
    loads[2].wait()

    @pl.when(turn > 0)
    def _():
        step = complex_times(
            left_high[...], left_low[...], jnp.concatenate([coupling[0], coupling[1]], axis=1)
        )
        for part in range(2):
            high, low = split(step[part])
            step_high[part * rows:(part + 1) * rows, :] = high
            step_low[part * rows:(part + 1) * rows, :] = low

    for load in loads[3:]:
        load.wait()
    pl.semaphore_wait(barrier, n_mom + 1)

    def hop(chunk):
        return pltpu.make_async_remote_copy(
            src_ref=greens.at[chunk], dst_ref=entering.at[chunk],
            send_sem=hop_send.at[chunk], recv_sem=hop_recv.at[chunk],
            device_id={"mom": me, "tm": lax.rem(turn + 1, n_tm)}, device_id_type=MESH,
        )

    def scatter(chunk, other):
        return pltpu.make_async_remote_copy(
            src_ref=outbox.at[chunk, other], dst_ref=inbox.at[chunk, me],
            send_sem=in_send.at[chunk], recv_sem=in_recv.at[chunk],
            device_id={"mom": other, "tm": turn}, device_id_type=MESH,
        )

    def collect(chunk, other):
        return pltpu.make_async_remote_copy(
            src_ref=formed.at[chunk, other], dst_ref=returned.at[chunk, me],
            send_sem=out_send.at[chunk], recv_sem=out_recv.at[chunk],
            device_id={"mom": other, "tm": turn}, device_id_type=MESH,
        )

    def settle(buffer, chunk, sem):
        block = buffer.at[chunk, pl.ds(0, n_mom - 1)]
        pltpu.make_async_copy(block, block, sem.at[chunk]).wait()

    def store(which, chunk):
        here, there = ((solved, solved_hbm), (sigma, sigma_hbm))[which]
        columns = pl.ds(pl.multiple_of(chunk * LANES, LANES), LANES)
        return pltpu.make_async_copy(here.at[chunk], there.at[:, 0, :, columns], store_sem.at[which, chunk])

    def advance(chunk):
        @pl.when(chunk > 0)
        def _():
            drive(chunk)

        @pl.when(turn == 0)
        def _():
            greens[chunk] = driven[chunk]

        @pl.when(turn > 0)
        def _():
            hop(chunk).wait_recv()
            real, imag = complex_times(step_high[...], step_low[...], entering[chunk])
            greens[chunk] = driven[chunk] + jnp.concatenate([real, imag], axis=1)

        @pl.when(turn < n_tm - 1)
        def _():
            hop(chunk).start()

        value = greens[chunk]
        real, imag = value[:, :LANES], value[:, LANES:]
        packed = jnp.concatenate(
            [real.reshape(n_mom, share, LANES), imag.reshape(n_mom, share, LANES)], axis=1
        )
        outbox[chunk] = packed.astype(jnp.bfloat16)
        inbox[chunk, me] = outbox[chunk, me]

        def send(step, carry):
            scatter(chunk, lax.rem(me + step, n_mom)).start()
            return carry

        lax.fori_loop(1, n_mom, send, 0)
        solved[chunk, 0] = real.astype(jnp.bfloat16)
        solved[chunk, 1] = imag.astype(jnp.bfloat16)
        store(0, chunk).start()

    def form(chunk):
        settle(inbox, chunk, in_recv)
        wide[...] = inbox[chunk].astype(jnp.float32)

        def one(step, carry):
            mom = lax.rem(me + step, n_mom)
            live = counts[mom]
            total_real = jnp.zeros((share, LANES), jnp.float32)
            total_imag = jnp.zeros((share, LANES), jnp.float32)
            for slot in range(slots):
                first, second, third = (wide[moms[place, slot, mom]] for place in range(3))
                factor = jnp.where(slot < live, vertex[weights[slot, mom]], 0.0)
                ar, ai = first[:share], first[share:]
                br, bi = second[:share], second[share:]
                cr, ci = third[:share], third[share:]
                prod_real = ar * br - ai * bi
                prod_imag = ar * bi + ai * br
                total_real = total_real + factor * (prod_real * cr + prod_imag * ci)
                total_imag = total_imag + factor * (prod_imag * cr - prod_real * ci)
            formed[chunk, mom] = jnp.concatenate([total_real, total_imag], axis=0).astype(jnp.bfloat16)

            @pl.when(step < n_mom)
            def _():
                collect(chunk, mom).start()

            return carry

        lax.fori_loop(1, n_mom + 1, one, 0)
        returned[chunk, me] = formed[chunk, me]

    def finish(chunk):
        settle(returned, chunk, out_recv)
        value = returned[chunk].astype(jnp.float32)
        sigma[chunk, 0] = value[:, :share].reshape(rows, LANES)
        sigma[chunk, 1] = value[:, share:].reshape(rows, LANES)
        store(1, chunk).start()

    def stage(step, carry):
        @pl.when(step < chunks)
        def _():
            advance(step)

        @pl.when((step >= 1) & (step < chunks + 1))
        def _():
            form(step - 1)

        @pl.when(step >= 2)
        def _():
            finish(step - 2)

        return carry

    lax.fori_loop(0, chunks + 2, stage, 0)

    def close(chunk, carry):
        @pl.when(turn < n_tm - 1)
        def _():
            hop(chunk).wait_send()

        settle(outbox, chunk, in_send)
        settle(formed, chunk, out_send)
        store(0, chunk).wait()
        store(1, chunk).wait()
        return carry

    lax.fori_loop(0, chunks, close, 0)


def local(source, inverse_diag, coupling, pair_moms, pair_count, pair_weight, vertex):
    rows, columns = source.shape[2], source.shape[3]
    n_mom = lax.axis_size("mom")
    chunks, share = columns // LANES, rows // n_mom
    f32, bf16 = jnp.float32, jnp.bfloat16
    hbm = pl.BlockSpec(memory_space=pltpu.HBM)
    piece = (chunks, n_mom, 2 * share, LANES)
    sems = pltpu.SemaphoreType.DMA((chunks,))
    return pl.pallas_call(
        kernel,
        out_shape=(
            jax.ShapeDtypeStruct(source.shape, bf16),
            jax.ShapeDtypeStruct(source.shape, f32),
        ),
        in_specs=[hbm] * 7,
        out_specs=(hbm, hbm),
        scratch_shapes=[
            pltpu.SMEM(pair_moms.shape[::-1], jnp.int32),
            pltpu.SMEM(pair_count.shape, jnp.int32),
            pltpu.SMEM(pair_weight.shape[::-1], jnp.int32),
            pltpu.SMEM(vertex.shape, f32),
            pltpu.VMEM((2, rows, columns), f32),
            pltpu.VMEM((2, rows, rows), f32),
            pltpu.VMEM((2, rows, rows), f32),
            pltpu.VMEM((2 * rows, rows), bf16),
            pltpu.VMEM((2 * rows, rows), bf16),
            pltpu.VMEM((2 * rows, rows), bf16),
            pltpu.VMEM((2 * rows, rows), bf16),
            pltpu.VMEM((chunks, rows, 2 * LANES), f32),
            pltpu.VMEM((chunks, rows, 2 * LANES), f32),
            pltpu.VMEM((chunks, rows, 2 * LANES), f32),
            pltpu.VMEM(piece, bf16),
            pltpu.VMEM(piece, bf16),
            pltpu.VMEM(piece[1:], f32),
            pltpu.VMEM(piece, bf16),
            pltpu.VMEM(piece, bf16),
            pltpu.VMEM((chunks, 2, rows, LANES), bf16),
            pltpu.VMEM((chunks, 2, rows, LANES), f32),
            pltpu.SemaphoreType.DMA((7,)),
            pltpu.SemaphoreType.DMA((2, chunks)),
            sems, sems, sems, sems, sems, sems,
        ],
        compiler_params=pltpu.CompilerParams(
            collective_id=0, has_side_effects=True, vmem_limit_bytes=58 << 20
        ),
    )(
        jnp.transpose(pair_moms, (2, 1, 0)), pair_count, jnp.transpose(pair_weight, (1, 0)), vertex,
        source, inverse_diag, coupling,
    )


def solution(mesh):
    return jax.shard_map(
        local,
        mesh=mesh,
        in_specs=(
            P(None, "mom", "tm", None),
            P(None, "mom", "tm", None, None),
            P(None, "mom", "tm", None, None),
            P(),
            P(),
            P(),
            P(),
        ),
        out_specs=(P(None, "mom", "tm", None), P(None, "mom", "tm", None)),
        check_vma=False,
    )
```

```python
import jax
import jax.numpy as jnp
from jax import lax
from jax.experimental import pallas as pl
from jax.experimental.pallas import tpu as pltpu
from jax.sharding import PartitionSpec as P

MESH = pl.DeviceIdType.MESH
LANES = 128


def split(value):
    high = value.astype(jnp.bfloat16)
    return high, (value - high.astype(jnp.float32)).astype(jnp.bfloat16)


def dot(left, right):
    return jnp.dot(left, right, preferred_element_type=jnp.float32)


def complex_times(high, low, value):
    rows, width = high.shape[1], value.shape[1] // 2
    value_high, value_low = split(value)
    both = dot(high, value_high) + (dot(high, value_low) + dot(low, value_high))
    real = both[:rows, :width] - both[rows:, width:]
    imag = both[:rows, width:] + both[rows:, :width]
    return real, imag


def pack(real, imag):
    axis = real.ndim - 1
    lower = lax.broadcasted_iota(jnp.int32, real.shape, axis) < LANES // 2
    return (
        jnp.where(lower, real, pltpu.roll(imag, LANES // 2, axis)),
        jnp.where(lower, pltpu.roll(real, LANES // 2, axis), imag),
    )


def packed_times(high, low, value):
    rows = high.shape[1]
    value_high, value_low = split(value)
    both = dot(high, value_high) + (dot(high, value_low) + dot(low, value_high))
    top, turned = both[:rows], pltpu.roll(both[rows:], LANES // 2, 1)
    lower = lax.broadcasted_iota(jnp.int32, top.shape, 1) < LANES // 2
    return top + jnp.where(lower, -turned, turned)


def kernel(
    moms_hbm, counts_hbm, weights_hbm, vertex_hbm, source_hbm, inverse_hbm, coupling_hbm,
    solved_hbm, sigma_hbm,
    moms, counts, weights, vertex, source, inverse, coupling, left_high, left_low, step_high, step_low, driven, entering, greens,
    outbox, inbox, wide, formed, returned, solved, sigma,
    load_sem, store_sem, hop_send, hop_recv, in_send, in_recv, out_send, out_recv,
):
    n_mom, n_tm = lax.axis_size("mom"), lax.axis_size("tm")
    me, turn = lax.axis_index("mom"), lax.axis_index("tm")
    rows, chunks = sigma.shape[2], sigma.shape[0]
    share = rows // n_mom
    slots = moms.shape[1]

    loads = [
        pltpu.make_async_copy(here, there, load_sem.at[place])
        for place, (here, there) in enumerate((
            (inverse_hbm.at[:, 0, 0], inverse),
            (source_hbm.at[:, 0], source),
            (coupling_hbm.at[:, 0, 0], coupling),
            (moms_hbm, moms),
            (counts_hbm, counts),
            (weights_hbm, weights),
            (vertex_hbm, vertex),
        ))
    ]
    for load in loads:
        load.start()

    barrier = pltpu.get_barrier_semaphore()

    def greet(step, carry):
        other = lax.rem(me + step, n_mom)
        pl.semaphore_signal(barrier, inc=1, device_id={"mom": other, "tm": turn}, device_id_type=MESH)
        return carry

    lax.fori_loop(1, n_mom, greet, 0)

    for other in (lax.rem(turn + 1, n_tm), lax.rem(turn + n_tm - 1, n_tm)):
        pl.semaphore_signal(barrier, inc=1, device_id={"mom": me, "tm": other}, device_id_type=MESH)

    def drive(chunk):
        columns = pl.ds(pl.multiple_of(chunk * LANES, LANES), LANES)
        forcing = jnp.concatenate([source[0, :, columns], source[1, :, columns]], axis=1)
        for half, value in enumerate(pack(*complex_times(left_high[...], left_low[...], forcing))):
            driven[2 * chunk + half] = value

    loads[0].wait()
    for part in range(2):
        high, low = split(inverse[part])
        left_high[part * rows:(part + 1) * rows, :] = high
        left_low[part * rows:(part + 1) * rows, :] = low
    loads[1].wait()
    drive(0)
    loads[2].wait()

    @pl.when(turn > 0)
    def _():
        step = complex_times(
            left_high[...], left_low[...], jnp.concatenate([coupling[0], coupling[1]], axis=1)
        )
        for part in range(2):
            high, low = split(step[part])
            step_high[part * rows:(part + 1) * rows, :] = high
            step_low[part * rows:(part + 1) * rows, :] = low

    for load in loads[3:]:
        load.wait()
    pl.semaphore_wait(barrier, n_mom + 1)

    def hop(chunk):
        return pltpu.make_async_remote_copy(
            src_ref=greens.at[chunk], dst_ref=entering.at[chunk],
            send_sem=hop_send.at[chunk], recv_sem=hop_recv.at[chunk],
            device_id={"mom": me, "tm": lax.rem(turn + 1, n_tm)}, device_id_type=MESH,
        )

    def scatter(chunk, other):
        return pltpu.make_async_remote_copy(
            src_ref=outbox.at[chunk, other], dst_ref=inbox.at[chunk, me],
            send_sem=in_send.at[chunk], recv_sem=in_recv.at[chunk],
            device_id={"mom": other, "tm": turn}, device_id_type=MESH,
        )

    def collect(chunk, other):
        return pltpu.make_async_remote_copy(
            src_ref=formed.at[chunk, other], dst_ref=returned.at[chunk, me],
            send_sem=out_send.at[chunk], recv_sem=out_recv.at[chunk],
            device_id={"mom": other, "tm": turn}, device_id_type=MESH,
        )

    def settle(buffer, chunk, sem):
        block = buffer.at[chunk, pl.ds(0, n_mom - 1)]
        pltpu.make_async_copy(block, block, sem.at[chunk]).wait()

    def store(which, chunk):
        here, there = ((solved, solved_hbm), (sigma, sigma_hbm))[which]
        columns = pl.ds(pl.multiple_of(chunk * LANES, LANES), LANES)
        return pltpu.make_async_copy(here.at[chunk], there.at[:, 0, :, columns], store_sem.at[which, chunk])

    def advance(piece, carry):
        @pl.when(turn == 0)
        def _():
            greens[piece] = driven[piece]

        @pl.when(turn > 0)
        def _():
            hop(piece).wait_recv()
            greens[piece] = driven[piece] + packed_times(step_high[...], step_low[...], entering[piece])

        @pl.when(turn < n_tm - 1)
        def _():
            hop(piece).start()

        outbox[piece] = greens[piece].reshape(n_mom, share, LANES).astype(jnp.bfloat16)
        inbox[piece, me] = outbox[piece, me]

        def send(step, carry):
            scatter(piece, lax.rem(me + step, n_mom)).start()
            return carry

        return lax.fori_loop(1, n_mom, send, carry)

    def keep(chunk):
        for part, value in enumerate(pack(greens[2 * chunk], greens[2 * chunk + 1])):
            solved[chunk, part] = value
        store(0, chunk).start()

    def form(chunk):
        for half in range(2):
            settle(inbox, 2 * chunk + half, in_recv)
        for part, value in enumerate(pack(*(inbox[2 * chunk + half].astype(jnp.float32) for half in range(2)))):
            wide[:, part * share:(part + 1) * share] = value

        def one(step, carry):
            mom = lax.rem(me + step, n_mom)
            live = counts[mom]
            total_real = jnp.zeros((share, LANES), jnp.float32)
            total_imag = jnp.zeros((share, LANES), jnp.float32)
            for slot in range(slots):
                first, second, third = (wide[moms[place, slot, mom]] for place in range(3))
                factor = jnp.where(slot < live, vertex[weights[slot, mom]], 0.0)
                ar, ai = first[:share], first[share:]
                br, bi = second[:share], second[share:]
                cr, ci = third[:share], third[share:]
                prod_real = ar * br - ai * bi
                prod_imag = ar * bi + ai * br
                total_real = total_real + factor * (prod_real * cr + prod_imag * ci)
                total_imag = total_imag + factor * (prod_imag * cr - prod_real * ci)
            formed[chunk, mom] = jnp.concatenate([total_real, total_imag], axis=0).astype(jnp.bfloat16)

            @pl.when(step < n_mom)
            def _():
                collect(chunk, mom).start()

            return carry

        lax.fori_loop(1, n_mom + 1, one, 0)
        returned[chunk, me] = formed[chunk, me]

    def finish(chunk):
        settle(returned, chunk, out_recv)
        value = returned[chunk].astype(jnp.float32)
        sigma[chunk, 0] = value[:, :share].reshape(rows, LANES)
        sigma[chunk, 1] = value[:, share:].reshape(rows, LANES)
        store(1, chunk).start()

    def stage(step, carry):
        @pl.when((step > 0) & (step < chunks))
        def _():
            drive(step)

        @pl.when(step < chunks)
        def _():
            lax.fori_loop(2 * step, 2 * step + 2, advance, 0)
            keep(step)

        @pl.when((step >= 1) & (step < chunks + 1))
        def _():
            form(step - 1)

        @pl.when(step >= 2)
        def _():
            finish(step - 2)

        return carry

    lax.fori_loop(0, chunks + 2, stage, 0)

    def close_piece(piece, carry):
        @pl.when(turn < n_tm - 1)
        def _():
            hop(piece).wait_send()

        settle(outbox, piece, in_send)
        return carry

    lax.fori_loop(0, 2 * chunks, close_piece, 0)

    def close(chunk, carry):
        settle(formed, chunk, out_send)
        store(0, chunk).wait()
        store(1, chunk).wait()
        return carry

    lax.fori_loop(0, chunks, close, 0)


def local(source, inverse_diag, coupling, pair_moms, pair_count, pair_weight, vertex):
    rows, columns = source.shape[2], source.shape[3]
    n_mom = lax.axis_size("mom")
    chunks, share = columns // LANES, rows // n_mom
    f32, bf16 = jnp.float32, jnp.bfloat16
    hbm = pl.BlockSpec(memory_space=pltpu.HBM)
    piece = (chunks, n_mom, 2 * share, LANES)
    sems, twice = pltpu.SemaphoreType.DMA((chunks,)), pltpu.SemaphoreType.DMA((2 * chunks,))
    greens, sigma = pl.pallas_call(
        kernel,
        out_shape=(
            jax.ShapeDtypeStruct(source.shape, f32),
            jax.ShapeDtypeStruct(source.shape, f32),
        ),
        in_specs=[hbm] * 7,
        out_specs=(hbm, hbm),
        scratch_shapes=[
            pltpu.SMEM(pair_moms.shape[::-1], jnp.int32),
            pltpu.SMEM(pair_count.shape, jnp.int32),
            pltpu.SMEM(pair_weight.shape[::-1], jnp.int32),
            pltpu.SMEM(vertex.shape, f32),
            pltpu.VMEM((2, rows, columns), f32),
            pltpu.VMEM((2, rows, rows), f32),
            pltpu.VMEM((2, rows, rows), f32),
            pltpu.VMEM((2 * rows, rows), bf16),
            pltpu.VMEM((2 * rows, rows), bf16),
            pltpu.VMEM((2 * rows, rows), bf16),
            pltpu.VMEM((2 * rows, rows), bf16),
            pltpu.VMEM((2 * chunks, rows, LANES), f32),
            pltpu.VMEM((2 * chunks, rows, LANES), f32),
            pltpu.VMEM((2 * chunks, rows, LANES), f32),
            pltpu.VMEM((2 * chunks, n_mom, share, LANES), bf16),
            pltpu.VMEM((2 * chunks, n_mom, share, LANES), bf16),
            pltpu.VMEM(piece[1:], f32),
            pltpu.VMEM(piece, bf16),
            pltpu.VMEM(piece, bf16),
            pltpu.VMEM((chunks, 2, rows, LANES), f32),
            pltpu.VMEM((chunks, 2, rows, LANES), f32),
            pltpu.SemaphoreType.DMA((7,)),
            pltpu.SemaphoreType.DMA((2, chunks)),
            twice, twice, twice, twice, sems, sems,
        ],
        compiler_params=pltpu.CompilerParams(
            collective_id=0, has_side_effects=True, vmem_limit_bytes=58 << 20
        ),
    )(
        jnp.transpose(pair_moms, (2, 1, 0)), pair_count, jnp.transpose(pair_weight, (1, 0)), vertex,
        source, inverse_diag, coupling,
    )
    return greens.astype(bf16), sigma


def solution(mesh):
    return jax.shard_map(
        local,
        mesh=mesh,
        in_specs=(
            P(None, "mom", "tm", None),
            P(None, "mom", "tm", None, None),
            P(None, "mom", "tm", None, None),
            P(),
            P(),
            P(),
            P(),
        ),
        out_specs=(P(None, "mom", "tm", None), P(None, "mom", "tm", None)),
        check_vma=False,
    )
```

```python
import jax
import jax.numpy as jnp
from jax import lax
from jax.experimental import pallas as pl
from jax.experimental.pallas import tpu as pltpu
from jax.sharding import PartitionSpec as P

MESH = pl.DeviceIdType.MESH
LANES = 128


def split(value):
    high = value.astype(jnp.bfloat16)
    return high, (value - high.astype(jnp.float32)).astype(jnp.bfloat16)


def dot(left, right):
    return jnp.dot(left, right, preferred_element_type=jnp.float32)


def product(high, low, value_high, value_low):
    return dot(high, value_high) + (dot(high, value_low) + dot(low, value_high))


def join(both):
    rows, width = both.shape[0] // 2, both.shape[1] // 2
    real = both[:rows, :width] - both[rows:, width:]
    imag = both[:rows, width:] + both[rows:, :width]
    return real, imag


def complex_times(high, low, value):
    return join(product(high, low, *split(value)))


def pack(real, imag):
    axis = real.ndim - 1
    lower = lax.broadcasted_iota(jnp.int32, real.shape, axis) < LANES // 2
    return (
        jnp.where(lower, real, pltpu.roll(imag, LANES // 2, axis)),
        jnp.where(lower, pltpu.roll(real, LANES // 2, axis), imag),
    )


def packed_times(high, low, value):
    rows = high.shape[1]
    both = product(high, low, *split(value))
    lower = lax.broadcasted_iota(jnp.int32, (rows, LANES), 1) < LANES // 2
    blocks = []
    for at in range(0, value.shape[1], LANES):
        turned = pltpu.roll(both[rows:, at:at + LANES], LANES // 2, 1)
        blocks.append(both[:rows, at:at + LANES] + jnp.where(lower, -turned, turned))
    return blocks


def kernel(
    moms_hbm, counts_hbm, weights_hbm, vertex_hbm, source_hbm, inverse_hbm, coupling_hbm,
    solved_hbm, sigma_hbm,
    moms, counts, weights, vertex, source, inverse, coupling, left_high, left_low, own_high, own_low, pair_high, pair_low, step_high, step_low,
    driven, lent, entering, greens,
    outbox, inbox, wide, formed, returned, solved, sigma,
    load_sem, store_sem, pair_send, pair_recv, lend_send, lend_recv, pass_send, hop_send, hop_recv, in_send, in_recv, out_send, out_recv,
):
    n_mom, n_tm = lax.axis_size("mom"), lax.axis_size("tm")
    me, turn = lax.axis_index("mom"), lax.axis_index("tm")
    rows, chunks = sigma.shape[2], sigma.shape[0]
    share = rows // n_mom
    slots = moms.shape[1]
    core, plane, planes = lax.rem(turn, 2), turn // 2, n_tm // 2
    partner = turn + 1 - 2 * core

    loads = [
        pltpu.make_async_copy(here, there, load_sem.at[place])
        for place, (here, there) in enumerate((
            (inverse_hbm.at[:, 0, 0], inverse),
            (source_hbm.at[:, 0], source),
            (coupling_hbm.at[:, 0, 0], coupling),
            (moms_hbm, moms),
            (counts_hbm, counts),
            (weights_hbm, weights),
            (vertex_hbm, vertex),
        ))
    ]
    for load in loads:
        load.start()

    barrier = pltpu.get_barrier_semaphore()

    def greet(step, carry):
        other = lax.rem(me + step, n_mom)
        pl.semaphore_signal(barrier, inc=1, device_id={"mom": other, "tm": turn}, device_id_type=MESH)
        return carry

    lax.fori_loop(1, n_mom, greet, 0)

    for other in (partner, lax.rem(turn + 2, n_tm), lax.rem(turn + n_tm - 2, n_tm)):
        pl.semaphore_signal(barrier, inc=1, device_id={"mom": me, "tm": other}, device_id_type=MESH)

    def drive(chunk):
        columns = pl.ds(pl.multiple_of(chunk * LANES, LANES), LANES)
        forcing = jnp.concatenate([source[0, :, columns], source[1, :, columns]], axis=1)
        for half, value in enumerate(pack(*complex_times(left_high[...], left_low[...], forcing))):
            driven[2 * chunk + half] = value

    loads[0].wait()
    for part in range(2):
        high, low = split(inverse[part])
        left_high[part * rows:(part + 1) * rows, :] = high
        left_low[part * rows:(part + 1) * rows, :] = low
    loads[1].wait()
    drive(0)
    loads[2].wait()

    def keep_matrix(high_ref, low_ref, matrix):
        for part in range(2):
            high, low = split(matrix[part])
            high_ref[part * rows:(part + 1) * rows, :] = high
            low_ref[part * rows:(part + 1) * rows, :] = low

    @pl.when((plane > 0) | (core == 1))
    def _():
        keep_matrix(own_high, own_low, complex_times(
            left_high[...], left_low[...], jnp.concatenate([coupling[0], coupling[1]], axis=1)
        ))

    for load in loads[3:]:
        load.wait()
    pl.semaphore_wait(barrier, n_mom + 2)

    def to(other, src, dst, send_sem, recv_sem):
        return pltpu.make_async_remote_copy(
            src_ref=src, dst_ref=dst, send_sem=send_sem, recv_sem=recv_sem,
            device_id={"mom": me, "tm": other}, device_id_type=MESH,
        )

    def lend(piece):
        return to(partner, driven.at[piece], lent.at[piece], lend_send.at[piece], lend_recv.at[piece])

    def hop(piece):
        return to(
            lax.rem(turn + 2, n_tm), greens.at[piece], entering.at[piece], hop_send.at[piece], hop_recv.at[piece]
        )

    def forward(piece):
        return to(partner, entering.at[piece], entering.at[piece], pass_send.at[piece], hop_recv.at[piece])

    pairs = (
        to(partner, own_high, pair_high, pair_send.at[0], pair_recv.at[0]),
        to(partner, own_low, pair_low, pair_send.at[1], pair_recv.at[1]),
    )

    @pl.when(core == 0)
    def _():
        for half in range(2):
            lend(half).start()

        @pl.when(plane > 0)
        def _():
            for pair in pairs:
                pair.start()
            step_high[...] = own_high[...]
            step_low[...] = own_low[...]

        def drive_and_lend(chunk, carry):
            drive(chunk)
            for half in range(2):
                lend(2 * chunk + half).start()
            return carry

        lax.fori_loop(1, chunks, drive_and_lend, 0)

    @pl.when((core == 1) & (plane > 0))
    def _():
        for pair in pairs:
            pair.wait_recv()
        both = product(
            own_high[...], own_low[...],
            jnp.concatenate([pair_high[:rows, :], pair_high[rows:, :]], axis=1),
            jnp.concatenate([pair_low[:rows, :], pair_low[rows:, :]], axis=1),
        )
        keep_matrix(step_high, step_low, join(both))

    def compose(chunk):
        @pl.when(chunk > 0)
        def _():
            drive(chunk)

        for half in range(2):
            lend(2 * chunk + half).wait_recv()
        value = jnp.concatenate([lent[2 * chunk], lent[2 * chunk + 1]], axis=1)
        for half, block in enumerate(packed_times(own_high[...], own_low[...], value)):
            driven[2 * chunk + half] = driven[2 * chunk + half] + block

    def scatter(chunk, other):
        return pltpu.make_async_remote_copy(
            src_ref=outbox.at[chunk, other], dst_ref=inbox.at[chunk, me],
            send_sem=in_send.at[chunk], recv_sem=in_recv.at[chunk],
            device_id={"mom": other, "tm": turn}, device_id_type=MESH,
        )

    def collect(chunk, other):
        return pltpu.make_async_remote_copy(
            src_ref=formed.at[chunk, other], dst_ref=returned.at[chunk, me],
            send_sem=out_send.at[chunk], recv_sem=out_recv.at[chunk],
            device_id={"mom": other, "tm": turn}, device_id_type=MESH,
        )

    def settle(buffer, chunk, sem):
        block = buffer.at[chunk, pl.ds(0, n_mom - 1)]
        pltpu.make_async_copy(block, block, sem.at[chunk]).wait()

    def store(which, chunk):
        here, there = ((solved, solved_hbm), (sigma, sigma_hbm))[which]
        columns = pl.ds(pl.multiple_of(chunk * LANES, LANES), LANES)
        return pltpu.make_async_copy(here.at[chunk], there.at[:, 0, :, columns], store_sem.at[which, chunk])

    def advance(piece, carry):
        @pl.when(plane == 0)
        def _():
            greens[piece] = driven[piece]

        @pl.when(plane > 0)
        def _():
            hop(piece).wait_recv()

            @pl.when(core == 1)
            def _():
                forward(piece).start()

            [block] = packed_times(step_high[...], step_low[...], entering[piece])
            greens[piece] = driven[piece] + block

        @pl.when((core == 1) & (plane < planes - 1))
        def _():
            hop(piece).start()

        outbox[piece] = greens[piece].reshape(n_mom, share, LANES).astype(jnp.bfloat16)
        inbox[piece, me] = outbox[piece, me]

        def send(step, carry):
            scatter(piece, lax.rem(me + step, n_mom)).start()
            return carry

        return lax.fori_loop(1, n_mom, send, carry)

    def keep(chunk):
        for part, value in enumerate(pack(greens[2 * chunk], greens[2 * chunk + 1])):
            solved[chunk, part] = value
        store(0, chunk).start()

    def form(chunk):
        for half in range(2):
            settle(inbox, 2 * chunk + half, in_recv)
        for part, value in enumerate(pack(*(inbox[2 * chunk + half].astype(jnp.float32) for half in range(2)))):
            wide[:, part * share:(part + 1) * share] = value

        def one(step, carry):
            mom = lax.rem(me + step, n_mom)
            live = counts[mom]
            total_real = jnp.zeros((share, LANES), jnp.float32)
            total_imag = jnp.zeros((share, LANES), jnp.float32)
            for slot in range(slots):
                first, second, third = (wide[moms[place, slot, mom]] for place in range(3))
                factor = jnp.where(slot < live, vertex[weights[slot, mom]], 0.0)
                ar, ai = first[:share], first[share:]
                br, bi = second[:share], second[share:]
                cr, ci = third[:share], third[share:]
                prod_real = ar * br - ai * bi
                prod_imag = ar * bi + ai * br
                total_real = total_real + factor * (prod_real * cr + prod_imag * ci)
                total_imag = total_imag + factor * (prod_imag * cr - prod_real * ci)
            formed[chunk, mom] = jnp.concatenate([total_real, total_imag], axis=0).astype(jnp.bfloat16)

            @pl.when(step < n_mom)
            def _():
                collect(chunk, mom).start()

            return carry

        lax.fori_loop(1, n_mom + 1, one, 0)
        returned[chunk, me] = formed[chunk, me]

    def finish(chunk):
        settle(returned, chunk, out_recv)
        value = returned[chunk].astype(jnp.float32)
        sigma[chunk, 0] = value[:, :share].reshape(rows, LANES)
        sigma[chunk, 1] = value[:, share:].reshape(rows, LANES)
        store(1, chunk).start()

    def stage(step, carry):
        @pl.when((core == 1) & (step < chunks))
        def _():
            compose(step)

        @pl.when(step < chunks)
        def _():
            lax.fori_loop(2 * step, 2 * step + 2, advance, 0)
            keep(step)

        @pl.when((step >= 1) & (step < chunks + 1))
        def _():
            form(step - 1)

        @pl.when(step >= 2)
        def _():
            finish(step - 2)

        return carry

    lax.fori_loop(0, chunks + 2, stage, 0)

    def close_piece(piece, carry):
        @pl.when(core == 0)
        def _():
            lend(piece).wait_send()

        @pl.when((core == 1) & (plane > 0))
        def _():
            forward(piece).wait_send()

        @pl.when((core == 1) & (plane < planes - 1))
        def _():
            hop(piece).wait_send()

        settle(outbox, piece, in_send)
        return carry

    lax.fori_loop(0, 2 * chunks, close_piece, 0)

    @pl.when((core == 0) & (plane > 0))
    def _():
        for pair in pairs:
            pair.wait_send()

    def close(chunk, carry):
        settle(formed, chunk, out_send)
        store(0, chunk).wait()
        store(1, chunk).wait()
        return carry

    lax.fori_loop(0, chunks, close, 0)


def local(source, inverse_diag, coupling, pair_moms, pair_count, pair_weight, vertex):
    rows, columns = source.shape[2], source.shape[3]
    n_mom = lax.axis_size("mom")
    chunks, share = columns // LANES, rows // n_mom
    f32, bf16 = jnp.float32, jnp.bfloat16
    hbm = pl.BlockSpec(memory_space=pltpu.HBM)
    piece = (chunks, n_mom, 2 * share, LANES)
    sems, twice = pltpu.SemaphoreType.DMA((chunks,)), pltpu.SemaphoreType.DMA((2 * chunks,))
    greens, sigma = pl.pallas_call(
        kernel,
        out_shape=(
            jax.ShapeDtypeStruct(source.shape, f32),
            jax.ShapeDtypeStruct(source.shape, f32),
        ),
        in_specs=[hbm] * 7,
        out_specs=(hbm, hbm),
        scratch_shapes=[
            pltpu.SMEM(pair_moms.shape[::-1], jnp.int32),
            pltpu.SMEM(pair_count.shape, jnp.int32),
            pltpu.SMEM(pair_weight.shape[::-1], jnp.int32),
            pltpu.SMEM(vertex.shape, f32),
            pltpu.VMEM((2, rows, columns), f32),
            pltpu.VMEM((2, rows, rows), f32),
            pltpu.VMEM((2, rows, rows), f32),
            *[pltpu.VMEM((2 * rows, rows), bf16) for _ in range(8)],
            pltpu.VMEM((2 * chunks, rows, LANES), f32),
            pltpu.VMEM((2 * chunks, rows, LANES), f32),
            pltpu.VMEM((2 * chunks, rows, LANES), f32),
            pltpu.VMEM((2 * chunks, rows, LANES), f32),
            pltpu.VMEM((2 * chunks, n_mom, share, LANES), bf16),
            pltpu.VMEM((2 * chunks, n_mom, share, LANES), bf16),
            pltpu.VMEM(piece[1:], f32),
            pltpu.VMEM(piece, bf16),
            pltpu.VMEM(piece, bf16),
            pltpu.VMEM((chunks, 2, rows, LANES), f32),
            pltpu.VMEM((chunks, 2, rows, LANES), f32),
            pltpu.SemaphoreType.DMA((7,)),
            pltpu.SemaphoreType.DMA((2, chunks)),
            pltpu.SemaphoreType.DMA((2,)),
            pltpu.SemaphoreType.DMA((2,)),
            twice, twice, twice, twice, twice, twice, twice, sems, sems,
        ],
        compiler_params=pltpu.CompilerParams(
            collective_id=0, has_side_effects=True, vmem_limit_bytes=58 << 20
        ),
    )(
        jnp.transpose(pair_moms, (2, 1, 0)), pair_count, jnp.transpose(pair_weight, (1, 0)), vertex,
        source, inverse_diag, coupling,
    )
    return greens.astype(bf16), sigma


def solution(mesh):
    return jax.shard_map(
        local,
        mesh=mesh,
        in_specs=(
            P(None, "mom", "tm", None),
            P(None, "mom", "tm", None, None),
            P(None, "mom", "tm", None, None),
            P(),
            P(),
            P(),
            P(),
        ),
        out_specs=(P(None, "mom", "tm", None), P(None, "mom", "tm", None)),
        check_vma=False,
    )
```

```python
import jax
import jax.numpy as jnp
from jax import lax
from jax.experimental import pallas as pl
from jax.experimental.pallas import tpu as pltpu
from jax.sharding import PartitionSpec as P

MESH = pl.DeviceIdType.MESH
LANES = 128


def split(value):
    high = value.astype(jnp.bfloat16)
    return high, (value - high.astype(jnp.float32)).astype(jnp.bfloat16)


def dot(left, right):
    return jnp.dot(left, right, preferred_element_type=jnp.float32)


def product(high, low, value_high, value_low):
    return dot(high, value_high) + (dot(high, value_low) + dot(low, value_high))


def join(both):
    rows, width = both.shape[0] // 2, both.shape[1] // 2
    real = both[:rows, :width] - both[rows:, width:]
    imag = both[:rows, width:] + both[rows:, :width]
    return real, imag


def complex_times(high, low, value):
    return join(product(high, low, *split(value)))


def pack(real, imag):
    axis = real.ndim - 1
    lower = lax.broadcasted_iota(jnp.int32, real.shape, axis) < LANES // 2
    return (
        jnp.where(lower, real, pltpu.roll(imag, LANES // 2, axis)),
        jnp.where(lower, pltpu.roll(real, LANES // 2, axis), imag),
    )


def packed_times(high, low, value):
    rows = high.shape[1]
    both = product(high, low, *split(value))
    lower = lax.broadcasted_iota(jnp.int32, (rows, LANES), 1) < LANES // 2
    blocks = []
    for at in range(0, value.shape[1], LANES):
        turned = pltpu.roll(both[rows:, at:at + LANES], LANES // 2, 1)
        blocks.append(both[:rows, at:at + LANES] + jnp.where(lower, -turned, turned))
    return blocks


def kernel(
    moms_hbm, counts_hbm, weights_hbm, vertex_hbm, source_hbm, inverse_hbm, coupling_hbm,
    solved_hbm, sigma_hbm,
    moms, counts, weights, vertex, source, inverse, coupling, left_high, left_low, own_high, own_low, pair_high, pair_low, step_high, step_low,
    driven, lent, entering, greens,
    outbox, inbox, wide, formed, returned, solved, sigma,
    load_sem, store_sem, pair_send, pair_recv, lend_send, lend_recv, pass_send, hop_send, hop_recv, in_send, in_recv, out_send, out_recv,
):
    n_mom, n_tm = lax.axis_size("mom"), lax.axis_size("tm")
    me, turn = lax.axis_index("mom"), lax.axis_index("tm")
    rows, chunks = sigma.shape[2], sigma.shape[0]
    share = rows // n_mom
    slots = moms.shape[1]
    core, plane, planes = lax.rem(turn, 2), turn // 2, n_tm // 2
    partner = turn + 1 - 2 * core
    first, last = plane == 0, plane == planes - 1
    ahead = 2 * (planes - 1)

    loads = [
        pltpu.make_async_copy(here, there, load_sem.at[place])
        for place, (here, there) in enumerate((
            (inverse_hbm.at[:, 0, 0], inverse),
            (source_hbm.at[:, 0], source),
            (coupling_hbm.at[:, 0, 0], coupling),
            (moms_hbm, moms),
            (counts_hbm, counts),
            (weights_hbm, weights),
            (vertex_hbm, vertex),
        ))
    ]
    for load in loads:
        load.start()

    barrier = pltpu.get_barrier_semaphore()

    def greet(step, carry):
        other = lax.rem(me + step, n_mom)
        pl.semaphore_signal(barrier, inc=1, device_id={"mom": other, "tm": turn}, device_id_type=MESH)
        return carry

    lax.fori_loop(1, n_mom, greet, 0)

    for other in (partner, lax.rem(turn + 2, n_tm), lax.rem(turn + n_tm - 2, n_tm)):
        pl.semaphore_signal(barrier, inc=1, device_id={"mom": me, "tm": other}, device_id_type=MESH)

    def greet_helper(shift):
        def greet_one(other, carry):
            pl.semaphore_signal(
                barrier, inc=1, device_id={"mom": other, "tm": turn + shift}, device_id_type=MESH
            )
            return carry

        lax.fori_loop(0, n_mom, greet_one, 0)

    @pl.when(first)
    def _():
        greet_helper(ahead)

    @pl.when(last)
    def _():
        greet_helper(-ahead)

    def drive(chunk):
        columns = pl.ds(pl.multiple_of(chunk * LANES, LANES), LANES)
        forcing = jnp.concatenate([source[0, :, columns], source[1, :, columns]], axis=1)
        for half, value in enumerate(pack(*complex_times(left_high[...], left_low[...], forcing))):
            driven[2 * chunk + half] = value

    loads[0].wait()
    for part in range(2):
        high, low = split(inverse[part])
        left_high[part * rows:(part + 1) * rows, :] = high
        left_low[part * rows:(part + 1) * rows, :] = low
    loads[1].wait()
    drive(0)
    loads[2].wait()

    def keep_matrix(high_ref, low_ref, matrix):
        for part in range(2):
            high, low = split(matrix[part])
            high_ref[part * rows:(part + 1) * rows, :] = high
            low_ref[part * rows:(part + 1) * rows, :] = low

    @pl.when((plane > 0) | (core == 1))
    def _():
        keep_matrix(own_high, own_low, complex_times(
            left_high[...], left_low[...], jnp.concatenate([coupling[0], coupling[1]], axis=1)
        ))

    for load in loads[3:]:
        load.wait()

    @pl.when(first | last)
    def _():
        pl.semaphore_wait(barrier, 2 * n_mom + 2)

    @pl.when(jnp.logical_not(first | last))
    def _():
        pl.semaphore_wait(barrier, n_mom + 2)

    def to(other, src, dst, send_sem, recv_sem):
        return pltpu.make_async_remote_copy(
            src_ref=src, dst_ref=dst, send_sem=send_sem, recv_sem=recv_sem,
            device_id={"mom": me, "tm": other}, device_id_type=MESH,
        )

    def lend(piece):
        return to(partner, driven.at[piece], lent.at[piece], lend_send.at[piece], lend_recv.at[piece])

    def hop(piece):
        return to(
            lax.rem(turn + 2, n_tm), greens.at[piece], entering.at[piece], hop_send.at[piece], hop_recv.at[piece]
        )

    def forward(piece):
        return to(partner, entering.at[piece], entering.at[piece], pass_send.at[piece], hop_recv.at[piece])

    pairs = (
        to(partner, own_high, pair_high, pair_send.at[0], pair_recv.at[0]),
        to(partner, own_low, pair_low, pair_send.at[1], pair_recv.at[1]),
    )

    @pl.when(core == 0)
    def _():
        for half in range(2):
            lend(half).start()

        @pl.when(plane > 0)
        def _():
            for pair in pairs:
                pair.start()
            step_high[...] = own_high[...]
            step_low[...] = own_low[...]

        def drive_and_lend(chunk, carry):
            drive(chunk)
            for half in range(2):
                lend(2 * chunk + half).start()
            return carry

        lax.fori_loop(1, chunks, drive_and_lend, 0)

    @pl.when((core == 1) & (plane > 0))
    def _():
        for pair in pairs:
            pair.wait_recv()
        both = product(
            own_high[...], own_low[...],
            jnp.concatenate([pair_high[:rows, :], pair_high[rows:, :]], axis=1),
            jnp.concatenate([pair_low[:rows, :], pair_low[rows:, :]], axis=1),
        )
        keep_matrix(step_high, step_low, join(both))

    def compose(chunk):
        @pl.when(chunk > 0)
        def _():
            drive(chunk)

        for half in range(2):
            lend(2 * chunk + half).wait_recv()
        value = jnp.concatenate([lent[2 * chunk], lent[2 * chunk + 1]], axis=1)
        for half, block in enumerate(packed_times(own_high[...], own_low[...], value)):
            driven[2 * chunk + half] = driven[2 * chunk + half] + block

    def send(src, dst, send_sem, recv_sem, other, there):
        pltpu.make_async_remote_copy(
            src_ref=src, dst_ref=dst, send_sem=send_sem, recv_sem=recv_sem,
            device_id={"mom": other, "tm": there}, device_id_type=MESH,
        ).start()

    def settle(block, sem):
        pltpu.make_async_copy(block, block, sem).wait()

    def others(body):
        def one(step, carry):
            body(lax.rem(me + step, n_mom))
            return carry

        return one

    def store(which, chunk):
        here, there = ((solved, solved_hbm), (sigma, sigma_hbm))[which]
        columns = pl.ds(pl.multiple_of(chunk * LANES, LANES), LANES)
        return pltpu.make_async_copy(here.at[chunk], there.at[:, 0, :, columns], store_sem.at[which, chunk])

    def advance(piece, carry):
        @pl.when(plane == 0)
        def _():
            greens[piece] = driven[piece]

        @pl.when(plane > 0)
        def _():
            hop(piece).wait_recv()

            @pl.when(core == 1)
            def _():
                forward(piece).start()

            [block] = packed_times(step_high[...], step_low[...], entering[piece])
            greens[piece] = driven[piece] + block

        @pl.when((core == 1) & (plane < planes - 1))
        def _():
            hop(piece).start()

        chunk, half = piece // 2, lax.rem(piece, 2)
        outbox[chunk, :, half] = greens[piece].reshape(n_mom, share, LANES).astype(jnp.bfloat16)
        given = last & (chunk == chunks - 1)

        @pl.when(jnp.logical_not(given))
        def _():
            inbox[chunk, me, half] = outbox[chunk, me, half]

        @pl.when(chunk == 0)
        def _():
            lax.fori_loop(1, n_mom, others(lambda other: send(
                outbox.at[0, other, half], inbox.at[0, me, half], in_send.at[half], in_recv.at[half], other, turn
            )), 0)

        @pl.when((chunk > 0) & (half == 1) & jnp.logical_not(given))
        def _():
            lax.fori_loop(1, n_mom, others(lambda other: send(
                outbox.at[chunk, other], inbox.at[chunk, me], in_send.at[chunk + 1], in_recv.at[chunk + 1], other, turn
            )), 0)

        @pl.when((half == 1) & given)
        def _():
            lax.fori_loop(0, n_mom, others(lambda other: send(
                outbox.at[chunk, other], inbox.at[chunks, me], in_send.at[chunk + 1], in_recv.at[chunks + 1],
                other, lax.rem(turn + 2, n_tm),
            )), 0)

        return carry

    def keep(chunk):
        for part, value in enumerate(pack(greens[2 * chunk], greens[2 * chunk + 1])):
            solved[chunk, part] = value.astype(jnp.bfloat16)
        store(0, chunk).start()

    def form(chunk, handed):
        if handed:
            settle(inbox.at[chunk], in_recv.at[chunk + 1])
        else:
            @pl.when(chunk == 0)
            def _():
                for half in range(2):
                    settle(inbox.at[0, pl.ds(0, n_mom - 1), half], in_recv.at[half])

            @pl.when(chunk > 0)
            def _():
                settle(inbox.at[chunk, pl.ds(0, n_mom - 1)], in_recv.at[chunk + 1])

        for part, value in enumerate(pack(*(inbox[chunk, :, half].astype(jnp.float32) for half in range(2)))):
            wide[:, part * share:(part + 1) * share] = value

        def one(step, carry):
            mom = lax.rem(me + step, n_mom)
            live = counts[mom]
            total_real = jnp.zeros((share, LANES), jnp.float32)
            total_imag = jnp.zeros((share, LANES), jnp.float32)
            for slot in range(slots):
                first, second, third = (wide[moms[place, slot, mom]] for place in range(3))
                factor = jnp.where(slot < live, vertex[weights[slot, mom]], 0.0)
                ar, ai = first[:share], first[share:]
                br, bi = second[:share], second[share:]
                cr, ci = third[:share], third[share:]
                prod_real = ar * br - ai * bi
                prod_imag = ar * bi + ai * br
                total_real = total_real + factor * (prod_real * cr + prod_imag * ci)
                total_imag = total_imag + factor * (prod_imag * cr - prod_real * ci)
            formed[chunk, mom] = jnp.concatenate([total_real, total_imag], axis=0).astype(jnp.bfloat16)

            if handed:
                send(
                    formed.at[chunk, mom], returned.at[chunks - 1, me], out_send.at[chunk], out_recv.at[chunks - 1],
                    mom, turn + ahead,
                )
            else:
                @pl.when(step < n_mom)
                def _():
                    send(
                        formed.at[chunk, mom], returned.at[chunk, me], out_send.at[chunk], out_recv.at[chunk], mom, turn
                    )

            return carry

        lax.fori_loop(1, n_mom + 1, one, 0)
        if not handed:
            returned[chunk, me] = formed[chunk, me]

    def finish(chunk):
        given = last & (chunk == chunks - 1)

        @pl.when(given)
        def _():
            settle(returned.at[chunk], out_recv.at[chunk])

        @pl.when(jnp.logical_not(given))
        def _():
            settle(returned.at[chunk, pl.ds(0, n_mom - 1)], out_recv.at[chunk])

        value = returned[chunk].astype(jnp.float32)
        sigma[chunk, 0] = value[:, :share].reshape(rows, LANES)
        sigma[chunk, 1] = value[:, share:].reshape(rows, LANES)
        store(1, chunk).start()

    def stage(step, carry):
        @pl.when((core == 1) & (step < chunks))
        def _():
            compose(step)

        @pl.when(step < chunks)
        def _():
            lax.fori_loop(2 * step, 2 * step + 2, advance, 0)
            keep(step)

        @pl.when((step >= 1) & ((step < chunks) | ((step == chunks) & jnp.logical_not(last))))
        def _():
            form(step - 1, False)

        @pl.when(step >= 2)
        def _():
            finish(step - 2)

        return carry

    lax.fori_loop(0, chunks + 2, stage, 0)

    @pl.when(first)
    def _():
        form(chunks, True)

    def close_piece(piece, carry):
        @pl.when(core == 0)
        def _():
            lend(piece).wait_send()

        @pl.when((core == 1) & (plane > 0))
        def _():
            forward(piece).wait_send()

        @pl.when((core == 1) & (plane < planes - 1))
        def _():
            hop(piece).wait_send()

        return carry

    lax.fori_loop(0, 2 * chunks, close_piece, 0)

    @pl.when((core == 0) & (plane > 0))
    def _():
        for pair in pairs:
            pair.wait_send()

    def close(chunk, carry):
        given = last & (chunk == chunks - 1)

        @pl.when(chunk == 0)
        def _():
            for half in range(2):
                settle(outbox.at[0, pl.ds(0, n_mom - 1), half], in_send.at[half])

        @pl.when((chunk > 0) & jnp.logical_not(given))
        def _():
            settle(outbox.at[chunk, pl.ds(0, n_mom - 1)], in_send.at[chunk + 1])

        @pl.when(given)
        def _():
            settle(outbox.at[chunk], in_send.at[chunk + 1])

        @pl.when(jnp.logical_not(given))
        def _():
            settle(formed.at[chunk, pl.ds(0, n_mom - 1)], out_send.at[chunk])

        store(0, chunk).wait()
        store(1, chunk).wait()
        return carry

    lax.fori_loop(0, chunks, close, 0)

    @pl.when(first)
    def _():
        settle(formed.at[chunks], out_send.at[chunks])


def write_out(solved, sigma, solved_out, sigma_out, solved_held, sigma_held, in_sem, out_sem):
    blocks = in_sem.shape[2]
    height = solved_held.shape[1] // blocks
    moves = []
    for place, (src, held, dst) in enumerate(((sigma, sigma_held, sigma_out), (solved, solved_held, solved_out))):
        for part in range(2):
            for block in range(blocks):
                span = pl.ds(block * height, height)
                moves.append((
                    pltpu.make_async_copy(src.at[part, 0, span], held.at[part, span], in_sem.at[place, part, block]),
                    pltpu.make_async_copy(held.at[part, span], dst.at[part, 0, span], out_sem.at[place, part, block]),
                ))
    for arrive, _ in moves:
        arrive.start()
    for arrive, leave in moves:
        arrive.wait()
        leave.start()
    for _, leave in moves:
        leave.wait()


def local(source, inverse_diag, coupling, pair_moms, pair_count, pair_weight, vertex):
    rows, columns = source.shape[2], source.shape[3]
    n_mom = lax.axis_size("mom")
    chunks, share = columns // LANES, rows // n_mom
    f32, bf16 = jnp.float32, jnp.bfloat16
    hbm = pl.BlockSpec(memory_space=pltpu.HBM)
    piece = (chunks, n_mom, 2 * share, LANES)
    twice = pltpu.SemaphoreType.DMA((2 * chunks,))
    results = pl.pallas_call(
        kernel,
        out_shape=(
            jax.ShapeDtypeStruct(source.shape, bf16),
            jax.ShapeDtypeStruct(source.shape, f32),
        ),
        in_specs=[hbm] * 7,
        out_specs=(hbm, hbm),
        scratch_shapes=[
            pltpu.SMEM(pair_moms.shape[::-1], jnp.int32),
            pltpu.SMEM(pair_count.shape, jnp.int32),
            pltpu.SMEM(pair_weight.shape[::-1], jnp.int32),
            pltpu.SMEM(vertex.shape, f32),
            pltpu.VMEM((2, rows, columns), f32),
            pltpu.VMEM((2, rows, rows), f32),
            pltpu.VMEM((2, rows, rows), f32),
            *[pltpu.VMEM((2 * rows, rows), bf16) for _ in range(8)],
            pltpu.VMEM((2 * chunks, rows, LANES), f32),
            pltpu.VMEM((2 * chunks, rows, LANES), f32),
            pltpu.VMEM((2 * chunks, rows, LANES), f32),
            pltpu.VMEM((2 * chunks, rows, LANES), f32),
            pltpu.VMEM((chunks, n_mom, 2, share, LANES), bf16),
            pltpu.VMEM((chunks + 1, n_mom, 2, share, LANES), bf16),
            pltpu.VMEM(piece[1:], f32),
            pltpu.VMEM((chunks + 1, *piece[1:]), bf16),
            pltpu.VMEM(piece, bf16),
            pltpu.VMEM((chunks, 2, rows, LANES), bf16),
            pltpu.VMEM((chunks, 2, rows, LANES), f32),
            pltpu.SemaphoreType.DMA((7,)),
            pltpu.SemaphoreType.DMA((2, chunks)),
            pltpu.SemaphoreType.DMA((2,)),
            pltpu.SemaphoreType.DMA((2,)),
            twice, twice, twice, twice, twice,
            *[pltpu.SemaphoreType.DMA((chunks + extra,)) for extra in (1, 2, 1, 0)],
        ],
        compiler_params=pltpu.CompilerParams(
            collective_id=0, has_side_effects=True, vmem_limit_bytes=58 << 20
        ),
    )(
        jnp.transpose(pair_moms, (2, 1, 0)), pair_count, jnp.transpose(pair_weight, (1, 0)), vertex,
        source, inverse_diag, coupling,
    )
    blocks = 4
    return pl.pallas_call(
        write_out,
        out_shape=[jax.ShapeDtypeStruct(result.shape, result.dtype) for result in results],
        in_specs=[hbm] * 2,
        out_specs=(hbm, hbm),
        scratch_shapes=[
            pltpu.VMEM((2, rows, columns), bf16),
            pltpu.VMEM((2, rows, columns), f32),
            pltpu.SemaphoreType.DMA((2, 2, blocks)),
            pltpu.SemaphoreType.DMA((2, 2, blocks)),
        ],
    )(*results)


def solution(mesh):
    return jax.shard_map(
        local,
        mesh=mesh,
        in_specs=(
            P(None, "mom", "tm", None),
            P(None, "mom", "tm", None, None),
            P(None, "mom", "tm", None, None),
            P(),
            P(),
            P(),
            P(),
        ),
        out_specs=(P(None, "mom", "tm", None), P(None, "mom", "tm", None)),
        check_vma=False,
    )
```

```python
import jax
import jax.numpy as jnp
from jax import lax
from jax.experimental import pallas as pl
from jax.experimental.pallas import tpu as pltpu
from jax.sharding import PartitionSpec as P

MESH = pl.DeviceIdType.MESH
LANES = 128
HANDED = 0


def split(value):
    high = value.astype(jnp.bfloat16)
    return high, (value - high.astype(jnp.float32)).astype(jnp.bfloat16)


def dot(left, right):
    return jnp.dot(left, right, preferred_element_type=jnp.float32)


def product(high, low, value_high, value_low):
    return dot(high, value_high) + (dot(high, value_low) + dot(low, value_high))


def join(both):
    rows, width = both.shape[0] // 2, both.shape[1] // 2
    real = both[:rows, :width] - both[rows:, width:]
    imag = both[:rows, width:] + both[rows:, :width]
    return real, imag


def complex_times(high, low, value):
    return join(product(high, low, *split(value)))


def pack(real, imag):
    axis = real.ndim - 1
    lower = lax.broadcasted_iota(jnp.int32, real.shape, axis) < LANES // 2
    return (
        jnp.where(lower, real, pltpu.roll(imag, LANES // 2, axis)),
        jnp.where(lower, pltpu.roll(real, LANES // 2, axis), imag),
    )


def packed_times(high, low, value):
    rows = high.shape[1]
    both = product(high, low, *split(value))
    lower = lax.broadcasted_iota(jnp.int32, (rows, LANES), 1) < LANES // 2
    blocks = []
    for at in range(0, value.shape[1], LANES):
        turned = pltpu.roll(both[rows:, at:at + LANES], LANES // 2, 1)
        blocks.append(both[:rows, at:at + LANES] + jnp.where(lower, -turned, turned))
    return blocks


def kernel(
    moms_hbm, counts_hbm, weights_hbm, vertex_hbm, source_hbm, inverse_hbm, coupling_hbm,
    solved_hbm, sigma_hbm,
    moms, counts, weights, vertex, source, inverse, coupling, left_high, left_low, own_high, own_low, pair_high, pair_low, step_high, step_low,
    driven, lent, entering, greens,
    outbox, inbox, wide, formed, returned, solved, sigma,
    load_sem, store_sem, pair_send, pair_recv, lend_send, lend_recv, pass_send, hop_send, hop_recv, in_send, in_recv, out_send, out_recv,
):
    n_mom, n_tm = lax.axis_size("mom"), lax.axis_size("tm")
    me, turn = lax.axis_index("mom"), lax.axis_index("tm")
    rows, chunks = sigma.shape[2], sigma.shape[0]
    share = rows // n_mom
    slots = moms.shape[1]
    core, plane, planes = lax.rem(turn, 2), turn // 2, n_tm // 2
    partner = turn + 1 - 2 * core
    first, last = plane == 0, plane == planes - 1
    ahead = 2 * (planes - 1)

    loads = [
        pltpu.make_async_copy(here, there, load_sem.at[place])
        for place, (here, there) in enumerate((
            (inverse_hbm.at[:, 0, 0], inverse),
            (source_hbm.at[:, 0], source),
            (coupling_hbm.at[:, 0, 0], coupling),
            (moms_hbm, moms),
            (counts_hbm, counts),
            (weights_hbm, weights),
            (vertex_hbm, vertex),
        ))
    ]
    for load in loads:
        load.start()

    barrier = pltpu.get_barrier_semaphore()

    def greet(step, carry):
        other = lax.rem(me + step, n_mom)
        pl.semaphore_signal(barrier, inc=1, device_id={"mom": other, "tm": turn}, device_id_type=MESH)
        return carry

    lax.fori_loop(1, n_mom, greet, 0)

    for other in (partner, lax.rem(turn + 2, n_tm), lax.rem(turn + n_tm - 2, n_tm)):
        pl.semaphore_signal(barrier, inc=1, device_id={"mom": me, "tm": other}, device_id_type=MESH)

    def drive(chunk):
        columns = pl.ds(pl.multiple_of(chunk * LANES, LANES), LANES)
        forcing = jnp.concatenate([source[0, :, columns], source[1, :, columns]], axis=1)
        for half, value in enumerate(pack(*complex_times(left_high[...], left_low[...], forcing))):
            driven[2 * chunk + half] = value

    loads[0].wait()
    for part in range(2):
        high, low = split(inverse[part])
        left_high[part * rows:(part + 1) * rows, :] = high
        left_low[part * rows:(part + 1) * rows, :] = low
    loads[1].wait()
    drive(0)
    loads[2].wait()

    def keep_matrix(high_ref, low_ref, matrix):
        for part in range(2):
            high, low = split(matrix[part])
            high_ref[part * rows:(part + 1) * rows, :] = high
            low_ref[part * rows:(part + 1) * rows, :] = low

    @pl.when((plane > 0) | (core == 1))
    def _():
        keep_matrix(own_high, own_low, complex_times(
            left_high[...], left_low[...], jnp.concatenate([coupling[0], coupling[1]], axis=1)
        ))

    for load in loads[3:]:
        load.wait()

    pl.semaphore_wait(barrier, n_mom + 2)

    def to(other, src, dst, send_sem, recv_sem):
        return pltpu.make_async_remote_copy(
            src_ref=src, dst_ref=dst, send_sem=send_sem, recv_sem=recv_sem,
            device_id={"mom": me, "tm": other}, device_id_type=MESH,
        )

    def lend(piece):
        return to(partner, driven.at[piece], lent.at[piece], lend_send.at[piece], lend_recv.at[piece])

    def hop(piece):
        return to(
            lax.rem(turn + 2, n_tm), greens.at[piece], entering.at[piece], hop_send.at[piece], hop_recv.at[piece]
        )

    def forward(piece):
        return to(partner, entering.at[piece], entering.at[piece], pass_send.at[piece], hop_recv.at[piece])

    pairs = (
        to(partner, own_high, pair_high, pair_send.at[0], pair_recv.at[0]),
        to(partner, own_low, pair_low, pair_send.at[1], pair_recv.at[1]),
    )

    @pl.when(core == 0)
    def _():
        for half in range(2):
            lend(half).start()

        @pl.when(plane > 0)
        def _():
            for pair in pairs:
                pair.start()
            step_high[...] = own_high[...]
            step_low[...] = own_low[...]

        def drive_and_lend(chunk, carry):
            drive(chunk)
            for half in range(2):
                lend(2 * chunk + half).start()
            return carry

        lax.fori_loop(1, chunks, drive_and_lend, 0)

    @pl.when((core == 1) & (plane > 0))
    def _():
        for pair in pairs:
            pair.wait_recv()
        both = product(
            own_high[...], own_low[...],
            jnp.concatenate([pair_high[:rows, :], pair_high[rows:, :]], axis=1),
            jnp.concatenate([pair_low[:rows, :], pair_low[rows:, :]], axis=1),
        )
        keep_matrix(step_high, step_low, join(both))

    def compose(chunk):
        @pl.when(chunk > 0)
        def _():
            drive(chunk)

        for half in range(2):
            lend(2 * chunk + half).wait_recv()
        value = jnp.concatenate([lent[2 * chunk], lent[2 * chunk + 1]], axis=1)
        for half, block in enumerate(packed_times(own_high[...], own_low[...], value)):
            driven[2 * chunk + half] = driven[2 * chunk + half] + block

    def send(src, dst, send_sem, recv_sem, other, there):
        pltpu.make_async_remote_copy(
            src_ref=src, dst_ref=dst, send_sem=send_sem, recv_sem=recv_sem,
            device_id={"mom": other, "tm": there}, device_id_type=MESH,
        ).start()

    def settle(block, sem):
        pltpu.make_async_copy(block, block, sem).wait()

    def others(body):
        def one(step, carry):
            body(lax.rem(me + step, n_mom))
            return carry

        return one

    def store(which, chunk):
        here, there = ((solved, solved_hbm), (sigma, sigma_hbm))[which]
        columns = pl.ds(pl.multiple_of(chunk * LANES, LANES), LANES)
        return pltpu.make_async_copy(here.at[chunk], there.at[:, 0, :, columns], store_sem.at[which, chunk])

    def advance(piece, carry):
        @pl.when(plane == 0)
        def _():
            greens[piece] = driven[piece]

        @pl.when(plane > 0)
        def _():
            hop(piece).wait_recv()

            @pl.when(core == 1)
            def _():
                forward(piece).start()

            [block] = packed_times(step_high[...], step_low[...], entering[piece])
            greens[piece] = driven[piece] + block

        @pl.when((core == 1) & (plane < planes - 1))
        def _():
            hop(piece).start()

        chunk, half = piece // 2, lax.rem(piece, 2)
        outbox[chunk, :, half] = greens[piece].reshape(n_mom, share, LANES).astype(jnp.bfloat16)
        given = last & (chunk == HANDED)

        @pl.when(jnp.logical_not(given))
        def _():
            inbox[chunk, me, half] = outbox[chunk, me, half]

        @pl.when(jnp.logical_not(given))
        def _():
            lax.fori_loop(1, n_mom, others(lambda other: send(
                outbox.at[chunk, other, half], inbox.at[chunk, me, half], in_send.at[chunk], in_recv.at[chunk],
                other, turn,
            )), 0)

        @pl.when(given)
        def _():
            lax.fori_loop(0, n_mom, others(lambda other: send(
                outbox.at[chunk, other, half], inbox.at[chunks, me, half], in_send.at[chunk], in_recv.at[chunks],
                other, lax.rem(turn + 2, n_tm),
            )), 0)

        return carry

    def keep(chunk):
        for part, value in enumerate(pack(greens[2 * chunk], greens[2 * chunk + 1])):
            solved[chunk, part] = value.astype(jnp.bfloat16)
        store(0, chunk).start()

    def form(chunk, handed):
        if handed:
            settle(inbox.at[chunk], in_recv.at[chunk])
        else:
            settle(inbox.at[chunk, pl.ds(0, n_mom - 1)], in_recv.at[chunk])

        for part, value in enumerate(pack(*(inbox[chunk, :, half].astype(jnp.float32) for half in range(2)))):
            wide[:, part * share:(part + 1) * share] = value

        def one(step, carry):
            mom = lax.rem(me + step, n_mom)
            live = counts[mom]
            total_real = jnp.zeros((share, LANES), jnp.float32)
            total_imag = jnp.zeros((share, LANES), jnp.float32)
            for slot in range(slots):
                first, second, third = (wide[moms[place, slot, mom]] for place in range(3))
                factor = jnp.where(slot < live, vertex[weights[slot, mom]], 0.0)
                ar, ai = first[:share], first[share:]
                br, bi = second[:share], second[share:]
                cr, ci = third[:share], third[share:]
                prod_real = ar * br - ai * bi
                prod_imag = ar * bi + ai * br
                total_real = total_real + factor * (prod_real * cr + prod_imag * ci)
                total_imag = total_imag + factor * (prod_imag * cr - prod_real * ci)
            formed[chunk, mom] = jnp.concatenate([total_real, total_imag], axis=0).astype(jnp.bfloat16)

            if handed:
                send(
                    formed.at[chunk, mom], returned.at[HANDED, me], out_send.at[chunk], out_recv.at[HANDED],
                    mom, turn + ahead,
                )
            else:
                @pl.when(step < n_mom)
                def _():
                    send(
                        formed.at[chunk, mom], returned.at[chunk, me], out_send.at[chunk], out_recv.at[chunk], mom, turn
                    )

            return carry

        lax.fori_loop(1, n_mom + 1, one, 0)
        if not handed:
            returned[chunk, me] = formed[chunk, me]

    def finish(chunk):
        given = last & (chunk == HANDED)

        @pl.when(given)
        def _():
            settle(returned.at[chunk], out_recv.at[chunk])

        @pl.when(jnp.logical_not(given))
        def _():
            settle(returned.at[chunk, pl.ds(0, n_mom - 1)], out_recv.at[chunk])

        value = returned[chunk].astype(jnp.float32)
        sigma[chunk, 0] = value[:, :share].reshape(rows, LANES)
        sigma[chunk, 1] = value[:, share:].reshape(rows, LANES)
        store(1, chunk).start()

    def stage(step, carry):
        @pl.when((core == 1) & (step < chunks))
        def _():
            compose(step)

        @pl.when(step < chunks)
        def _():
            lax.fori_loop(2 * step, 2 * step + 2, advance, 0)
            keep(step)

        @pl.when((step >= 1) & (step < chunks + 1) & jnp.logical_not(last & (step - 1 == HANDED)))
        def _():
            form(step - 1, False)

        @pl.when((step >= 2) & jnp.logical_not(last & (step - 2 == HANDED)))
        def _():
            finish(step - 2)

        return carry

    lax.fori_loop(0, chunks + 2, stage, 0)

    @pl.when(first)
    def _():
        form(chunks, True)

    @pl.when(last)
    def _():
        finish(HANDED)

    def close_piece(piece, carry):
        @pl.when(core == 0)
        def _():
            lend(piece).wait_send()

        @pl.when((core == 1) & (plane > 0))
        def _():
            forward(piece).wait_send()

        @pl.when((core == 1) & (plane < planes - 1))
        def _():
            hop(piece).wait_send()

        return carry

    lax.fori_loop(0, 2 * chunks, close_piece, 0)

    @pl.when((core == 0) & (plane > 0))
    def _():
        for pair in pairs:
            pair.wait_send()

    def close(chunk, carry):
        given = last & (chunk == HANDED)

        @pl.when(jnp.logical_not(given))
        def _():
            settle(outbox.at[chunk, pl.ds(0, n_mom - 1)], in_send.at[chunk])

        @pl.when(given)
        def _():
            settle(outbox.at[chunk], in_send.at[chunk])

        @pl.when(jnp.logical_not(given))
        def _():
            settle(formed.at[chunk, pl.ds(0, n_mom - 1)], out_send.at[chunk])

        store(0, chunk).wait()
        store(1, chunk).wait()
        return carry

    lax.fori_loop(0, chunks, close, 0)

    @pl.when(first)
    def _():
        settle(formed.at[chunks], out_send.at[chunks])


def write_out(solved, sigma, solved_out, sigma_out, solved_held, sigma_held, in_sem, out_sem):
    blocks = in_sem.shape[2]
    height = solved_held.shape[1] // blocks
    moves = []
    for place, (src, held, dst) in enumerate(((sigma, sigma_held, sigma_out), (solved, solved_held, solved_out))):
        for part in range(2):
            for block in range(blocks):
                span = pl.ds(block * height, height)
                moves.append((
                    pltpu.make_async_copy(src.at[part, 0, span], held.at[part, span], in_sem.at[place, part, block]),
                    pltpu.make_async_copy(held.at[part, span], dst.at[part, 0, span], out_sem.at[place, part, block]),
                ))
    for arrive, _ in moves:
        arrive.start()
    for arrive, leave in moves:
        arrive.wait()
        leave.start()
    for _, leave in moves:
        leave.wait()


def local(source, inverse_diag, coupling, pair_moms, pair_count, pair_weight, vertex):
    rows, columns = source.shape[2], source.shape[3]
    n_mom = lax.axis_size("mom")
    chunks, share = columns // LANES, rows // n_mom
    f32, bf16 = jnp.float32, jnp.bfloat16
    hbm = pl.BlockSpec(memory_space=pltpu.HBM)
    piece = (chunks, n_mom, 2 * share, LANES)
    twice = pltpu.SemaphoreType.DMA((2 * chunks,))
    results = pl.pallas_call(
        kernel,
        out_shape=(
            jax.ShapeDtypeStruct(source.shape, bf16),
            jax.ShapeDtypeStruct(source.shape, f32),
        ),
        in_specs=[hbm] * 7,
        out_specs=(hbm, hbm),
        scratch_shapes=[
            pltpu.SMEM(pair_moms.shape[::-1], jnp.int32),
            pltpu.SMEM(pair_count.shape, jnp.int32),
            pltpu.SMEM(pair_weight.shape[::-1], jnp.int32),
            pltpu.SMEM(vertex.shape, f32),
            pltpu.VMEM((2, rows, columns), f32),
            pltpu.VMEM((2, rows, rows), f32),
            pltpu.VMEM((2, rows, rows), f32),
            *[pltpu.VMEM((2 * rows, rows), bf16) for _ in range(8)],
            pltpu.VMEM((2 * chunks, rows, LANES), f32),
            pltpu.VMEM((2 * chunks, rows, LANES), f32),
            pltpu.VMEM((2 * chunks, rows, LANES), f32),
            pltpu.VMEM((2 * chunks, rows, LANES), f32),
            pltpu.VMEM((chunks, n_mom, 2, share, LANES), bf16),
            pltpu.VMEM((chunks + 1, n_mom, 2, share, LANES), bf16),
            pltpu.VMEM(piece[1:], f32),
            pltpu.VMEM((chunks + 1, *piece[1:]), bf16),
            pltpu.VMEM(piece, bf16),
            pltpu.VMEM((chunks, 2, rows, LANES), bf16),
            pltpu.VMEM((chunks, 2, rows, LANES), f32),
            pltpu.SemaphoreType.DMA((7,)),
            pltpu.SemaphoreType.DMA((2, chunks)),
            pltpu.SemaphoreType.DMA((2,)),
            pltpu.SemaphoreType.DMA((2,)),
            twice, twice, twice, twice, twice,
            *[pltpu.SemaphoreType.DMA((chunks + extra,)) for extra in (0, 1, 1, 0)],
        ],
        compiler_params=pltpu.CompilerParams(
            collective_id=0, has_side_effects=True, vmem_limit_bytes=58 << 20
        ),
    )(
        jnp.transpose(pair_moms, (2, 1, 0)), pair_count, jnp.transpose(pair_weight, (1, 0)), vertex,
        source, inverse_diag, coupling,
    )
    blocks = 4
    return pl.pallas_call(
        write_out,
        out_shape=[jax.ShapeDtypeStruct(result.shape, result.dtype) for result in results],
        in_specs=[hbm] * 2,
        out_specs=(hbm, hbm),
        scratch_shapes=[
            pltpu.VMEM((2, rows, columns), bf16),
            pltpu.VMEM((2, rows, columns), f32),
            pltpu.SemaphoreType.DMA((2, 2, blocks)),
            pltpu.SemaphoreType.DMA((2, 2, blocks)),
        ],
    )(*results)


def solution(mesh):
    return jax.shard_map(
        local,
        mesh=mesh,
        in_specs=(
            P(None, "mom", "tm", None),
            P(None, "mom", "tm", None, None),
            P(None, "mom", "tm", None, None),
            P(),
            P(),
            P(),
            P(),
        ),
        out_specs=(P(None, "mom", "tm", None), P(None, "mom", "tm", None)),
        check_vma=False,
    )
```

```python
import jax
import jax.numpy as jnp
from jax import lax
from jax.experimental import pallas as pl
from jax.experimental.pallas import tpu as pltpu
from jax.sharding import PartitionSpec as P

MESH = pl.DeviceIdType.MESH
LANES = 128
HANDED = 0


def split(value):
    high = value.astype(jnp.bfloat16)
    return high, (value - high.astype(jnp.float32)).astype(jnp.bfloat16)


def dot(left, right):
    return jnp.dot(left, right, preferred_element_type=jnp.float32)


def product(high, low, value_high, value_low):
    return dot(high, value_high) + (dot(high, value_low) + dot(low, value_high))


def join(both):
    rows, width = both.shape[0] // 2, both.shape[1] // 2
    real = both[:rows, :width] - both[rows:, width:]
    imag = both[:rows, width:] + both[rows:, :width]
    return real, imag


def complex_times(high, low, value):
    return join(product(high, low, *split(value)))


def pack(real, imag):
    axis = real.ndim - 1
    lower = lax.broadcasted_iota(jnp.int32, real.shape, axis) < LANES // 2
    return (
        jnp.where(lower, real, pltpu.roll(imag, LANES // 2, axis)),
        jnp.where(lower, pltpu.roll(real, LANES // 2, axis), imag),
    )


def packed_times(high, low, value):
    rows = high.shape[1]
    both = product(high, low, *split(value))
    lower = lax.broadcasted_iota(jnp.int32, (rows, LANES), 1) < LANES // 2
    blocks = []
    for at in range(0, value.shape[1], LANES):
        turned = pltpu.roll(both[rows:, at:at + LANES], LANES // 2, 1)
        blocks.append(both[:rows, at:at + LANES] + jnp.where(lower, -turned, turned))
    return blocks


def kernel(
    moms_hbm, counts_hbm, weights_hbm, vertex_hbm, source_hbm, inverse_hbm, coupling_hbm,
    solved_hbm, sigma_hbm,
    moms, counts, weights, vertex, source, inverse, coupling, left_high, left_low, own_high, own_low, pair_high, pair_low, step_high, step_low,
    driven, lent, entering, greens,
    outbox, inbox, wide, formed, returned, solved, sigma,
    load_sem, store_sem, pair_send, pair_recv, lend_send, lend_recv, pass_send, hop_send, hop_recv, in_send, in_recv, out_send, out_recv,
):
    n_mom, n_tm = lax.axis_size("mom"), lax.axis_size("tm")
    me, turn = lax.axis_index("mom"), lax.axis_index("tm")
    rows, chunks = sigma.shape[2], sigma.shape[0]
    share = rows // n_mom
    slots = moms.shape[1]
    core, plane, planes = lax.rem(turn, 2), turn // 2, n_tm // 2
    partner = turn + 1 - 2 * core
    first, last = plane == 0, plane == planes - 1
    ahead = 2 * (planes - 1)

    loads = [
        pltpu.make_async_copy(here, there, load_sem.at[place])
        for place, (here, there) in enumerate((
            (inverse_hbm.at[:, 0, 0], inverse),
            (source_hbm.at[:, 0], source),
            (coupling_hbm.at[:, 0, 0], coupling),
            (moms_hbm, moms),
            (counts_hbm, counts),
            (weights_hbm, weights),
            (vertex_hbm, vertex),
        ))
    ]
    for load in loads:
        load.start()

    barrier = pltpu.get_barrier_semaphore()

    def greet(step, carry):
        other = lax.rem(me + step, n_mom)
        pl.semaphore_signal(barrier, inc=1, device_id={"mom": other, "tm": turn}, device_id_type=MESH)
        return carry

    lax.fori_loop(1, n_mom, greet, 0)

    for other in (partner, lax.rem(turn + 2, n_tm), lax.rem(turn + n_tm - 2, n_tm)):
        pl.semaphore_signal(barrier, inc=1, device_id={"mom": me, "tm": other}, device_id_type=MESH)

    def drive(chunk):
        columns = pl.ds(pl.multiple_of(chunk * LANES, LANES), LANES)
        forcing = jnp.concatenate([source[0, :, columns], source[1, :, columns]], axis=1)
        for half, value in enumerate(pack(*complex_times(left_high[...], left_low[...], forcing))):
            driven[2 * chunk + half] = value

    loads[0].wait()
    for part in range(2):
        high, low = split(inverse[part])
        left_high[part * rows:(part + 1) * rows, :] = high
        left_low[part * rows:(part + 1) * rows, :] = low
    loads[1].wait()
    drive(0)
    loads[2].wait()

    def keep_matrix(high_ref, low_ref, matrix):
        for part in range(2):
            high, low = split(matrix[part])
            high_ref[part * rows:(part + 1) * rows, :] = high
            low_ref[part * rows:(part + 1) * rows, :] = low

    @pl.when((plane > 0) | (core == 1))
    def _():
        keep_matrix(own_high, own_low, complex_times(
            left_high[...], left_low[...], jnp.concatenate([coupling[0], coupling[1]], axis=1)
        ))

    for load in loads[3:]:
        load.wait()

    pl.semaphore_wait(barrier, n_mom + 2)

    def to(other, src, dst, send_sem, recv_sem):
        return pltpu.make_async_remote_copy(
            src_ref=src, dst_ref=dst, send_sem=send_sem, recv_sem=recv_sem,
            device_id={"mom": me, "tm": other}, device_id_type=MESH,
        )

    def lend(piece):
        return to(partner, driven.at[piece], lent.at[piece], lend_send.at[piece], lend_recv.at[piece])

    def hop(piece):
        return to(
            lax.rem(turn + 2, n_tm), greens.at[piece], entering.at[piece], hop_send.at[piece], hop_recv.at[piece]
        )

    def forward(piece):
        return to(partner, entering.at[piece], entering.at[piece], pass_send.at[piece], hop_recv.at[piece])

    pairs = (
        to(partner, own_high, pair_high, pair_send.at[0], pair_recv.at[0]),
        to(partner, own_low, pair_low, pair_send.at[1], pair_recv.at[1]),
    )

    @pl.when(core == 0)
    def _():
        for half in range(2):
            lend(half).start()

        @pl.when(plane > 0)
        def _():
            for pair in pairs:
                pair.start()
            step_high[...] = own_high[...]
            step_low[...] = own_low[...]

        def drive_and_lend(chunk, carry):
            drive(chunk)
            for half in range(2):
                lend(2 * chunk + half).start()
            return carry

        lax.fori_loop(1, chunks, drive_and_lend, 0)

    @pl.when((core == 1) & (plane > 0))
    def _():
        for pair in pairs:
            pair.wait_recv()
        both = product(
            own_high[...], own_low[...],
            jnp.concatenate([pair_high[:rows, :], pair_high[rows:, :]], axis=1),
            jnp.concatenate([pair_low[:rows, :], pair_low[rows:, :]], axis=1),
        )
        keep_matrix(step_high, step_low, join(both))

    def compose(chunk):
        @pl.when(chunk > 0)
        def _():
            drive(chunk)

        for half in range(2):
            lend(2 * chunk + half).wait_recv()
        value = jnp.concatenate([lent[2 * chunk], lent[2 * chunk + 1]], axis=1)
        for half, block in enumerate(packed_times(own_high[...], own_low[...], value)):
            driven[2 * chunk + half] = driven[2 * chunk + half] + block

    def send(src, dst, send_sem, recv_sem, other, there):
        pltpu.make_async_remote_copy(
            src_ref=src, dst_ref=dst, send_sem=send_sem, recv_sem=recv_sem,
            device_id={"mom": other, "tm": there}, device_id_type=MESH,
        ).start()

    def settle(block, sem):
        pltpu.make_async_copy(block, block, sem).wait()

    def others(body):
        def one(step, carry):
            body(lax.rem(me + step, n_mom))
            return carry

        return one

    def store(which, chunk):
        here, there = ((solved, solved_hbm), (sigma, sigma_hbm))[which]
        columns = pl.ds(pl.multiple_of(chunk * LANES, LANES), LANES)
        return pltpu.make_async_copy(here.at[chunk], there.at[:, 0, :, columns], store_sem.at[which, chunk])

    def advance(piece, carry):
        @pl.when(plane == 0)
        def _():
            greens[piece] = driven[piece]

        @pl.when(plane > 0)
        def _():
            hop(piece).wait_recv()

            @pl.when(core == 1)
            def _():
                forward(piece).start()

            [block] = packed_times(step_high[...], step_low[...], entering[piece])
            greens[piece] = driven[piece] + block

        @pl.when((core == 1) & (plane < planes - 1))
        def _():
            hop(piece).start()

        chunk, half = piece // 2, lax.rem(piece, 2)
        outbox[chunk, :, half] = greens[piece].reshape(n_mom, share, LANES).astype(jnp.bfloat16)
        given = last & (chunk == HANDED)

        @pl.when(jnp.logical_not(given))
        def _():
            inbox[chunk, me, half] = outbox[chunk, me, half]

        @pl.when(jnp.logical_not(given))
        def _():
            lax.fori_loop(1, n_mom, others(lambda other: send(
                outbox.at[chunk, other, half], inbox.at[chunk, me, half], in_send.at[chunk], in_recv.at[chunk],
                other, turn,
            )), 0)

        @pl.when(given)
        def _():
            lax.fori_loop(0, n_mom, others(lambda other: send(
                outbox.at[chunk, other, half], inbox.at[chunks, me, half], in_send.at[chunk], in_recv.at[chunks],
                other, lax.rem(turn + 2, n_tm),
            )), 0)

        return carry

    def keep(chunk):
        for part, value in enumerate(pack(greens[2 * chunk], greens[2 * chunk + 1])):
            solved[chunk, part] = value.astype(jnp.bfloat16)
        store(0, chunk).start()

    def form(chunk, handed):
        if handed:
            settle(inbox.at[chunk], in_recv.at[chunk])
        else:
            settle(inbox.at[chunk, pl.ds(0, n_mom - 1)], in_recv.at[chunk])

        for part, value in enumerate(pack(*(inbox[chunk, :, half].astype(jnp.float32) for half in range(2)))):
            wide[:, part * share:(part + 1) * share] = value

        def one(step, carry):
            mom = lax.rem(me + step, n_mom)
            live = counts[mom]
            total_real = jnp.zeros((share, LANES), jnp.float32)
            total_imag = jnp.zeros((share, LANES), jnp.float32)
            for slot in range(slots):
                first, second, third = (wide[moms[place, slot, mom]] for place in range(3))
                factor = jnp.where(slot < live, vertex[weights[slot, mom]], 0.0)
                ar, ai = first[:share], first[share:]
                br, bi = second[:share], second[share:]
                cr, ci = third[:share], third[share:]
                prod_real = ar * br - ai * bi
                prod_imag = ar * bi + ai * br
                total_real = total_real + factor * (prod_real * cr + prod_imag * ci)
                total_imag = total_imag + factor * (prod_imag * cr - prod_real * ci)
            formed[chunk, mom] = jnp.concatenate([total_real, total_imag], axis=0).astype(jnp.bfloat16)

            if handed:
                send(
                    formed.at[chunk, mom], returned.at[HANDED, me], out_send.at[chunk], out_recv.at[HANDED],
                    mom, turn + ahead,
                )
            else:
                @pl.when(step < n_mom)
                def _():
                    send(
                        formed.at[chunk, mom], returned.at[chunk, me], out_send.at[chunk], out_recv.at[chunk], mom, turn
                    )

            return carry

        lax.fori_loop(1, n_mom + 1, one, 0)
        if not handed:
            returned[chunk, me] = formed[chunk, me]

    def finish(chunk):
        given = last & (chunk == HANDED)

        @pl.when(given)
        def _():
            settle(returned.at[chunk], out_recv.at[chunk])

        @pl.when(jnp.logical_not(given))
        def _():
            settle(returned.at[chunk, pl.ds(0, n_mom - 1)], out_recv.at[chunk])

        value = returned[chunk].astype(jnp.float32)
        sigma[chunk, 0] = value[:, :share].reshape(rows, LANES)
        sigma[chunk, 1] = value[:, share:].reshape(rows, LANES)
        store(1, chunk).start()

    def solve(chunk, carry):
        @pl.when(core == 1)
        def _():
            compose(chunk)

        lax.fori_loop(2 * chunk, 2 * chunk + 2, advance, 0)
        keep(chunk)
        return carry

    def form_own(chunk, carry):
        @pl.when(jnp.logical_not(last & (chunk == HANDED)))
        def _():
            form(chunk, False)

        return carry

    def finish_own(chunk, carry):
        finish(chunk)
        return carry

    lax.fori_loop(0, chunks, solve, 0)
    lax.fori_loop(0, chunks, form_own, 0)

    @pl.when(first)
    def _():
        form(chunks, True)

    lax.fori_loop(0, chunks, finish_own, 0)

    def close_piece(piece, carry):
        @pl.when(core == 0)
        def _():
            lend(piece).wait_send()

        @pl.when((core == 1) & (plane > 0))
        def _():
            forward(piece).wait_send()

        @pl.when((core == 1) & (plane < planes - 1))
        def _():
            hop(piece).wait_send()

        return carry

    lax.fori_loop(0, 2 * chunks, close_piece, 0)

    @pl.when((core == 0) & (plane > 0))
    def _():
        for pair in pairs:
            pair.wait_send()

    def close(chunk, carry):
        given = last & (chunk == HANDED)

        @pl.when(jnp.logical_not(given))
        def _():
            settle(outbox.at[chunk, pl.ds(0, n_mom - 1)], in_send.at[chunk])

        @pl.when(given)
        def _():
            settle(outbox.at[chunk], in_send.at[chunk])

        @pl.when(jnp.logical_not(given))
        def _():
            settle(formed.at[chunk, pl.ds(0, n_mom - 1)], out_send.at[chunk])

        store(0, chunk).wait()
        store(1, chunk).wait()
        return carry

    lax.fori_loop(0, chunks, close, 0)

    @pl.when(first)
    def _():
        settle(formed.at[chunks], out_send.at[chunks])


def write_out(solved, sigma, solved_out, sigma_out, solved_held, sigma_held, in_sem, out_sem):
    blocks = in_sem.shape[2]
    height = solved_held.shape[1] // blocks
    moves = []
    for place, (src, held, dst) in enumerate(((sigma, sigma_held, sigma_out), (solved, solved_held, solved_out))):
        for part in range(2):
            for block in range(blocks):
                span = pl.ds(block * height, height)
                moves.append((
                    pltpu.make_async_copy(src.at[part, 0, span], held.at[part, span], in_sem.at[place, part, block]),
                    pltpu.make_async_copy(held.at[part, span], dst.at[part, 0, span], out_sem.at[place, part, block]),
                ))
    for arrive, _ in moves:
        arrive.start()
    for arrive, leave in moves:
        arrive.wait()
        leave.start()
    for _, leave in moves:
        leave.wait()


def local(source, inverse_diag, coupling, pair_moms, pair_count, pair_weight, vertex):
    rows, columns = source.shape[2], source.shape[3]
    n_mom = lax.axis_size("mom")
    chunks, share = columns // LANES, rows // n_mom
    f32, bf16 = jnp.float32, jnp.bfloat16
    hbm = pl.BlockSpec(memory_space=pltpu.HBM)
    piece = (chunks, n_mom, 2 * share, LANES)
    twice = pltpu.SemaphoreType.DMA((2 * chunks,))
    results = pl.pallas_call(
        kernel,
        out_shape=(
            jax.ShapeDtypeStruct(source.shape, bf16),
            jax.ShapeDtypeStruct(source.shape, f32),
        ),
        in_specs=[hbm] * 7,
        out_specs=(hbm, hbm),
        scratch_shapes=[
            pltpu.SMEM(pair_moms.shape[::-1], jnp.int32),
            pltpu.SMEM(pair_count.shape, jnp.int32),
            pltpu.SMEM(pair_weight.shape[::-1], jnp.int32),
            pltpu.SMEM(vertex.shape, f32),
            pltpu.VMEM((2, rows, columns), f32),
            pltpu.VMEM((2, rows, rows), f32),
            pltpu.VMEM((2, rows, rows), f32),
            *[pltpu.VMEM((2 * rows, rows), bf16) for _ in range(8)],
            pltpu.VMEM((2 * chunks, rows, LANES), f32),
            pltpu.VMEM((2 * chunks, rows, LANES), f32),
            pltpu.VMEM((2 * chunks, rows, LANES), f32),
            pltpu.VMEM((2 * chunks, rows, LANES), f32),
            pltpu.VMEM((chunks, n_mom, 2, share, LANES), bf16),
            pltpu.VMEM((chunks + 1, n_mom, 2, share, LANES), bf16),
            pltpu.VMEM(piece[1:], f32),
            pltpu.VMEM((chunks + 1, *piece[1:]), bf16),
            pltpu.VMEM(piece, bf16),
            pltpu.VMEM((chunks, 2, rows, LANES), bf16),
            pltpu.VMEM((chunks, 2, rows, LANES), f32),
            pltpu.SemaphoreType.DMA((7,)),
            pltpu.SemaphoreType.DMA((2, chunks)),
            pltpu.SemaphoreType.DMA((2,)),
            pltpu.SemaphoreType.DMA((2,)),
            twice, twice, twice, twice, twice,
            *[pltpu.SemaphoreType.DMA((chunks + extra,)) for extra in (0, 1, 1, 0)],
        ],
        compiler_params=pltpu.CompilerParams(
            collective_id=0, has_side_effects=True, vmem_limit_bytes=58 << 20
        ),
    )(
        jnp.transpose(pair_moms, (2, 1, 0)), pair_count, jnp.transpose(pair_weight, (1, 0)), vertex,
        source, inverse_diag, coupling,
    )
    blocks = 4
    return pl.pallas_call(
        write_out,
        out_shape=[jax.ShapeDtypeStruct(result.shape, result.dtype) for result in results],
        in_specs=[hbm] * 2,
        out_specs=(hbm, hbm),
        scratch_shapes=[
            pltpu.VMEM((2, rows, columns), bf16),
            pltpu.VMEM((2, rows, columns), f32),
            pltpu.SemaphoreType.DMA((2, 2, blocks)),
            pltpu.SemaphoreType.DMA((2, 2, blocks)),
        ],
    )(*results)


def solution(mesh):
    return jax.shard_map(
        local,
        mesh=mesh,
        in_specs=(
            P(None, "mom", "tm", None),
            P(None, "mom", "tm", None, None),
            P(None, "mom", "tm", None, None),
            P(),
            P(),
            P(),
            P(),
        ),
        out_specs=(P(None, "mom", "tm", None), P(None, "mom", "tm", None)),
        check_vma=False,
    )
```

```python
import functools

import jax
import jax.numpy as jnp
from jax import lax
from jax.experimental import pallas as pl
from jax.experimental.pallas import tpu as pltpu
from jax.sharding import PartitionSpec as P

MESH = pl.DeviceIdType.MESH
LANES = 128
HANDED = ((0, 0), (0, 1), (1, 0))


def split(value):
    high = value.astype(jnp.bfloat16)
    return high, (value - high.astype(jnp.float32)).astype(jnp.bfloat16)


def dot(left, right):
    return jnp.dot(left, right, preferred_element_type=jnp.float32)


def product(high, low, value_high, value_low):
    return dot(high, value_high) + (dot(high, value_low) + dot(low, value_high))


def join(both):
    rows, width = both.shape[0] // 2, both.shape[1] // 2
    real = both[:rows, :width] - both[rows:, width:]
    imag = both[:rows, width:] + both[rows:, :width]
    return real, imag


def complex_times(high, low, value):
    return join(product(high, low, *split(value)))


def pack(real, imag):
    axis = real.ndim - 1
    lower = lax.broadcasted_iota(jnp.int32, real.shape, axis) < LANES // 2
    return (
        jnp.where(lower, real, pltpu.roll(imag, LANES // 2, axis)),
        jnp.where(lower, pltpu.roll(real, LANES // 2, axis), imag),
    )


def packed_times(high, low, value):
    rows = high.shape[1]
    both = product(high, low, *split(value))
    lower = lax.broadcasted_iota(jnp.int32, (rows, LANES), 1) < LANES // 2
    blocks = []
    for at in range(0, value.shape[1], LANES):
        turned = pltpu.roll(both[rows:, at:at + LANES], LANES // 2, 1)
        blocks.append(both[:rows, at:at + LANES] + jnp.where(lower, -turned, turned))
    return blocks


def kernel(
    moms_hbm, counts_hbm, weights_hbm, vertex_hbm, source_hbm, inverse_hbm, coupling_hbm,
    solved_hbm, sigma_hbm,
    moms, counts, weights, vertex, source, inverse, coupling, left_high, left_low, own_high, own_low, pair_high, pair_low, step_high, step_low,
    driven, lent, entering, greens,
    outbox, inbox, wide, formed, returned, solved, sigma,
    load_sem, store_sem, pair_send, pair_recv, lend_send, lend_recv, pass_send, hop_send, hop_recv, in_send, in_recv, out_send, out_recv,
):
    n_mom, n_tm = lax.axis_size("mom"), lax.axis_size("tm")
    me, turn = lax.axis_index("mom"), lax.axis_index("tm")
    rows, chunks = sigma.shape[2], sigma.shape[0]
    share = rows // n_mom
    slots = moms.shape[1]
    core, plane, planes = lax.rem(turn, 2), turn // 2, n_tm // 2
    partner = turn + 1 - 2 * core
    first, behind = plane == 0, planes - 1 - plane

    def is_handed(chunk):
        return functools.reduce(jnp.logical_or, [(behind == back) & (chunk == which) for back, which in HANDED])


    loads = [
        pltpu.make_async_copy(here, there, load_sem.at[place])
        for place, (here, there) in enumerate((
            (inverse_hbm.at[:, 0, 0], inverse),
            (source_hbm.at[:, 0], source),
            (coupling_hbm.at[:, 0, 0], coupling),
            (moms_hbm, moms),
            (counts_hbm, counts),
            (weights_hbm, weights),
            (vertex_hbm, vertex),
        ))
    ]
    for load in loads:
        load.start()

    barrier = pltpu.get_barrier_semaphore()

    def greet(step, carry):
        other = lax.rem(me + step, n_mom)
        pl.semaphore_signal(barrier, inc=1, device_id={"mom": other, "tm": turn}, device_id_type=MESH)
        return carry

    lax.fori_loop(1, n_mom, greet, 0)

    for other in (partner, lax.rem(turn + 2, n_tm), lax.rem(turn + n_tm - 2, n_tm)):
        pl.semaphore_signal(barrier, inc=1, device_id={"mom": me, "tm": other}, device_id_type=MESH)

    def drive(chunk):
        columns = pl.ds(pl.multiple_of(chunk * LANES, LANES), LANES)
        forcing = jnp.concatenate([source[0, :, columns], source[1, :, columns]], axis=1)
        for half, value in enumerate(pack(*complex_times(left_high[...], left_low[...], forcing))):
            driven[2 * chunk + half] = value

    loads[0].wait()
    for part in range(2):
        high, low = split(inverse[part])
        left_high[part * rows:(part + 1) * rows, :] = high
        left_low[part * rows:(part + 1) * rows, :] = low
    loads[1].wait()
    drive(0)
    loads[2].wait()

    def keep_matrix(high_ref, low_ref, matrix):
        for part in range(2):
            high, low = split(matrix[part])
            high_ref[part * rows:(part + 1) * rows, :] = high
            low_ref[part * rows:(part + 1) * rows, :] = low

    @pl.when((plane > 0) | (core == 1))
    def _():
        keep_matrix(own_high, own_low, complex_times(
            left_high[...], left_low[...], jnp.concatenate([coupling[0], coupling[1]], axis=1)
        ))

    for load in loads[3:]:
        load.wait()

    pl.semaphore_wait(barrier, n_mom + 2)

    def to(other, src, dst, send_sem, recv_sem):
        return pltpu.make_async_remote_copy(
            src_ref=src, dst_ref=dst, send_sem=send_sem, recv_sem=recv_sem,
            device_id={"mom": me, "tm": other}, device_id_type=MESH,
        )

    def lend(piece):
        return to(partner, driven.at[piece], lent.at[piece], lend_send.at[piece], lend_recv.at[piece])

    def hop(piece):
        return to(
            lax.rem(turn + 2, n_tm), greens.at[piece], entering.at[piece], hop_send.at[piece], hop_recv.at[piece]
        )

    def forward(piece):
        return to(partner, entering.at[piece], entering.at[piece], pass_send.at[piece], hop_recv.at[piece])

    pairs = (
        to(partner, own_high, pair_high, pair_send.at[0], pair_recv.at[0]),
        to(partner, own_low, pair_low, pair_send.at[1], pair_recv.at[1]),
    )

    @pl.when(core == 0)
    def _():
        for half in range(2):
            lend(half).start()

        @pl.when(plane > 0)
        def _():
            for pair in pairs:
                pair.start()
            step_high[...] = own_high[...]
            step_low[...] = own_low[...]

        def drive_and_lend(chunk, carry):
            drive(chunk)
            for half in range(2):
                lend(2 * chunk + half).start()
            return carry

        lax.fori_loop(1, chunks, drive_and_lend, 0)

    @pl.when((core == 1) & (plane > 0))
    def _():
        for pair in pairs:
            pair.wait_recv()
        both = product(
            own_high[...], own_low[...],
            jnp.concatenate([pair_high[:rows, :], pair_high[rows:, :]], axis=1),
            jnp.concatenate([pair_low[:rows, :], pair_low[rows:, :]], axis=1),
        )
        keep_matrix(step_high, step_low, join(both))

    def compose(chunk):
        @pl.when(chunk > 0)
        def _():
            drive(chunk)

        for half in range(2):
            lend(2 * chunk + half).wait_recv()
        value = jnp.concatenate([lent[2 * chunk], lent[2 * chunk + 1]], axis=1)
        for half, block in enumerate(packed_times(own_high[...], own_low[...], value)):
            driven[2 * chunk + half] = driven[2 * chunk + half] + block

    def send(src, dst, send_sem, recv_sem, other, there):
        pltpu.make_async_remote_copy(
            src_ref=src, dst_ref=dst, send_sem=send_sem, recv_sem=recv_sem,
            device_id={"mom": other, "tm": there}, device_id_type=MESH,
        ).start()

    def settle(block, sem):
        pltpu.make_async_copy(block, block, sem).wait()

    def others(body):
        def one(step, carry):
            body(lax.rem(me + step, n_mom))
            return carry

        return one

    def store(which, chunk):
        here, there = ((solved, solved_hbm), (sigma, sigma_hbm))[which]
        columns = pl.ds(pl.multiple_of(chunk * LANES, LANES), LANES)
        return pltpu.make_async_copy(here.at[chunk], there.at[:, 0, :, columns], store_sem.at[which, chunk])

    def advance(piece, carry):
        @pl.when(plane == 0)
        def _():
            greens[piece] = driven[piece]

        @pl.when(plane > 0)
        def _():
            hop(piece).wait_recv()

            @pl.when(core == 1)
            def _():
                forward(piece).start()

            [block] = packed_times(step_high[...], step_low[...], entering[piece])
            greens[piece] = driven[piece] + block

        @pl.when((core == 1) & (plane < planes - 1))
        def _():
            hop(piece).start()

        chunk, half = piece // 2, lax.rem(piece, 2)
        outbox[chunk, :, half] = greens[piece].reshape(n_mom, share, LANES).astype(jnp.bfloat16)
        given = is_handed(chunk)

        @pl.when(jnp.logical_not(given))
        def _():
            inbox[chunk, me, half] = outbox[chunk, me, half]

        def spread(part):
            @pl.when(jnp.logical_not(given))
            def _():
                for step in range(1, n_mom):
                    other = lax.rem(me + step, n_mom)
                    send(
                        outbox.at[(chunk, other, *part)], inbox.at[(chunk, me, *part)],
                        in_send.at[chunk], in_recv.at[chunk], other, turn,
                    )

            @pl.when(given)
            def _():
                slot = chunks + 2 * behind + chunk
                lax.fori_loop(0, n_mom, others(lambda other: send(
                    outbox.at[(chunk, other, *part)], inbox.at[(slot, me, *part)],
                    in_send.at[chunk], in_recv.at[slot], other, core,
                )), 0)

        @pl.when(chunk == 0)
        def _():
            spread((half,))

        @pl.when((chunk > 0) & (half == 1))
        def _():
            spread(())

        return carry

    def keep(chunk):
        for part, value in enumerate(pack(greens[2 * chunk], greens[2 * chunk + 1])):
            solved[chunk, part] = value.astype(jnp.bfloat16)
        store(0, chunk).start()

    def form(chunk, handed):
        if handed:
            settle(inbox.at[chunk], in_recv.at[chunk])
        else:
            settle(inbox.at[chunk, pl.ds(0, n_mom - 1)], in_recv.at[chunk])

        for part, value in enumerate(pack(*(inbox[chunk, :, half].astype(jnp.float32) for half in range(2)))):
            wide[:, part * share:(part + 1) * share] = value

        def one(step, carry):
            mom = lax.rem(me + step, n_mom)
            live = counts[mom]
            total_real = jnp.zeros((share, LANES), jnp.float32)
            total_imag = jnp.zeros((share, LANES), jnp.float32)
            for slot in range(slots):
                first, second, third = (wide[moms[place, slot, mom]] for place in range(3))
                factor = jnp.where(slot < live, vertex[weights[slot, mom]], 0.0)
                ar, ai = first[:share], first[share:]
                br, bi = second[:share], second[share:]
                cr, ci = third[:share], third[share:]
                prod_real = ar * br - ai * bi
                prod_imag = ar * bi + ai * br
                total_real = total_real + factor * (prod_real * cr + prod_imag * ci)
                total_imag = total_imag + factor * (prod_imag * cr - prod_real * ci)
            formed[chunk, mom] = jnp.concatenate([total_real, total_imag], axis=0).astype(jnp.bfloat16)

            if handed:
                send(
                    formed.at[chunk, mom], returned.at[lax.rem(chunk - chunks, 2), me], out_send.at[chunk],
                    out_recv.at[lax.rem(chunk - chunks, 2)], mom, turn + 2 * (planes - 1 - (chunk - chunks) // 2),
                )
            else:
                @pl.when(step < n_mom)
                def _():
                    send(
                        formed.at[chunk, mom], returned.at[chunk, me], out_send.at[chunk], out_recv.at[chunk], mom, turn
                    )

            return carry

        lax.fori_loop(1, n_mom + 1, one, 0)
        if not handed:
            returned[chunk, me] = formed[chunk, me]

    def finish(chunk):
        given = is_handed(chunk)

        @pl.when(given)
        def _():
            settle(returned.at[chunk], out_recv.at[chunk])

        @pl.when(jnp.logical_not(given))
        def _():
            settle(returned.at[chunk, pl.ds(0, n_mom - 1)], out_recv.at[chunk])

        value = returned[chunk].astype(jnp.float32)
        sigma[chunk, 0] = value[:, :share].reshape(rows, LANES)
        sigma[chunk, 1] = value[:, share:].reshape(rows, LANES)
        store(1, chunk).start()

    def solve(chunk, carry):
        @pl.when((core == 1) & (chunk > plane))
        def _():
            compose(chunk)

        lax.fori_loop(2 * chunk, 2 * chunk + 2, advance, 0)
        keep(chunk)
        return carry

    def form_own(chunk, carry):
        @pl.when(jnp.logical_not(is_handed(chunk)))
        def _():
            form(chunk, False)

        return carry

    def finish_own(chunk, carry):
        finish(chunk)
        return carry

    @pl.when(core == 1)
    def _():
        def compose_early(chunk, carry):
            compose(chunk)
            return carry

        lax.fori_loop(0, lax.min(chunks, plane + 1), compose_early, 0)

    lax.fori_loop(0, chunks, solve, 0)
    lax.fori_loop(0, chunks, form_own, 0)

    @pl.when(first)
    def _():
        def form_other(place, carry):
            form(chunks + lax.rem(place + len(HANDED) - 1, len(HANDED)), True)
            return carry

        lax.fori_loop(0, len(HANDED), form_other, 0)

    lax.fori_loop(0, chunks, finish_own, 0)

    def close_piece(piece, carry):
        @pl.when(core == 0)
        def _():
            lend(piece).wait_send()

        @pl.when((core == 1) & (plane > 0))
        def _():
            forward(piece).wait_send()

        @pl.when((core == 1) & (plane < planes - 1))
        def _():
            hop(piece).wait_send()

        return carry

    lax.fori_loop(0, 2 * chunks, close_piece, 0)

    @pl.when((core == 0) & (plane > 0))
    def _():
        for pair in pairs:
            pair.wait_send()

    def close(chunk, carry):
        given = is_handed(chunk)

        @pl.when(jnp.logical_not(given))
        def _():
            settle(outbox.at[chunk, pl.ds(0, n_mom - 1)], in_send.at[chunk])

        @pl.when(given)
        def _():
            settle(outbox.at[chunk], in_send.at[chunk])

        @pl.when(jnp.logical_not(given))
        def _():
            settle(formed.at[chunk, pl.ds(0, n_mom - 1)], out_send.at[chunk])

        store(0, chunk).wait()
        store(1, chunk).wait()
        return carry

    lax.fori_loop(0, chunks, close, 0)

    @pl.when(first)
    def _():
        def close_other(slot, carry):
            settle(formed.at[slot], out_send.at[slot])
            return carry

        lax.fori_loop(chunks, chunks + len(HANDED), close_other, 0)


def write_out(solved, sigma, solved_out, sigma_out, solved_held, sigma_held, in_sem, out_sem):
    blocks = in_sem.shape[2]
    height = solved_held.shape[1] // blocks
    moves = []
    for place, (src, held, dst) in enumerate(((sigma, sigma_held, sigma_out), (solved, solved_held, solved_out))):
        for part in range(2):
            for block in range(blocks):
                span = pl.ds(block * height, height)
                moves.append((
                    pltpu.make_async_copy(src.at[part, 0, span], held.at[part, span], in_sem.at[place, part, block]),
                    pltpu.make_async_copy(held.at[part, span], dst.at[part, 0, span], out_sem.at[place, part, block]),
                ))
    for arrive, _ in moves:
        arrive.start()
    for arrive, leave in moves:
        arrive.wait()
        leave.start()
    for _, leave in moves:
        leave.wait()


def local(source, inverse_diag, coupling, pair_moms, pair_count, pair_weight, vertex):
    rows, columns = source.shape[2], source.shape[3]
    n_mom = lax.axis_size("mom")
    chunks, share = columns // LANES, rows // n_mom
    f32, bf16 = jnp.float32, jnp.bfloat16
    hbm = pl.BlockSpec(memory_space=pltpu.HBM)
    piece = (chunks, n_mom, 2 * share, LANES)
    twice = pltpu.SemaphoreType.DMA((2 * chunks,))
    results = pl.pallas_call(
        kernel,
        out_shape=(
            jax.ShapeDtypeStruct(source.shape, bf16),
            jax.ShapeDtypeStruct(source.shape, f32),
        ),
        in_specs=[hbm] * 7,
        out_specs=(hbm, hbm),
        scratch_shapes=[
            pltpu.SMEM(pair_moms.shape[::-1], jnp.int32),
            pltpu.SMEM(pair_count.shape, jnp.int32),
            pltpu.SMEM(pair_weight.shape[::-1], jnp.int32),
            pltpu.SMEM(vertex.shape, f32),
            pltpu.VMEM((2, rows, columns), f32),
            pltpu.VMEM((2, rows, rows), f32),
            pltpu.VMEM((2, rows, rows), f32),
            *[pltpu.VMEM((2 * rows, rows), bf16) for _ in range(8)],
            pltpu.VMEM((2 * chunks, rows, LANES), f32),
            pltpu.VMEM((2 * chunks, rows, LANES), f32),
            pltpu.VMEM((2 * chunks, rows, LANES), f32),
            pltpu.VMEM((2 * chunks, rows, LANES), f32),
            pltpu.VMEM((chunks, n_mom, 2, share, LANES), bf16),
            pltpu.VMEM((chunks + len(HANDED), n_mom, 2, share, LANES), bf16),
            pltpu.VMEM(piece[1:], f32),
            pltpu.VMEM((chunks + len(HANDED), *piece[1:]), bf16),
            pltpu.VMEM(piece, bf16),
            pltpu.VMEM((chunks, 2, rows, LANES), bf16),
            pltpu.VMEM((chunks, 2, rows, LANES), f32),
            pltpu.SemaphoreType.DMA((7,)),
            pltpu.SemaphoreType.DMA((2, chunks)),
            pltpu.SemaphoreType.DMA((2,)),
            pltpu.SemaphoreType.DMA((2,)),
            twice, twice, twice, twice, twice,
            *[pltpu.SemaphoreType.DMA((chunks + extra,)) for extra in (0, len(HANDED), len(HANDED), 0)],
        ],
        compiler_params=pltpu.CompilerParams(
            collective_id=0, has_side_effects=True, vmem_limit_bytes=58 << 20
        ),
    )(
        jnp.transpose(pair_moms, (2, 1, 0)), pair_count, jnp.transpose(pair_weight, (1, 0)), vertex,
        source, inverse_diag, coupling,
    )
    blocks = 4
    return pl.pallas_call(
        write_out,
        out_shape=[jax.ShapeDtypeStruct(result.shape, result.dtype) for result in results],
        in_specs=[hbm] * 2,
        out_specs=(hbm, hbm),
        scratch_shapes=[
            pltpu.VMEM((2, rows, columns), bf16),
            pltpu.VMEM((2, rows, columns), f32),
            pltpu.SemaphoreType.DMA((2, 2, blocks)),
            pltpu.SemaphoreType.DMA((2, 2, blocks)),
        ],
    )(*results)


def solution(mesh):
    return jax.shard_map(
        local,
        mesh=mesh,
        in_specs=(
            P(None, "mom", "tm", None),
            P(None, "mom", "tm", None, None),
            P(None, "mom", "tm", None, None),
            P(),
            P(),
            P(),
            P(),
        ),
        out_specs=(P(None, "mom", "tm", None), P(None, "mom", "tm", None)),
        check_vma=False,
    )
```

```python
import functools

import jax
import jax.numpy as jnp
from jax import lax
from jax.experimental import pallas as pl
from jax.experimental.pallas import tpu as pltpu
from jax.sharding import PartitionSpec as P

MESH = pl.DeviceIdType.MESH
LANES = 128
EXTRA = 16
HANDED = ((0, 0), (0, 1), (1, 0))


def split(value):
    high = value.astype(jnp.bfloat16)
    return high, (value - high.astype(jnp.float32)).astype(jnp.bfloat16)


def dot(left, right):
    return jnp.dot(left, right, preferred_element_type=jnp.float32)


def product(high, low, value_high, value_low):
    return dot(high, value_high) + (dot(high, value_low) + dot(low, value_high))


def join(both):
    rows, width = both.shape[0] // 2, both.shape[1] // 2
    real = both[:rows, :width] - both[rows:, width:]
    imag = both[:rows, width:] + both[rows:, :width]
    return real, imag


def complex_times(high, low, value):
    return join(product(high, low, *split(value)))


def pack(real, imag):
    axis = real.ndim - 1
    lower = lax.broadcasted_iota(jnp.int32, real.shape, axis) < LANES // 2
    return (
        jnp.where(lower, real, pltpu.roll(imag, LANES // 2, axis)),
        jnp.where(lower, pltpu.roll(real, LANES // 2, axis), imag),
    )


def packed_times(high, low, value):
    rows = high.shape[1]
    both = product(high, low, *split(value))
    lower = lax.broadcasted_iota(jnp.int32, (rows, LANES), 1) < LANES // 2
    blocks = []
    for at in range(0, value.shape[1], LANES):
        turned = pltpu.roll(both[rows:, at:at + LANES], LANES // 2, 1)
        blocks.append(both[:rows, at:at + LANES] + jnp.where(lower, -turned, turned))
    return blocks


def encode(value):
    peak = jnp.max(jnp.abs(value), axis=0, keepdims=True)
    level = jnp.ceil(jnp.log2(jnp.maximum(peak * 1.0001, 1e-30)))
    levels = jnp.broadcast_to(level, (EXTRA, value.shape[1]))
    code = jnp.concatenate([jnp.round(value * jnp.exp2(15.0 - level)), levels], axis=0)
    return code.astype(jnp.int32).astype(jnp.int16)


def decode(code):
    value = code.astype(jnp.int32).astype(jnp.float32)
    rows = code.shape[0] - EXTRA
    return value[:rows] * jnp.exp2(value[rows:rows + 1] - 15.0)


def kernel(
    moms_hbm, counts_hbm, weights_hbm, vertex_hbm, source_hbm, inverse_hbm, coupling_hbm,
    solved_hbm, sigma_hbm,
    moms, counts, weights, vertex, source, inverse, coupling, left_high, left_low, own_high, own_low, pair_high, pair_low, step_high, step_low,
    driven, lent, wire, entering, greens,
    outbox, inbox, wide, formed, returned, solved, sigma,
    load_sem, store_sem, pair_send, pair_recv, lend_send, lend_recv, pass_send, hop_send, hop_recv, in_send, in_recv, out_send, out_recv,
):
    n_mom, n_tm = lax.axis_size("mom"), lax.axis_size("tm")
    me, turn = lax.axis_index("mom"), lax.axis_index("tm")
    rows, chunks = sigma.shape[2], sigma.shape[0]
    share = rows // n_mom
    slots = moms.shape[1]
    core, plane, planes = lax.rem(turn, 2), turn // 2, n_tm // 2
    partner = turn + 1 - 2 * core
    first, behind = plane == 0, planes - 1 - plane

    def is_handed(chunk):
        return functools.reduce(jnp.logical_or, [(behind == back) & (chunk == which) for back, which in HANDED])


    loads = [
        pltpu.make_async_copy(here, there, load_sem.at[place])
        for place, (here, there) in enumerate((
            (inverse_hbm.at[:, 0, 0], inverse),
            (source_hbm.at[:, 0], source),
            (coupling_hbm.at[:, 0, 0], coupling),
            (moms_hbm, moms),
            (counts_hbm, counts),
            (weights_hbm, weights),
            (vertex_hbm, vertex),
        ))
    ]
    for load in loads:
        load.start()

    barrier = pltpu.get_barrier_semaphore()

    def greet(step, carry):
        other = lax.rem(me + step, n_mom)
        pl.semaphore_signal(barrier, inc=1, device_id={"mom": other, "tm": turn}, device_id_type=MESH)
        return carry

    lax.fori_loop(1, n_mom, greet, 0)

    for other in (partner, lax.rem(turn + 2, n_tm), lax.rem(turn + n_tm - 2, n_tm)):
        pl.semaphore_signal(barrier, inc=1, device_id={"mom": me, "tm": other}, device_id_type=MESH)

    def drive(chunk):
        columns = pl.ds(pl.multiple_of(chunk * LANES, LANES), LANES)
        forcing = jnp.concatenate([source[0, :, columns], source[1, :, columns]], axis=1)
        for half, value in enumerate(pack(*complex_times(left_high[...], left_low[...], forcing))):
            driven[2 * chunk + half] = value

    loads[0].wait()
    for part in range(2):
        high, low = split(inverse[part])
        left_high[part * rows:(part + 1) * rows, :] = high
        left_low[part * rows:(part + 1) * rows, :] = low
    loads[1].wait()
    drive(0)
    loads[2].wait()

    def keep_matrix(high_ref, low_ref, matrix):
        for part in range(2):
            high, low = split(matrix[part])
            high_ref[part * rows:(part + 1) * rows, :] = high
            low_ref[part * rows:(part + 1) * rows, :] = low

    @pl.when((plane > 0) | (core == 1))
    def _():
        keep_matrix(own_high, own_low, complex_times(
            left_high[...], left_low[...], jnp.concatenate([coupling[0], coupling[1]], axis=1)
        ))

    for load in loads[3:]:
        load.wait()

    pl.semaphore_wait(barrier, n_mom + 2)

    def to(other, src, dst, send_sem, recv_sem):
        return pltpu.make_async_remote_copy(
            src_ref=src, dst_ref=dst, send_sem=send_sem, recv_sem=recv_sem,
            device_id={"mom": me, "tm": other}, device_id_type=MESH,
        )

    def lend(piece):
        return to(partner, driven.at[piece], lent.at[piece], lend_send.at[piece], lend_recv.at[piece])

    def hop(piece):
        return to(
            lax.rem(turn + 2, n_tm), wire.at[piece], entering.at[piece], hop_send.at[piece], hop_recv.at[piece]
        )

    def forward(piece):
        return to(partner, entering.at[piece], entering.at[piece], pass_send.at[piece], hop_recv.at[piece])

    pairs = (
        to(partner, own_high, pair_high, pair_send.at[0], pair_recv.at[0]),
        to(partner, own_low, pair_low, pair_send.at[1], pair_recv.at[1]),
    )

    @pl.when(core == 0)
    def _():
        for half in range(2):
            lend(half).start()

        @pl.when(plane > 0)
        def _():
            for pair in pairs:
                pair.start()
            step_high[...] = own_high[...]
            step_low[...] = own_low[...]

        def drive_and_lend(chunk, carry):
            drive(chunk)
            for half in range(2):
                lend(2 * chunk + half).start()
            return carry

        lax.fori_loop(1, chunks, drive_and_lend, 0)

    @pl.when(core == 1)
    def _():
        def drive_rest(chunk, carry):
            drive(chunk)
            return carry

        lax.fori_loop(1, chunks, drive_rest, 0)

    @pl.when((core == 1) & (plane > 0))
    def _():
        for pair in pairs:
            pair.wait_recv()
        both = product(
            own_high[...], own_low[...],
            jnp.concatenate([pair_high[:rows, :], pair_high[rows:, :]], axis=1),
            jnp.concatenate([pair_low[:rows, :], pair_low[rows:, :]], axis=1),
        )
        keep_matrix(step_high, step_low, join(both))

    def compose(chunk):
        for half in range(2):
            lend(2 * chunk + half).wait_recv()
        value = jnp.concatenate([lent[2 * chunk], lent[2 * chunk + 1]], axis=1)
        for half, block in enumerate(packed_times(own_high[...], own_low[...], value)):
            driven[2 * chunk + half] = driven[2 * chunk + half] + block

    def send(src, dst, send_sem, recv_sem, other, there):
        pltpu.make_async_remote_copy(
            src_ref=src, dst_ref=dst, send_sem=send_sem, recv_sem=recv_sem,
            device_id={"mom": other, "tm": there}, device_id_type=MESH,
        ).start()

    def settle(block, sem):
        pltpu.make_async_copy(block, block, sem).wait()

    def others(body):
        def one(step, carry):
            body(lax.rem(me + step, n_mom))
            return carry

        return one

    def store(which, chunk):
        here, there = ((solved, solved_hbm), (sigma, sigma_hbm))[which]
        columns = pl.ds(pl.multiple_of(chunk * LANES, LANES), LANES)
        return pltpu.make_async_copy(here.at[chunk], there.at[:, 0, :, columns], store_sem.at[which, chunk])

    def advance(piece, carry):
        @pl.when(plane == 0)
        def _():
            greens[piece] = driven[piece]

        @pl.when(plane > 0)
        def _():
            hop(piece).wait_recv()

            @pl.when(core == 1)
            def _():
                forward(piece).start()

            [block] = packed_times(step_high[...], step_low[...], decode(entering[piece]))
            greens[piece] = driven[piece] + block

        @pl.when((core == 1) & (plane < planes - 1))
        def _():
            wire[piece] = encode(greens[piece])
            hop(piece).start()

        chunk, half = piece // 2, lax.rem(piece, 2)
        outbox[chunk, :, half] = greens[piece].reshape(n_mom, share, LANES).astype(jnp.bfloat16)
        given = is_handed(chunk)

        @pl.when(jnp.logical_not(given))
        def _():
            inbox[chunk, me, half] = outbox[chunk, me, half]

        def spread(part):
            @pl.when(jnp.logical_not(given))
            def _():
                for step in range(1, n_mom):
                    other = lax.rem(me + step, n_mom)
                    send(
                        outbox.at[(chunk, other, *part)], inbox.at[(chunk, me, *part)],
                        in_send.at[chunk], in_recv.at[chunk], other, turn,
                    )

            @pl.when(given)
            def _():
                slot = chunks + 2 * behind + chunk
                lax.fori_loop(0, n_mom, others(lambda other: send(
                    outbox.at[(chunk, other, *part)], inbox.at[(slot, me, *part)],
                    in_send.at[chunk], in_recv.at[slot], other, core,
                )), 0)

        @pl.when(chunk == 0)
        def _():
            spread((half,))

        @pl.when((chunk > 0) & (half == 1))
        def _():
            spread(())

        return carry

    def keep(chunk):
        for part, value in enumerate(pack(greens[2 * chunk], greens[2 * chunk + 1])):
            solved[chunk, part] = value.astype(jnp.bfloat16)
        store(0, chunk).start()

    def form(chunk, handed):
        if handed:
            settle(inbox.at[chunk], in_recv.at[chunk])
        else:
            settle(inbox.at[chunk, pl.ds(0, n_mom - 1)], in_recv.at[chunk])

        for part, value in enumerate(pack(*(inbox[chunk, :, half].astype(jnp.float32) for half in range(2)))):
            wide[:, part * share:(part + 1) * share] = value

        def one(step, carry):
            mom = lax.rem(me + step, n_mom)
            live = counts[mom]
            total_real = jnp.zeros((share, LANES), jnp.float32)
            total_imag = jnp.zeros((share, LANES), jnp.float32)
            for slot in range(slots):
                first, second, third = (wide[moms[place, slot, mom]] for place in range(3))
                factor = jnp.where(slot < live, vertex[weights[slot, mom]], 0.0)
                ar, ai = first[:share], first[share:]
                br, bi = second[:share], second[share:]
                cr, ci = third[:share], third[share:]
                prod_real = ar * br - ai * bi
                prod_imag = ar * bi + ai * br
                total_real = total_real + factor * (prod_real * cr + prod_imag * ci)
                total_imag = total_imag + factor * (prod_imag * cr - prod_real * ci)
            formed[chunk, mom] = jnp.concatenate([total_real, total_imag], axis=0).astype(jnp.bfloat16)

            if handed:
                send(
                    formed.at[chunk, mom], returned.at[lax.rem(chunk - chunks, 2), me], out_send.at[chunk],
                    out_recv.at[lax.rem(chunk - chunks, 2)], mom, turn + 2 * (planes - 1 - (chunk - chunks) // 2),
                )
            else:
                @pl.when(step < n_mom)
                def _():
                    send(
                        formed.at[chunk, mom], returned.at[chunk, me], out_send.at[chunk], out_recv.at[chunk], mom, turn
                    )

            return carry

        lax.fori_loop(1, n_mom + 1, one, 0)
        if not handed:
            returned[chunk, me] = formed[chunk, me]

    def finish(chunk):
        given = is_handed(chunk)

        @pl.when(given)
        def _():
            settle(returned.at[chunk], out_recv.at[chunk])

        @pl.when(jnp.logical_not(given))
        def _():
            settle(returned.at[chunk, pl.ds(0, n_mom - 1)], out_recv.at[chunk])

        value = returned[chunk].astype(jnp.float32)
        sigma[chunk, 0] = value[:, :share].reshape(rows, LANES)
        sigma[chunk, 1] = value[:, share:].reshape(rows, LANES)
        store(1, chunk).start()

    def solve(chunk, carry):
        @pl.when((core == 1) & (chunk > plane))
        def _():
            compose(chunk)

        lax.fori_loop(2 * chunk, 2 * chunk + 2, advance, 0)
        keep(chunk)
        return carry

    def form_own(chunk, carry):
        @pl.when(jnp.logical_not(is_handed(chunk)))
        def _():
            form(chunk, False)

        return carry

    def finish_own(chunk, carry):
        finish(chunk)
        return carry

    @pl.when(core == 1)
    def _():
        def compose_early(chunk, carry):
            compose(chunk)
            return carry

        lax.fori_loop(0, lax.min(chunks, plane + 1), compose_early, 0)

    lax.fori_loop(0, chunks, solve, 0)
    lax.fori_loop(0, chunks, form_own, 0)

    @pl.when(first)
    def _():
        def form_other(place, carry):
            form(chunks + lax.rem(place + len(HANDED) - 1, len(HANDED)), True)
            return carry

        lax.fori_loop(0, len(HANDED), form_other, 0)

    lax.fori_loop(0, chunks, finish_own, 0)

    def close_piece(piece, carry):
        @pl.when(core == 0)
        def _():
            lend(piece).wait_send()

        @pl.when((core == 1) & (plane > 0))
        def _():
            forward(piece).wait_send()

        @pl.when((core == 1) & (plane < planes - 1))
        def _():
            hop(piece).wait_send()

        return carry

    lax.fori_loop(0, 2 * chunks, close_piece, 0)

    @pl.when((core == 0) & (plane > 0))
    def _():
        for pair in pairs:
            pair.wait_send()

    def close(chunk, carry):
        given = is_handed(chunk)

        @pl.when(jnp.logical_not(given))
        def _():
            settle(outbox.at[chunk, pl.ds(0, n_mom - 1)], in_send.at[chunk])

        @pl.when(given)
        def _():
            settle(outbox.at[chunk], in_send.at[chunk])

        @pl.when(jnp.logical_not(given))
        def _():
            settle(formed.at[chunk, pl.ds(0, n_mom - 1)], out_send.at[chunk])

        store(0, chunk).wait()
        store(1, chunk).wait()
        return carry

    lax.fori_loop(0, chunks, close, 0)

    @pl.when(first)
    def _():
        def close_other(slot, carry):
            settle(formed.at[slot], out_send.at[slot])
            return carry

        lax.fori_loop(chunks, chunks + len(HANDED), close_other, 0)


def write_out(solved, sigma, solved_out, sigma_out, solved_held, sigma_held, in_sem, out_sem):
    blocks = in_sem.shape[2]
    height = solved_held.shape[1] // blocks
    moves = []
    for place, (src, held, dst) in enumerate(((sigma, sigma_held, sigma_out), (solved, solved_held, solved_out))):
        for part in range(2):
            for block in range(blocks):
                span = pl.ds(block * height, height)
                moves.append((
                    pltpu.make_async_copy(src.at[part, 0, span], held.at[part, span], in_sem.at[place, part, block]),
                    pltpu.make_async_copy(held.at[part, span], dst.at[part, 0, span], out_sem.at[place, part, block]),
                ))
    for arrive, _ in moves:
        arrive.start()
    for arrive, leave in moves:
        arrive.wait()
        leave.start()
    for _, leave in moves:
        leave.wait()


def local(source, inverse_diag, coupling, pair_moms, pair_count, pair_weight, vertex):
    rows, columns = source.shape[2], source.shape[3]
    n_mom = lax.axis_size("mom")
    chunks, share = columns // LANES, rows // n_mom
    f32, bf16 = jnp.float32, jnp.bfloat16
    hbm = pl.BlockSpec(memory_space=pltpu.HBM)
    piece = (chunks, n_mom, 2 * share, LANES)
    twice = pltpu.SemaphoreType.DMA((2 * chunks,))
    results = pl.pallas_call(
        kernel,
        out_shape=(
            jax.ShapeDtypeStruct(source.shape, bf16),
            jax.ShapeDtypeStruct(source.shape, f32),
        ),
        in_specs=[hbm] * 7,
        out_specs=(hbm, hbm),
        scratch_shapes=[
            pltpu.SMEM(pair_moms.shape[::-1], jnp.int32),
            pltpu.SMEM(pair_count.shape, jnp.int32),
            pltpu.SMEM(pair_weight.shape[::-1], jnp.int32),
            pltpu.SMEM(vertex.shape, f32),
            pltpu.VMEM((2, rows, columns), f32),
            pltpu.VMEM((2, rows, rows), f32),
            pltpu.VMEM((2, rows, rows), f32),
            *[pltpu.VMEM((2 * rows, rows), bf16) for _ in range(8)],
            pltpu.VMEM((2 * chunks, rows, LANES), f32),
            pltpu.VMEM((2 * chunks, rows, LANES), f32),
            pltpu.VMEM((2 * chunks, rows + EXTRA, LANES), jnp.int16),
            pltpu.VMEM((2 * chunks, rows + EXTRA, LANES), jnp.int16),
            pltpu.VMEM((2 * chunks, rows, LANES), f32),
            pltpu.VMEM((chunks, n_mom, 2, share, LANES), bf16),
            pltpu.VMEM((chunks + len(HANDED), n_mom, 2, share, LANES), bf16),
            pltpu.VMEM(piece[1:], f32),
            pltpu.VMEM((chunks + len(HANDED), *piece[1:]), bf16),
            pltpu.VMEM(piece, bf16),
            pltpu.VMEM((chunks, 2, rows, LANES), bf16),
            pltpu.VMEM((chunks, 2, rows, LANES), f32),
            pltpu.SemaphoreType.DMA((7,)),
            pltpu.SemaphoreType.DMA((2, chunks)),
            pltpu.SemaphoreType.DMA((2,)),
            pltpu.SemaphoreType.DMA((2,)),
            twice, twice, twice, twice, twice,
            *[pltpu.SemaphoreType.DMA((chunks + extra,)) for extra in (0, len(HANDED), len(HANDED), 0)],
        ],
        compiler_params=pltpu.CompilerParams(
            collective_id=0, has_side_effects=True, vmem_limit_bytes=58 << 20
        ),
    )(
        jnp.transpose(pair_moms, (2, 1, 0)), pair_count, jnp.transpose(pair_weight, (1, 0)), vertex,
        source, inverse_diag, coupling,
    )
    blocks = 4
    return pl.pallas_call(
        write_out,
        out_shape=[jax.ShapeDtypeStruct(result.shape, result.dtype) for result in results],
        in_specs=[hbm] * 2,
        out_specs=(hbm, hbm),
        scratch_shapes=[
            pltpu.VMEM((2, rows, columns), bf16),
            pltpu.VMEM((2, rows, columns), f32),
            pltpu.SemaphoreType.DMA((2, 2, blocks)),
            pltpu.SemaphoreType.DMA((2, 2, blocks)),
        ],
    )(*results)


def solution(mesh):
    return jax.shard_map(
        local,
        mesh=mesh,
        in_specs=(
            P(None, "mom", "tm", None),
            P(None, "mom", "tm", None, None),
            P(None, "mom", "tm", None, None),
            P(),
            P(),
            P(),
            P(),
        ),
        out_specs=(P(None, "mom", "tm", None), P(None, "mom", "tm", None)),
        check_vma=False,
    )
```

```python
import jax
import jax.numpy as jnp
from jax import lax
from jax.experimental import pallas as pl
from jax.experimental.pallas import tpu as pltpu
from jax.sharding import PartitionSpec as P

MESH = pl.DeviceIdType.MESH
LANES = 128
EXTRA = 16
HANDED = 2


def split(value):
    high = value.astype(jnp.bfloat16)
    return high, (value - high.astype(jnp.float32)).astype(jnp.bfloat16)


def dot(left, right):
    return jnp.dot(left, right, preferred_element_type=jnp.float32)


def product(high, low, value_high, value_low):
    return dot(high, value_high) + (dot(high, value_low) + dot(low, value_high))


def join(both):
    rows, width = both.shape[0] // 2, both.shape[1] // 2
    real = both[:rows, :width] - both[rows:, width:]
    imag = both[:rows, width:] + both[rows:, :width]
    return real, imag


def complex_times(high, low, value):
    return join(product(high, low, *split(value)))


def pack(real, imag):
    axis = real.ndim - 1
    lower = lax.broadcasted_iota(jnp.int32, real.shape, axis) < LANES // 2
    return (
        jnp.where(lower, real, pltpu.roll(imag, LANES // 2, axis)),
        jnp.where(lower, pltpu.roll(real, LANES // 2, axis), imag),
    )


def packed_times(high, low, value):
    rows = high.shape[1]
    both = product(high, low, *split(value))
    lower = lax.broadcasted_iota(jnp.int32, (rows, LANES), 1) < LANES // 2
    blocks = []
    for at in range(0, value.shape[1], LANES):
        turned = pltpu.roll(both[rows:, at:at + LANES], LANES // 2, 1)
        blocks.append(both[:rows, at:at + LANES] + jnp.where(lower, -turned, turned))
    return blocks


def encode(value):
    peak = jnp.max(jnp.abs(value), axis=0, keepdims=True)
    level = jnp.ceil(jnp.log2(jnp.maximum(peak * 1.0001, 1e-30)))
    levels = jnp.broadcast_to(level, (EXTRA, value.shape[1]))
    code = jnp.concatenate([jnp.round(value * jnp.exp2(15.0 - level)), levels], axis=0)
    return code.astype(jnp.int32).astype(jnp.int16)


def decode(code):
    value = code.astype(jnp.int32).astype(jnp.float32)
    rows = code.shape[0] - EXTRA
    return value[:rows] * jnp.exp2(value[rows:rows + 1] - 15.0)


def kernel(
    moms_hbm, counts_hbm, weights_hbm, vertex_hbm, source_hbm, inverse_hbm, coupling_hbm,
    solved_out, sigma_out,
    moms, counts, weights, vertex, source, inverse, coupling, left_high, left_low, own_high, own_low, pair_high, pair_low, step_high, step_low,
    driven, lent, wire, entering, greens,
    outbox, inbox, wide, formed, returned,
    load_sem, pair_send, pair_recv, lend_send, lend_recv, pass_send, hop_send, hop_recv, in_send, in_recv, out_send, out_recv,
):
    n_mom, n_tm = lax.axis_size("mom"), lax.axis_size("tm")
    me, turn = lax.axis_index("mom"), lax.axis_index("tm")
    rows, chunks = driven.shape[1], driven.shape[0] // 2
    share = rows // n_mom
    slots = moms.shape[1]
    core, plane, planes = lax.rem(turn, 2), turn // 2, n_tm // 2
    partner = turn + 1 - 2 * core
    first, behind = plane == 0, planes - 1 - plane

    def is_handed(chunk):
        return (behind < HANDED) & (chunk == 0)


    loads = [
        pltpu.make_async_copy(here, there, load_sem.at[place])
        for place, (here, there) in enumerate((
            (inverse_hbm.at[:, 0, 0], inverse),
            (source_hbm.at[:, 0], source),
            (coupling_hbm.at[:, 0, 0], coupling),
            (moms_hbm, moms),
            (counts_hbm, counts),
            (weights_hbm, weights),
            (vertex_hbm, vertex),
        ))
    ]
    for load in loads:
        load.start()

    barrier = pltpu.get_barrier_semaphore()

    def greet(step, carry):
        other = lax.rem(me + step, n_mom)
        pl.semaphore_signal(barrier, inc=1, device_id={"mom": other, "tm": turn}, device_id_type=MESH)
        return carry

    lax.fori_loop(1, n_mom, greet, 0)

    for other in (partner, lax.rem(turn + 2, n_tm), lax.rem(turn + n_tm - 2, n_tm)):
        pl.semaphore_signal(barrier, inc=1, device_id={"mom": me, "tm": other}, device_id_type=MESH)

    def drive(chunk):
        columns = pl.ds(pl.multiple_of(chunk * LANES, LANES), LANES)
        forcing = jnp.concatenate([source[0, :, columns], source[1, :, columns]], axis=1)
        for half, value in enumerate(pack(*complex_times(left_high[...], left_low[...], forcing))):
            driven[2 * chunk + half] = value

    loads[0].wait()
    for part in range(2):
        high, low = split(inverse[part])
        left_high[part * rows:(part + 1) * rows, :] = high
        left_low[part * rows:(part + 1) * rows, :] = low
    loads[1].wait()
    drive(0)
    loads[2].wait()

    def keep_matrix(high_ref, low_ref, matrix):
        for part in range(2):
            high, low = split(matrix[part])
            high_ref[part * rows:(part + 1) * rows, :] = high
            low_ref[part * rows:(part + 1) * rows, :] = low

    @pl.when((plane > 0) | (core == 1))
    def _():
        keep_matrix(own_high, own_low, complex_times(
            left_high[...], left_low[...], jnp.concatenate([coupling[0], coupling[1]], axis=1)
        ))

    for load in loads[3:]:
        load.wait()

    pl.semaphore_wait(barrier, n_mom + 2)

    def to(other, src, dst, send_sem, recv_sem):
        return pltpu.make_async_remote_copy(
            src_ref=src, dst_ref=dst, send_sem=send_sem, recv_sem=recv_sem,
            device_id={"mom": me, "tm": other}, device_id_type=MESH,
        )

    def lend(piece):
        return to(partner, driven.at[piece], lent.at[piece], lend_send.at[piece], lend_recv.at[piece])

    def hop(piece):
        return to(
            lax.rem(turn + 2, n_tm), wire.at[piece], entering.at[piece], hop_send.at[piece], hop_recv.at[piece]
        )

    def forward(piece):
        return to(partner, entering.at[piece], entering.at[piece], pass_send.at[piece], hop_recv.at[piece])

    pairs = (
        to(partner, own_high, pair_high, pair_send.at[0], pair_recv.at[0]),
        to(partner, own_low, pair_low, pair_send.at[1], pair_recv.at[1]),
    )

    @pl.when(core == 0)
    def _():
        for half in range(2):
            lend(half).start()

        @pl.when(plane > 0)
        def _():
            for pair in pairs:
                pair.start()
            step_high[...] = own_high[...]
            step_low[...] = own_low[...]

        def drive_and_lend(chunk, carry):
            drive(chunk)
            for half in range(2):
                lend(2 * chunk + half).start()
            return carry

        lax.fori_loop(1, chunks, drive_and_lend, 0)

    @pl.when(core == 1)
    def _():
        def drive_rest(chunk, carry):
            drive(chunk)
            return carry

        lax.fori_loop(1, chunks, drive_rest, 0)

    @pl.when((core == 1) & (plane > 0))
    def _():
        for pair in pairs:
            pair.wait_recv()
        both = product(
            own_high[...], own_low[...],
            jnp.concatenate([pair_high[:rows, :], pair_high[rows:, :]], axis=1),
            jnp.concatenate([pair_low[:rows, :], pair_low[rows:, :]], axis=1),
        )
        keep_matrix(step_high, step_low, join(both))

    def compose(chunk):
        for half in range(2):
            lend(2 * chunk + half).wait_recv()
        value = jnp.concatenate([lent[2 * chunk], lent[2 * chunk + 1]], axis=1)
        for half, block in enumerate(packed_times(own_high[...], own_low[...], value)):
            driven[2 * chunk + half] = driven[2 * chunk + half] + block

    def send(src, dst, send_sem, recv_sem, other, there):
        pltpu.make_async_remote_copy(
            src_ref=src, dst_ref=dst, send_sem=send_sem, recv_sem=recv_sem,
            device_id={"mom": other, "tm": there}, device_id_type=MESH,
        ).start()

    def settle(block, sem):
        pltpu.make_async_copy(block, block, sem).wait()

    def others(body):
        def one(step, carry):
            body(lax.rem(me + step, n_mom))
            return carry

        return one

    def span(chunk):
        return pl.ds(pl.multiple_of(chunk * LANES, LANES), LANES)

    def advance(piece, carry):
        @pl.when(plane == 0)
        def _():
            greens[piece] = driven[piece]

        @pl.when(plane > 0)
        def _():
            hop(piece).wait_recv()

            @pl.when(core == 1)
            def _():
                forward(piece).start()

            [block] = packed_times(step_high[...], step_low[...], decode(entering[piece]))
            greens[piece] = driven[piece] + block

        @pl.when((core == 1) & (plane < planes - 1))
        def _():
            wire[piece] = encode(greens[piece])
            hop(piece).start()

        chunk, half = piece // 2, lax.rem(piece, 2)
        outbox[chunk, :, half] = greens[piece].reshape(n_mom, share, LANES).astype(jnp.bfloat16)
        given = is_handed(chunk)

        @pl.when(jnp.logical_not(given))
        def _():
            inbox[chunk, me, half] = outbox[chunk, me, half]

        def spread(part):
            @pl.when(jnp.logical_not(given))
            def _():
                for step in range(1, n_mom):
                    other = lax.rem(me + step, n_mom)
                    send(
                        outbox.at[(chunk, other, *part)], inbox.at[(chunk, me, *part)],
                        in_send.at[chunk], in_recv.at[chunk], other, turn,
                    )

            @pl.when(given)
            def _():
                slot = chunks + behind
                lax.fori_loop(0, n_mom, others(lambda other: send(
                    outbox.at[(chunk, other, *part)], inbox.at[(slot, me, *part)],
                    in_send.at[chunk], in_recv.at[slot], other, core,
                )), 0)

        @pl.when(chunk == 0)
        def _():
            spread((half,))

        @pl.when((chunk > 0) & (half == 1))
        def _():
            spread(())

        return carry

    def keep(chunk):
        for part, value in enumerate(pack(greens[2 * chunk], greens[2 * chunk + 1])):
            solved_out[part, :, span(chunk)] = value.astype(jnp.bfloat16)

    def form(chunk, handed):
        if handed:
            settle(inbox.at[chunk], in_recv.at[chunk])
        else:
            settle(inbox.at[chunk, pl.ds(0, n_mom - 1)], in_recv.at[chunk])

        for part, value in enumerate(pack(*(inbox[chunk, :, half].astype(jnp.float32) for half in range(2)))):
            wide[:, part * share:(part + 1) * share] = value

        def one(step, carry):
            mom = lax.rem(me + step, n_mom)
            live = counts[mom]
            total_real = jnp.zeros((share, LANES), jnp.float32)
            total_imag = jnp.zeros((share, LANES), jnp.float32)
            for slot in range(slots):
                first, second, third = (wide[moms[place, slot, mom]] for place in range(3))
                factor = jnp.where(slot < live, vertex[weights[slot, mom]], 0.0)
                ar, ai = first[:share], first[share:]
                br, bi = second[:share], second[share:]
                cr, ci = third[:share], third[share:]
                prod_real = ar * br - ai * bi
                prod_imag = ar * bi + ai * br
                total_real = total_real + factor * (prod_real * cr + prod_imag * ci)
                total_imag = total_imag + factor * (prod_imag * cr - prod_real * ci)
            formed[chunk, mom] = jnp.concatenate([total_real, total_imag], axis=0).astype(jnp.bfloat16)

            if handed:
                send(
                    formed.at[chunk, mom], returned.at[0, me], out_send.at[chunk],
                    out_recv.at[0], mom, turn + 2 * (planes - 1 - (chunk - chunks)),
                )
            else:
                @pl.when(step < n_mom)
                def _():
                    send(
                        formed.at[chunk, mom], returned.at[chunk, me], out_send.at[chunk], out_recv.at[chunk], mom, turn
                    )

            return carry

        lax.fori_loop(1, n_mom + 1, one, 0)
        if not handed:
            returned[chunk, me] = formed[chunk, me]

    def finish(chunk):
        given = is_handed(chunk)

        @pl.when(given)
        def _():
            settle(returned.at[chunk], out_recv.at[chunk])

        @pl.when(jnp.logical_not(given))
        def _():
            settle(returned.at[chunk, pl.ds(0, n_mom - 1)], out_recv.at[chunk])

        value = returned[chunk].astype(jnp.float32)
        sigma_out[0, :, span(chunk)] = value[:, :share].reshape(rows, LANES)
        sigma_out[1, :, span(chunk)] = value[:, share:].reshape(rows, LANES)

    def solve(chunk, carry):
        @pl.when((core == 1) & (chunk > plane))
        def _():
            compose(chunk)

        lax.fori_loop(2 * chunk, 2 * chunk + 2, advance, 0)
        keep(chunk)
        return carry

    def form_own(chunk, carry):
        @pl.when(jnp.logical_not(is_handed(chunk)))
        def _():
            form(chunk, False)

        return carry

    def finish_own(chunk, carry):
        finish(lax.rem(chunk + plane // (planes - HANDED), chunks))
        return carry

    @pl.when(core == 1)
    def _():
        def compose_early(chunk, carry):
            compose(chunk)
            return carry

        lax.fori_loop(0, lax.min(chunks, plane + 1), compose_early, 0)

    lax.fori_loop(0, chunks, solve, 0)
    lax.fori_loop(0, chunks, form_own, 0)

    @pl.when(first)
    def _():
        def form_other(place, carry):
            form(chunks + HANDED - 1 - place, True)
            return carry

        lax.fori_loop(0, HANDED, form_other, 0)

    lax.fori_loop(0, chunks, finish_own, 0)

    def close_piece(piece, carry):
        @pl.when(core == 0)
        def _():
            lend(piece).wait_send()

        @pl.when((core == 1) & (plane > 0))
        def _():
            forward(piece).wait_send()

        @pl.when((core == 1) & (plane < planes - 1))
        def _():
            hop(piece).wait_send()

        return carry

    lax.fori_loop(0, 2 * chunks, close_piece, 0)

    @pl.when((core == 0) & (plane > 0))
    def _():
        for pair in pairs:
            pair.wait_send()

    def close(chunk, carry):
        given = is_handed(chunk)

        @pl.when(jnp.logical_not(given))
        def _():
            settle(outbox.at[chunk, pl.ds(0, n_mom - 1)], in_send.at[chunk])

        @pl.when(given)
        def _():
            settle(outbox.at[chunk], in_send.at[chunk])

        @pl.when(jnp.logical_not(given))
        def _():
            settle(formed.at[chunk, pl.ds(0, n_mom - 1)], out_send.at[chunk])
        return carry

    lax.fori_loop(0, chunks, close, 0)

    @pl.when(first)
    def _():
        def close_other(slot, carry):
            settle(formed.at[slot], out_send.at[slot])
            return carry

        lax.fori_loop(chunks, chunks + HANDED, close_other, 0)


def write_out(solved, sigma, solved_out, sigma_out, sem):
    blocks = sem.shape[2]
    height = solved.shape[1] // blocks
    copies = []
    for place, (src, dst) in enumerate(((sigma, sigma_out), (solved, solved_out))):
        for part in range(2):
            for block in range(blocks):
                span = pl.ds(block * height, height)
                copies.append(pltpu.make_async_copy(src.at[part, span], dst.at[part, 0, span], sem.at[place, part, block]))
    for copy in copies:
        copy.start()
    for copy in copies:
        copy.wait()


def local(source, inverse_diag, coupling, pair_moms, pair_count, pair_weight, vertex):
    rows, columns = source.shape[2], source.shape[3]
    n_mom = lax.axis_size("mom")
    chunks, share = columns // LANES, rows // n_mom
    f32, bf16 = jnp.float32, jnp.bfloat16
    hbm, vmem = pl.BlockSpec(memory_space=pltpu.HBM), pl.BlockSpec(memory_space=pltpu.VMEM)
    piece = (chunks, n_mom, 2 * share, LANES)
    twice = pltpu.SemaphoreType.DMA((2 * chunks,))
    results = pl.pallas_call(
        kernel,
        out_shape=(
            pltpu.VMEM((2, rows, columns), bf16),
            pltpu.VMEM((2, rows, columns), f32),
        ),
        in_specs=[hbm] * 7,
        out_specs=(vmem, vmem),
        scratch_shapes=[
            pltpu.SMEM(pair_moms.shape[::-1], jnp.int32),
            pltpu.SMEM(pair_count.shape, jnp.int32),
            pltpu.SMEM(pair_weight.shape[::-1], jnp.int32),
            pltpu.SMEM(vertex.shape, f32),
            pltpu.VMEM((2, rows, columns), f32),
            pltpu.VMEM((2, rows, rows), f32),
            pltpu.VMEM((2, rows, rows), f32),
            *[pltpu.VMEM((2 * rows, rows), bf16) for _ in range(8)],
            pltpu.VMEM((2 * chunks, rows, LANES), f32),
            pltpu.VMEM((2 * chunks, rows, LANES), f32),
            pltpu.VMEM((2 * chunks, rows + EXTRA, LANES), jnp.int16),
            pltpu.VMEM((2 * chunks, rows + EXTRA, LANES), jnp.int16),
            pltpu.VMEM((2 * chunks, rows, LANES), f32),
            pltpu.VMEM((chunks, n_mom, 2, share, LANES), bf16),
            pltpu.VMEM((chunks + HANDED, n_mom, 2, share, LANES), bf16),
            pltpu.VMEM(piece[1:], f32),
            pltpu.VMEM((chunks + HANDED, *piece[1:]), bf16),
            pltpu.VMEM(piece, bf16),
            pltpu.SemaphoreType.DMA((7,)),
            pltpu.SemaphoreType.DMA((2,)),
            pltpu.SemaphoreType.DMA((2,)),
            twice, twice, twice, twice, twice,
            *[pltpu.SemaphoreType.DMA((chunks + extra,)) for extra in (0, HANDED, HANDED, 0)],
        ],
        compiler_params=pltpu.CompilerParams(
            collective_id=0, has_side_effects=True, vmem_limit_bytes=58 << 20
        ),
    )(
        jnp.transpose(pair_moms, (2, 1, 0)), pair_count, jnp.transpose(pair_weight, (1, 0)), vertex,
        source, inverse_diag, coupling,
    )
    return pl.pallas_call(
        write_out,
        out_shape=[jax.ShapeDtypeStruct(source.shape, dtype) for dtype in (bf16, f32)],
        in_specs=[vmem] * 2,
        out_specs=[hbm] * 2,
        scratch_shapes=[pltpu.SemaphoreType.DMA((2, 2, 4))],
        compiler_params=pltpu.CompilerParams(vmem_limit_bytes=32 << 20),
    )(*results)


def solution(mesh):
    return jax.shard_map(
        local,
        mesh=mesh,
        in_specs=(
            P(None, "mom", "tm", None),
            P(None, "mom", "tm", None, None),
            P(None, "mom", "tm", None, None),
            P(),
            P(),
            P(),
            P(),
        ),
        out_specs=(P(None, "mom", "tm", None), P(None, "mom", "tm", None)),
        check_vma=False,
    )
```

```python
import jax
import jax.numpy as jnp
from jax import lax
from jax.experimental import pallas as pl
from jax.experimental.pallas import tpu as pltpu
from jax.sharding import PartitionSpec as P

MESH = pl.DeviceIdType.MESH
LANES = 128
EXTRA = 16
HANDED = 3


def split(value):
    high = value.astype(jnp.bfloat16)
    return high, (value - high.astype(jnp.float32)).astype(jnp.bfloat16)


def dot(left, right):
    return jnp.dot(left, right, preferred_element_type=jnp.float32)


def product(high, low, value_high, value_low):
    return dot(high, value_high) + (dot(high, value_low) + dot(low, value_high))


def join(both):
    rows, width = both.shape[0] // 2, both.shape[1] // 2
    real = both[:rows, :width] - both[rows:, width:]
    imag = both[:rows, width:] + both[rows:, :width]
    return real, imag


def complex_times(high, low, value):
    return join(product(high, low, *split(value)))


def pack(real, imag):
    axis = real.ndim - 1
    lower = lax.broadcasted_iota(jnp.int32, real.shape, axis) < LANES // 2
    return (
        jnp.where(lower, real, pltpu.roll(imag, LANES // 2, axis)),
        jnp.where(lower, pltpu.roll(real, LANES // 2, axis), imag),
    )


def packed_times(high, low, value):
    rows = high.shape[1]
    both = product(high, low, *split(value))
    lower = lax.broadcasted_iota(jnp.int32, (rows, LANES), 1) < LANES // 2
    blocks = []
    for at in range(0, value.shape[1], LANES):
        turned = pltpu.roll(both[rows:, at:at + LANES], LANES // 2, 1)
        blocks.append(both[:rows, at:at + LANES] + jnp.where(lower, -turned, turned))
    return blocks


def encode(value):
    peak = jnp.max(jnp.abs(value), axis=0, keepdims=True)
    level = jnp.ceil(jnp.log2(jnp.maximum(peak * 1.0001, 1e-30)))
    levels = jnp.broadcast_to(level, (EXTRA, value.shape[1]))
    code = jnp.concatenate([jnp.round(value * jnp.exp2(15.0 - level)), levels], axis=0)
    return code.astype(jnp.int32).astype(jnp.int16)


def decode(code):
    value = code.astype(jnp.int32).astype(jnp.float32)
    rows = code.shape[0] - EXTRA
    return value[:rows] * jnp.exp2(value[rows:rows + 1] - 15.0)


def kernel(
    moms_hbm, counts_hbm, weights_hbm, vertex_hbm, source_hbm, inverse_hbm, coupling_hbm,
    solved_out, sigma_out,
    moms, counts, weights, vertex, source, inverse, coupling, left_high, left_low, own_high, own_low, pair_high, pair_low, step_high, step_low,
    driven, lent, wire, entering, greens,
    outbox, inbox, wide, formed, returned,
    load_sem, pair_send, pair_recv, lend_send, lend_recv, pass_send, hop_send, hop_recv, in_send, in_recv, out_send, out_recv,
):
    n_mom, n_tm = lax.axis_size("mom"), lax.axis_size("tm")
    me, turn = lax.axis_index("mom"), lax.axis_index("tm")
    rows, chunks = driven.shape[1], driven.shape[0] // 2
    share = rows // n_mom
    slots = moms.shape[1]
    core, plane, planes = lax.rem(turn, 2), turn // 2, n_tm // 2
    partner = turn + 1 - 2 * core
    first, behind = plane == 0, planes - 1 - plane

    def is_handed(chunk):
        from_last = (behind == 0) & ((chunk == 0) | ((chunk == 1) & (core == 0)))
        return from_last | ((behind == 1) & (chunk == chunks // 2))

    def handed_from(slot):
        return lax.rem(slot, 2), slot // 2 + lax.rem(slot, 2) * (chunks // 2)

    def slot_of(chunk):
        return chunks + behind + 2 * chunk * (1 - behind)


    loads = [
        pltpu.make_async_copy(here, there, load_sem.at[place])
        for place, (here, there) in enumerate((
            (inverse_hbm.at[:, 0, 0], inverse),
            (source_hbm.at[:, 0], source),
            (coupling_hbm.at[:, 0, 0], coupling),
            (moms_hbm, moms),
            (counts_hbm, counts),
            (weights_hbm, weights),
            (vertex_hbm, vertex),
        ))
    ]
    for load in loads:
        load.start()

    barrier = pltpu.get_barrier_semaphore()

    def greet(step, carry):
        other = lax.rem(me + step, n_mom)
        pl.semaphore_signal(barrier, inc=1, device_id={"mom": other, "tm": turn}, device_id_type=MESH)
        return carry

    lax.fori_loop(1, n_mom, greet, 0)

    for other in (partner, lax.rem(turn + 2, n_tm), lax.rem(turn + n_tm - 2, n_tm)):
        pl.semaphore_signal(barrier, inc=1, device_id={"mom": me, "tm": other}, device_id_type=MESH)

    def drive(chunk):
        columns = pl.ds(pl.multiple_of(chunk * LANES, LANES), LANES)
        forcing = jnp.concatenate([source[0, :, columns], source[1, :, columns]], axis=1)
        for half, value in enumerate(pack(*complex_times(left_high[...], left_low[...], forcing))):
            driven[2 * chunk + half] = value

    loads[0].wait()
    for part in range(2):
        high, low = split(inverse[part])
        left_high[part * rows:(part + 1) * rows, :] = high
        left_low[part * rows:(part + 1) * rows, :] = low
    loads[1].wait()
    drive(0)
    loads[2].wait()

    def keep_matrix(high_ref, low_ref, matrix):
        for part in range(2):
            high, low = split(matrix[part])
            high_ref[part * rows:(part + 1) * rows, :] = high
            low_ref[part * rows:(part + 1) * rows, :] = low

    @pl.when((plane > 0) | (core == 1))
    def _():
        keep_matrix(own_high, own_low, complex_times(
            left_high[...], left_low[...], jnp.concatenate([coupling[0], coupling[1]], axis=1)
        ))

    for load in loads[3:]:
        load.wait()

    pl.semaphore_wait(barrier, n_mom + 2)

    def to(other, src, dst, send_sem, recv_sem):
        return pltpu.make_async_remote_copy(
            src_ref=src, dst_ref=dst, send_sem=send_sem, recv_sem=recv_sem,
            device_id={"mom": me, "tm": other}, device_id_type=MESH,
        )

    def lend(piece):
        return to(partner, driven.at[piece], lent.at[piece], lend_send.at[piece], lend_recv.at[piece])

    def hop(piece):
        return to(
            lax.rem(turn + 2, n_tm), wire.at[piece], entering.at[piece], hop_send.at[piece], hop_recv.at[piece]
        )

    def forward(piece):
        return to(partner, entering.at[piece], entering.at[piece], pass_send.at[piece], hop_recv.at[piece])

    pairs = (
        to(partner, own_high, pair_high, pair_send.at[0], pair_recv.at[0]),
        to(partner, own_low, pair_low, pair_send.at[1], pair_recv.at[1]),
    )

    @pl.when(core == 0)
    def _():
        for half in range(2):
            lend(half).start()

        @pl.when(plane > 0)
        def _():
            for pair in pairs:
                pair.start()
            step_high[...] = own_high[...]
            step_low[...] = own_low[...]

        def drive_and_lend(chunk, carry):
            drive(chunk)
            for half in range(2):
                lend(2 * chunk + half).start()
            return carry

        lax.fori_loop(1, chunks, drive_and_lend, 0)

    @pl.when(core == 1)
    def _():
        def drive_rest(chunk, carry):
            drive(chunk)
            return carry

        lax.fori_loop(1, chunks, drive_rest, 0)

    @pl.when((core == 1) & (plane > 0))
    def _():
        for pair in pairs:
            pair.wait_recv()
        both = product(
            own_high[...], own_low[...],
            jnp.concatenate([pair_high[:rows, :], pair_high[rows:, :]], axis=1),
            jnp.concatenate([pair_low[:rows, :], pair_low[rows:, :]], axis=1),
        )
        keep_matrix(step_high, step_low, join(both))

    def compose(chunk):
        for half in range(2):
            lend(2 * chunk + half).wait_recv()
        value = jnp.concatenate([lent[2 * chunk], lent[2 * chunk + 1]], axis=1)
        for half, block in enumerate(packed_times(own_high[...], own_low[...], value)):
            driven[2 * chunk + half] = driven[2 * chunk + half] + block

    def send(src, dst, send_sem, recv_sem, other, there):
        pltpu.make_async_remote_copy(
            src_ref=src, dst_ref=dst, send_sem=send_sem, recv_sem=recv_sem,
            device_id={"mom": other, "tm": there}, device_id_type=MESH,
        ).start()

    def settle(block, sem):
        pltpu.make_async_copy(block, block, sem).wait()

    def others(body):
        def one(step, carry):
            body(lax.rem(me + step, n_mom))
            return carry

        return one

    def span(chunk):
        return pl.ds(pl.multiple_of(chunk * LANES, LANES), LANES)

    def advance(piece, carry):
        @pl.when(plane == 0)
        def _():
            greens[piece] = driven[piece]

        @pl.when(plane > 0)
        def _():
            hop(piece).wait_recv()

            @pl.when(core == 1)
            def _():
                forward(piece).start()

            [block] = packed_times(step_high[...], step_low[...], decode(entering[piece]))
            greens[piece] = driven[piece] + block

        @pl.when((core == 1) & (plane < planes - 1))
        def _():
            wire[piece] = encode(greens[piece])
            hop(piece).start()

        chunk, half = piece // 2, lax.rem(piece, 2)
        outbox[chunk, :, half] = greens[piece].reshape(n_mom, share, LANES).astype(jnp.bfloat16)
        given = is_handed(chunk)

        @pl.when(jnp.logical_not(given))
        def _():
            inbox[chunk, me, half] = outbox[chunk, me, half]

        def spread(part):
            @pl.when(jnp.logical_not(given))
            def _():
                for step in range(1, n_mom):
                    other = lax.rem(me + step, n_mom)
                    send(
                        outbox.at[(chunk, other, *part)], inbox.at[(chunk, me, *part)],
                        in_send.at[chunk], in_recv.at[chunk], other, turn,
                    )

            @pl.when(given)
            def _():
                slot = slot_of(chunk)
                lax.fori_loop(0, n_mom, others(lambda other: send(
                    outbox.at[(chunk, other, *part)], inbox.at[(slot, me, *part)],
                    in_send.at[chunk], in_recv.at[slot], other, core,
                )), 0)

        @pl.when(chunk == 0)
        def _():
            spread((half,))

        @pl.when((chunk > 0) & (half == 1))
        def _():
            spread(())

        return carry

    def keep(chunk):
        for part, value in enumerate(pack(greens[2 * chunk], greens[2 * chunk + 1])):
            solved_out[part, :, span(chunk)] = value.astype(jnp.bfloat16)

    def form(chunk, handed):
        if handed:
            settle(inbox.at[chunk], in_recv.at[chunk])
        else:
            settle(inbox.at[chunk, pl.ds(0, n_mom - 1)], in_recv.at[chunk])

        for part, value in enumerate(pack(*(inbox[chunk, :, half].astype(jnp.float32) for half in range(2)))):
            wide[:, part * share:(part + 1) * share] = value

        def one(step, carry):
            mom = lax.rem(me + step, n_mom)
            live = counts[mom]
            total_real = jnp.zeros((share, LANES), jnp.float32)
            total_imag = jnp.zeros((share, LANES), jnp.float32)
            for slot in range(slots):
                first, second, third = (wide[moms[place, slot, mom]] for place in range(3))
                factor = jnp.where(slot < live, vertex[weights[slot, mom]], 0.0)
                ar, ai = first[:share], first[share:]
                br, bi = second[:share], second[share:]
                cr, ci = third[:share], third[share:]
                prod_real = ar * br - ai * bi
                prod_imag = ar * bi + ai * br
                total_real = total_real + factor * (prod_real * cr + prod_imag * ci)
                total_imag = total_imag + factor * (prod_imag * cr - prod_real * ci)
            formed[chunk, mom] = jnp.concatenate([total_real, total_imag], axis=0).astype(jnp.bfloat16)

            if handed:
                back, which = handed_from(chunk - chunks)
                send(
                    formed.at[chunk, mom], returned.at[which, me], out_send.at[chunk],
                    out_recv.at[which], mom, turn + 2 * (planes - 1 - back),
                )
            else:
                @pl.when(step < n_mom)
                def _():
                    send(
                        formed.at[chunk, mom], returned.at[chunk, me], out_send.at[chunk], out_recv.at[chunk], mom, turn
                    )

            return carry

        lax.fori_loop(1, n_mom + 1, one, 0)
        if not handed:
            returned[chunk, me] = formed[chunk, me]

    def finish(chunk):
        given = is_handed(chunk)

        @pl.when(given)
        def _():
            settle(returned.at[chunk], out_recv.at[chunk])

        @pl.when(jnp.logical_not(given))
        def _():
            settle(returned.at[chunk, pl.ds(0, n_mom - 1)], out_recv.at[chunk])

        value = returned[chunk].astype(jnp.float32)
        sigma_out[0, :, span(chunk)] = value[:, :share].reshape(rows, LANES)
        sigma_out[1, :, span(chunk)] = value[:, share:].reshape(rows, LANES)

    def solve(chunk, carry):
        @pl.when((core == 1) & (chunk > plane))
        def _():
            compose(chunk)

        lax.fori_loop(2 * chunk, 2 * chunk + 2, advance, 0)
        keep(chunk)
        return carry

    def form_own(chunk, carry):
        @pl.when(jnp.logical_not(is_handed(chunk)))
        def _():
            form(chunk, False)

        return carry

    def finish_own(chunk, carry):
        finish(lax.rem(chunk + (2 * plane // planes) * (2 + behind), chunks))
        return carry

    @pl.when(core == 1)
    def _():
        def compose_early(chunk, carry):
            compose(chunk)
            return carry

        lax.fori_loop(0, lax.min(chunks, plane + 1), compose_early, 0)

    lax.fori_loop(0, chunks, solve, 0)
    lax.fori_loop(0, chunks, form_own, 0)

    @pl.when(first)
    def _():
        def form_other(place, carry):
            form(chunks + place, True)
            return carry

        lax.fori_loop(0, HANDED - core, form_other, 0)

    lax.fori_loop(0, chunks, finish_own, 0)

    def close_piece(piece, carry):
        @pl.when(core == 0)
        def _():
            lend(piece).wait_send()

        @pl.when((core == 1) & (plane > 0))
        def _():
            forward(piece).wait_send()

        @pl.when((core == 1) & (plane < planes - 1))
        def _():
            hop(piece).wait_send()

        return carry

    lax.fori_loop(0, 2 * chunks, close_piece, 0)

    @pl.when((core == 0) & (plane > 0))
    def _():
        for pair in pairs:
            pair.wait_send()

    def close(chunk, carry):
        given = is_handed(chunk)

        @pl.when(jnp.logical_not(given))
        def _():
            settle(outbox.at[chunk, pl.ds(0, n_mom - 1)], in_send.at[chunk])

        @pl.when(given)
        def _():
            settle(outbox.at[chunk], in_send.at[chunk])

        @pl.when(jnp.logical_not(given))
        def _():
            settle(formed.at[chunk, pl.ds(0, n_mom - 1)], out_send.at[chunk])
        return carry

    lax.fori_loop(0, chunks, close, 0)

    @pl.when(first)
    def _():
        def close_other(slot, carry):
            settle(formed.at[slot], out_send.at[slot])
            return carry

        lax.fori_loop(chunks, chunks + HANDED - core, close_other, 0)


def write_out(solved, sigma, solved_out, sigma_out, sem):
    blocks = sem.shape[2]
    height = solved.shape[1] // blocks
    copies = []
    for place, (src, dst) in enumerate(((sigma, sigma_out), (solved, solved_out))):
        for part in range(2):
            for block in range(blocks):
                span = pl.ds(block * height, height)
                copies.append(pltpu.make_async_copy(src.at[part, span], dst.at[part, 0, span], sem.at[place, part, block]))
    for copy in copies:
        copy.start()
    for copy in copies:
        copy.wait()


def local(source, inverse_diag, coupling, pair_moms, pair_count, pair_weight, vertex):
    rows, columns = source.shape[2], source.shape[3]
    n_mom = lax.axis_size("mom")
    chunks, share = columns // LANES, rows // n_mom
    f32, bf16 = jnp.float32, jnp.bfloat16
    hbm, vmem = pl.BlockSpec(memory_space=pltpu.HBM), pl.BlockSpec(memory_space=pltpu.VMEM)
    piece = (chunks, n_mom, 2 * share, LANES)
    twice = pltpu.SemaphoreType.DMA((2 * chunks,))
    results = pl.pallas_call(
        kernel,
        out_shape=(
            pltpu.VMEM((2, rows, columns), bf16),
            pltpu.VMEM((2, rows, columns), f32),
        ),
        in_specs=[hbm] * 7,
        out_specs=(vmem, vmem),
        scratch_shapes=[
            pltpu.SMEM(pair_moms.shape[::-1], jnp.int32),
            pltpu.SMEM(pair_count.shape, jnp.int32),
            pltpu.SMEM(pair_weight.shape[::-1], jnp.int32),
            pltpu.SMEM(vertex.shape, f32),
            pltpu.VMEM((2, rows, columns), f32),
            pltpu.VMEM((2, rows, rows), f32),
            pltpu.VMEM((2, rows, rows), f32),
            *[pltpu.VMEM((2 * rows, rows), bf16) for _ in range(8)],
            pltpu.VMEM((2 * chunks, rows, LANES), f32),
            pltpu.VMEM((2 * chunks, rows, LANES), f32),
            pltpu.VMEM((2 * chunks, rows + EXTRA, LANES), jnp.int16),
            pltpu.VMEM((2 * chunks, rows + EXTRA, LANES), jnp.int16),
            pltpu.VMEM((2 * chunks, rows, LANES), f32),
            pltpu.VMEM((chunks, n_mom, 2, share, LANES), bf16),
            pltpu.VMEM((chunks + HANDED, n_mom, 2, share, LANES), bf16),
            pltpu.VMEM(piece[1:], f32),
            pltpu.VMEM((chunks + HANDED, *piece[1:]), bf16),
            pltpu.VMEM(piece, bf16),
            pltpu.SemaphoreType.DMA((7,)),
            pltpu.SemaphoreType.DMA((2,)),
            pltpu.SemaphoreType.DMA((2,)),
            twice, twice, twice, twice, twice,
            *[pltpu.SemaphoreType.DMA((chunks + extra,)) for extra in (0, HANDED, HANDED, 0)],
        ],
        compiler_params=pltpu.CompilerParams(
            collective_id=0, has_side_effects=True, vmem_limit_bytes=58 << 20
        ),
    )(
        jnp.transpose(pair_moms, (2, 1, 0)), pair_count, jnp.transpose(pair_weight, (1, 0)), vertex,
        source, inverse_diag, coupling,
    )
    return pl.pallas_call(
        write_out,
        out_shape=[jax.ShapeDtypeStruct(source.shape, dtype) for dtype in (bf16, f32)],
        in_specs=[vmem] * 2,
        out_specs=[hbm] * 2,
        scratch_shapes=[pltpu.SemaphoreType.DMA((2, 2, 4))],
        compiler_params=pltpu.CompilerParams(vmem_limit_bytes=32 << 20),
    )(*results)


def solution(mesh):
    return jax.shard_map(
        local,
        mesh=mesh,
        in_specs=(
            P(None, "mom", "tm", None),
            P(None, "mom", "tm", None, None),
            P(None, "mom", "tm", None, None),
            P(),
            P(),
            P(),
            P(),
        ),
        out_specs=(P(None, "mom", "tm", None), P(None, "mom", "tm", None)),
        check_vma=False,
    )
```

```python
import jax
import jax.numpy as jnp
from jax import lax
from jax.experimental import pallas as pl
from jax.experimental.pallas import tpu as pltpu
from jax.sharding import PartitionSpec as P

MESH = pl.DeviceIdType.MESH
LANES = 128
EXTRA = 16
EARLY = 2
HANDED = 3


def split(value):
    high = value.astype(jnp.bfloat16)
    return high, (value - high.astype(jnp.float32)).astype(jnp.bfloat16)


def dot(left, right):
    return jnp.dot(left, right, preferred_element_type=jnp.float32)


def product(high, low, value_high, value_low):
    return dot(high, value_high) + (dot(high, value_low) + dot(low, value_high))


def join(both):
    rows, width = both.shape[0] // 2, both.shape[1] // 2
    real = both[:rows, :width] - both[rows:, width:]
    imag = both[:rows, width:] + both[rows:, :width]
    return real, imag


def complex_times(high, low, value):
    return join(product(high, low, *split(value)))


def pack(real, imag):
    axis = real.ndim - 1
    lower = lax.broadcasted_iota(jnp.int32, real.shape, axis) < LANES // 2
    return (
        jnp.where(lower, real, pltpu.roll(imag, LANES // 2, axis)),
        jnp.where(lower, pltpu.roll(real, LANES // 2, axis), imag),
    )


def packed_times(high, low, value):
    rows = high.shape[1]
    both = product(high, low, *split(value))
    lower = lax.broadcasted_iota(jnp.int32, (rows, LANES), 1) < LANES // 2
    blocks = []
    for at in range(0, value.shape[1], LANES):
        turned = pltpu.roll(both[rows:, at:at + LANES], LANES // 2, 1)
        blocks.append(both[:rows, at:at + LANES] + jnp.where(lower, -turned, turned))
    return blocks


def encode(value):
    peak = jnp.max(jnp.abs(value), axis=0, keepdims=True)
    level = jnp.ceil(jnp.log2(jnp.maximum(peak * 1.0001, 1e-30)))
    levels = jnp.broadcast_to(level, (EXTRA, value.shape[1]))
    code = jnp.concatenate([jnp.round(value * jnp.exp2(15.0 - level)), levels], axis=0)
    return code.astype(jnp.int32).astype(jnp.int16)


def decode(code):
    value = code.astype(jnp.int32).astype(jnp.float32)
    rows = code.shape[0] - EXTRA
    return value[:rows] * jnp.exp2(value[rows:rows + 1] - 15.0)


def kernel(
    moms_hbm, counts_hbm, weights_hbm, vertex_hbm, source_hbm, inverse_hbm, coupling_hbm,
    solved_out, sigma_out,
    moms, counts, weights, vertex, source, inverse, coupling, left_high, left_low, own_high, own_low, pair_high, pair_low, step_high, step_low,
    driven, lent, wire, entering, greens,
    outbox, inbox, wide, formed, returned,
    load_sem, pair_send, pair_recv, lend_send, lend_recv, pass_send, hop_send, hop_recv, in_send, in_recv, out_send, out_recv,
):
    n_mom, n_tm = lax.axis_size("mom"), lax.axis_size("tm")
    me, turn = lax.axis_index("mom"), lax.axis_index("tm")
    rows, chunks = driven.shape[1], driven.shape[0] // 2
    share = rows // n_mom
    slots = moms.shape[1]
    core, plane, planes = lax.rem(turn, 2), turn // 2, n_tm // 2
    partner = turn + 1 - 2 * core
    first, behind = plane == 0, planes - 1 - plane

    def is_handed(chunk):
        from_last = (behind == 0) & (chunk < 2)
        return from_last | ((behind == 1) & (chunk == 1))

    def handed_from(slot):
        return lax.rem(slot, 2), slot // 2 + lax.rem(slot, 2)

    def slot_of(chunk):
        return chunks + behind + 2 * chunk * (1 - behind)


    loads = [
        pltpu.make_async_copy(here, there, load_sem.at[place])
        for place, (here, there) in enumerate((
            (inverse_hbm.at[:, 0, 0], inverse),
            (source_hbm.at[:, 0], source),
            (coupling_hbm.at[:, 0, 0], coupling),
            (moms_hbm, moms),
            (counts_hbm, counts),
            (weights_hbm, weights),
            (vertex_hbm, vertex),
        ))
    ]
    for load in loads:
        load.start()

    barrier = pltpu.get_barrier_semaphore()

    def greet(step, carry):
        other = lax.rem(me + step, n_mom)
        pl.semaphore_signal(barrier, inc=1, device_id={"mom": other, "tm": turn}, device_id_type=MESH)
        return carry

    lax.fori_loop(1, n_mom, greet, 0)

    for other in (partner, lax.rem(turn + 2, n_tm), lax.rem(turn + n_tm - 2, n_tm)):
        pl.semaphore_signal(barrier, inc=1, device_id={"mom": me, "tm": other}, device_id_type=MESH)

    def drive(chunk):
        columns = pl.ds(pl.multiple_of(chunk * LANES, LANES), LANES)
        forcing = jnp.concatenate([source[0, :, columns], source[1, :, columns]], axis=1)
        for half, value in enumerate(pack(*complex_times(left_high[...], left_low[...], forcing))):
            driven[2 * chunk + half] = value

    loads[0].wait()
    for part in range(2):
        high, low = split(inverse[part])
        left_high[part * rows:(part + 1) * rows, :] = high
        left_low[part * rows:(part + 1) * rows, :] = low
    loads[1].wait()
    drive(0)
    loads[2].wait()

    def keep_matrix(high_ref, low_ref, matrix):
        for part in range(2):
            high, low = split(matrix[part])
            high_ref[part * rows:(part + 1) * rows, :] = high
            low_ref[part * rows:(part + 1) * rows, :] = low

    @pl.when((plane > 0) | (core == 1))
    def _():
        keep_matrix(own_high, own_low, complex_times(
            left_high[...], left_low[...], jnp.concatenate([coupling[0], coupling[1]], axis=1)
        ))

    for load in loads[3:]:
        load.wait()

    pl.semaphore_wait(barrier, n_mom + 2)

    def to(other, src, dst, send_sem, recv_sem):
        return pltpu.make_async_remote_copy(
            src_ref=src, dst_ref=dst, send_sem=send_sem, recv_sem=recv_sem,
            device_id={"mom": me, "tm": other}, device_id_type=MESH,
        )

    def lend(piece):
        return to(partner, driven.at[piece], lent.at[piece], lend_send.at[piece], lend_recv.at[piece])

    def hop(piece):
        return to(
            lax.rem(turn + 2, n_tm), wire.at[piece], entering.at[piece], hop_send.at[piece], hop_recv.at[piece]
        )

    def forward(piece):
        return to(partner, entering.at[piece], entering.at[piece], pass_send.at[piece], hop_recv.at[piece])

    pairs = (
        to(partner, own_high, pair_high, pair_send.at[0], pair_recv.at[0]),
        to(partner, own_low, pair_low, pair_send.at[1], pair_recv.at[1]),
    )

    @pl.when(core == 0)
    def _():
        for half in range(2):
            lend(half).start()

        @pl.when(plane > 0)
        def _():
            for pair in pairs:
                pair.start()
            step_high[...] = own_high[...]
            step_low[...] = own_low[...]

        def drive_and_lend(chunk, carry):
            drive(chunk)
            for half in range(2):
                lend(2 * chunk + half).start()
            return carry

        lax.fori_loop(1, chunks, drive_and_lend, 0)

    @pl.when(core == 1)
    def _():
        def drive_rest(chunk, carry):
            drive(chunk)
            return carry

        lax.fori_loop(1, chunks, drive_rest, 0)

    @pl.when((core == 1) & (plane > 0))
    def _():
        for pair in pairs:
            pair.wait_recv()
        both = product(
            own_high[...], own_low[...],
            jnp.concatenate([pair_high[:rows, :], pair_high[rows:, :]], axis=1),
            jnp.concatenate([pair_low[:rows, :], pair_low[rows:, :]], axis=1),
        )
        keep_matrix(step_high, step_low, join(both))

    def compose(chunk):
        for half in range(2):
            lend(2 * chunk + half).wait_recv()
        value = jnp.concatenate([lent[2 * chunk], lent[2 * chunk + 1]], axis=1)
        for half, block in enumerate(packed_times(own_high[...], own_low[...], value)):
            driven[2 * chunk + half] = driven[2 * chunk + half] + block

    def send(src, dst, send_sem, recv_sem, other, there):
        pltpu.make_async_remote_copy(
            src_ref=src, dst_ref=dst, send_sem=send_sem, recv_sem=recv_sem,
            device_id={"mom": other, "tm": there}, device_id_type=MESH,
        ).start()

    def settle(block, sem):
        pltpu.make_async_copy(block, block, sem).wait()

    def others(body):
        def one(step, carry):
            body(lax.rem(me + step, n_mom))
            return carry

        return one

    def span(chunk):
        return pl.ds(pl.multiple_of(chunk * LANES, LANES), LANES)

    def advance(piece, carry):
        @pl.when(plane == 0)
        def _():
            greens[piece] = driven[piece]

        @pl.when(plane > 0)
        def _():
            hop(piece).wait_recv()

            @pl.when(core == 1)
            def _():
                forward(piece).start()

            [block] = packed_times(step_high[...], step_low[...], decode(entering[piece]))
            greens[piece] = driven[piece] + block

        @pl.when((core == 1) & (plane < planes - 1))
        def _():
            wire[piece] = encode(greens[piece])
            hop(piece).start()

        chunk, half = piece // 2, lax.rem(piece, 2)
        outbox[chunk, :, half] = greens[piece].reshape(n_mom, share, LANES).astype(jnp.bfloat16)
        given = is_handed(chunk)

        @pl.when(jnp.logical_not(given))
        def _():
            inbox[chunk, me, half] = outbox[chunk, me, half]

        def spread(part):
            @pl.when(jnp.logical_not(given))
            def _():
                for step in range(1, n_mom):
                    other = lax.rem(me + step, n_mom)
                    send(
                        outbox.at[(chunk, other, *part)], inbox.at[(chunk, me, *part)],
                        in_send.at[chunk], in_recv.at[chunk], other, turn,
                    )

            @pl.when(given)
            def _():
                slot = slot_of(chunk)
                lax.fori_loop(0, n_mom, others(lambda other: send(
                    outbox.at[(chunk, other, *part)], inbox.at[(slot, me, *part)],
                    in_send.at[chunk], in_recv.at[slot], other, core,
                )), 0)

        spread((half,))
        return carry

    def keep(chunk):
        for part, value in enumerate(pack(greens[2 * chunk], greens[2 * chunk + 1])):
            solved_out[part, :, span(chunk)] = value.astype(jnp.bfloat16)

    def form(chunk, handed):
        if handed:
            settle(inbox.at[chunk], in_recv.at[chunk])
        else:
            settle(inbox.at[chunk, pl.ds(0, n_mom - 1)], in_recv.at[chunk])

        for part, value in enumerate(pack(*(inbox[chunk, :, half].astype(jnp.float32) for half in range(2)))):
            wide[:, part * share:(part + 1) * share] = value

        def one(step, carry):
            mom = lax.rem(me + step, n_mom)
            live = counts[mom]
            total_real = jnp.zeros((share, LANES), jnp.float32)
            total_imag = jnp.zeros((share, LANES), jnp.float32)
            for slot in range(slots):
                first, second, third = (wide[moms[place, slot, mom]] for place in range(3))
                factor = jnp.where(slot < live, vertex[weights[slot, mom]], 0.0)
                ar, ai = first[:share], first[share:]
                br, bi = second[:share], second[share:]
                cr, ci = third[:share], third[share:]
                prod_real = ar * br - ai * bi
                prod_imag = ar * bi + ai * br
                total_real = total_real + factor * (prod_real * cr + prod_imag * ci)
                total_imag = total_imag + factor * (prod_imag * cr - prod_real * ci)
            formed[chunk, mom] = jnp.concatenate([total_real, total_imag], axis=0).astype(jnp.bfloat16)

            if handed:
                back, which = handed_from(chunk - chunks)
                send(
                    formed.at[chunk, mom], returned.at[which, me], out_send.at[chunk],
                    out_recv.at[which], mom, turn + 2 * (planes - 1 - back),
                )
            else:
                @pl.when(step < n_mom)
                def _():
                    send(
                        formed.at[chunk, mom], returned.at[chunk, me], out_send.at[chunk], out_recv.at[chunk], mom, turn
                    )

            return carry

        lax.fori_loop(1, n_mom + 1, one, 0)
        if not handed:
            returned[chunk, me] = formed[chunk, me]

    def finish(chunk):
        given = is_handed(chunk)

        @pl.when(given)
        def _():
            settle(returned.at[chunk], out_recv.at[chunk])

        @pl.when(jnp.logical_not(given))
        def _():
            settle(returned.at[chunk, pl.ds(0, n_mom - 1)], out_recv.at[chunk])

        value = returned[chunk].astype(jnp.float32)
        sigma_out[0, :, span(chunk)] = value[:, :share].reshape(rows, LANES)
        sigma_out[1, :, span(chunk)] = value[:, share:].reshape(rows, LANES)

    def solve(chunk, carry):
        @pl.when((core == 1) & (chunk > plane))
        def _():
            compose(chunk)

        lax.fori_loop(2 * chunk, 2 * chunk + 2, advance, 0)
        keep(chunk)
        return carry

    def form_own(chunk, carry):
        @pl.when(jnp.logical_not(is_handed(chunk)))
        def _():
            form(chunk, False)

        return carry

    def finish_own(chunk, carry):
        finish(lax.rem(chunk + (2 * plane // planes) * 2, chunks))
        return carry

    @pl.when(core == 1)
    def _():
        def compose_early(chunk, carry):
            compose(chunk)
            return carry

        lax.fori_loop(0, lax.min(chunks, plane + 1), compose_early, 0)

    lax.fori_loop(0, chunks, solve, 0)
    lax.fori_loop(0, EARLY, form_own, 0)

    @pl.when(first)
    def _():
        def form_other(place, carry):
            form(chunks + place, True)
            return carry

        lax.fori_loop(0, HANDED, form_other, 0)

    lax.fori_loop(EARLY, chunks, form_own, 0)
    lax.fori_loop(0, chunks, finish_own, 0)

    def close_piece(piece, carry):
        @pl.when(core == 0)
        def _():
            lend(piece).wait_send()

        @pl.when((core == 1) & (plane > 0))
        def _():
            forward(piece).wait_send()

        @pl.when((core == 1) & (plane < planes - 1))
        def _():
            hop(piece).wait_send()

        return carry

    lax.fori_loop(0, 2 * chunks, close_piece, 0)

    @pl.when((core == 0) & (plane > 0))
    def _():
        for pair in pairs:
            pair.wait_send()

    def close(chunk, carry):
        given = is_handed(chunk)

        @pl.when(jnp.logical_not(given))
        def _():
            settle(outbox.at[chunk, pl.ds(0, n_mom - 1)], in_send.at[chunk])

        @pl.when(given)
        def _():
            settle(outbox.at[chunk], in_send.at[chunk])

        @pl.when(jnp.logical_not(given))
        def _():
            settle(formed.at[chunk, pl.ds(0, n_mom - 1)], out_send.at[chunk])
        return carry

    lax.fori_loop(0, chunks, close, 0)

    @pl.when(first)
    def _():
        def close_other(slot, carry):
            settle(formed.at[slot], out_send.at[slot])
            return carry

        lax.fori_loop(chunks, chunks + HANDED, close_other, 0)


def write_out(solved, sigma, solved_out, sigma_out, sem):
    blocks = sem.shape[2]
    height = solved.shape[1] // blocks
    copies = []
    for place, (src, dst) in enumerate(((sigma, sigma_out), (solved, solved_out))):
        for part in range(2):
            for block in range(blocks):
                span = pl.ds(block * height, height)
                copies.append(pltpu.make_async_copy(src.at[part, span], dst.at[part, 0, span], sem.at[place, part, block]))
    for copy in copies:
        copy.start()
    for copy in copies:
        copy.wait()


def local(source, inverse_diag, coupling, pair_moms, pair_count, pair_weight, vertex):
    rows, columns = source.shape[2], source.shape[3]
    n_mom = lax.axis_size("mom")
    chunks, share = columns // LANES, rows // n_mom
    f32, bf16 = jnp.float32, jnp.bfloat16
    hbm, vmem = pl.BlockSpec(memory_space=pltpu.HBM), pl.BlockSpec(memory_space=pltpu.VMEM)
    piece = (chunks, n_mom, 2 * share, LANES)
    twice = pltpu.SemaphoreType.DMA((2 * chunks,))
    results = pl.pallas_call(
        kernel,
        out_shape=(
            pltpu.VMEM((2, rows, columns), bf16),
            pltpu.VMEM((2, rows, columns), f32),
        ),
        in_specs=[hbm] * 7,
        out_specs=(vmem, vmem),
        scratch_shapes=[
            pltpu.SMEM(pair_moms.shape[::-1], jnp.int32),
            pltpu.SMEM(pair_count.shape, jnp.int32),
            pltpu.SMEM(pair_weight.shape[::-1], jnp.int32),
            pltpu.SMEM(vertex.shape, f32),
            pltpu.VMEM((2, rows, columns), f32),
            pltpu.VMEM((2, rows, rows), f32),
            pltpu.VMEM((2, rows, rows), f32),
            *[pltpu.VMEM((2 * rows, rows), bf16) for _ in range(8)],
            pltpu.VMEM((2 * chunks, rows, LANES), f32),
            pltpu.VMEM((2 * chunks, rows, LANES), f32),
            pltpu.VMEM((2 * chunks, rows + EXTRA, LANES), jnp.int16),
            pltpu.VMEM((2 * chunks, rows + EXTRA, LANES), jnp.int16),
            pltpu.VMEM((2 * chunks, rows, LANES), f32),
            pltpu.VMEM((chunks, n_mom, 2, share, LANES), bf16),
            pltpu.VMEM((chunks + HANDED, n_mom, 2, share, LANES), bf16),
            pltpu.VMEM(piece[1:], f32),
            pltpu.VMEM((chunks + HANDED, *piece[1:]), bf16),
            pltpu.VMEM(piece, bf16),
            pltpu.SemaphoreType.DMA((7,)),
            pltpu.SemaphoreType.DMA((2,)),
            pltpu.SemaphoreType.DMA((2,)),
            twice, twice, twice, twice, twice,
            *[pltpu.SemaphoreType.DMA((chunks + extra,)) for extra in (0, HANDED, HANDED, 0)],
        ],
        compiler_params=pltpu.CompilerParams(
            collective_id=0, has_side_effects=True, vmem_limit_bytes=58 << 20
        ),
    )(
        jnp.transpose(pair_moms, (2, 1, 0)), pair_count, jnp.transpose(pair_weight, (1, 0)), vertex,
        source, inverse_diag, coupling,
    )
    return pl.pallas_call(
        write_out,
        out_shape=[jax.ShapeDtypeStruct(source.shape, dtype) for dtype in (bf16, f32)],
        in_specs=[vmem] * 2,
        out_specs=[hbm] * 2,
        scratch_shapes=[pltpu.SemaphoreType.DMA((2, 2, 4))],
        compiler_params=pltpu.CompilerParams(vmem_limit_bytes=32 << 20),
    )(*results)


def solution(mesh):
    return jax.shard_map(
        local,
        mesh=mesh,
        in_specs=(
            P(None, "mom", "tm", None),
            P(None, "mom", "tm", None, None),
            P(None, "mom", "tm", None, None),
            P(),
            P(),
            P(),
            P(),
        ),
        out_specs=(P(None, "mom", "tm", None), P(None, "mom", "tm", None)),
        check_vma=False,
    )
```

```python
import jax
import jax.numpy as jnp
from jax import lax
from jax.experimental import pallas as pl
from jax.experimental.pallas import tpu as pltpu
from jax.sharding import PartitionSpec as P

MESH = pl.DeviceIdType.MESH
LANES = 128
EXTRA = 16
HANDED = 2


def split(value):
    high = value.astype(jnp.bfloat16)
    return high, (value - high.astype(jnp.float32)).astype(jnp.bfloat16)


def dot(left, right):
    return jnp.dot(left, right, preferred_element_type=jnp.float32)


def product(high, low, value_high, value_low):
    return dot(high, value_high) + (dot(high, value_low) + dot(low, value_high))


def join(both):
    rows, width = both.shape[0] // 2, both.shape[1] // 2
    real = both[:rows, :width] - both[rows:, width:]
    imag = both[:rows, width:] + both[rows:, :width]
    return real, imag


def complex_times(high, low, value):
    return join(product(high, low, *split(value)))


def pack(real, imag):
    axis = real.ndim - 1
    lower = lax.broadcasted_iota(jnp.int32, real.shape, axis) < LANES // 2
    return (
        jnp.where(lower, real, pltpu.roll(imag, LANES // 2, axis)),
        jnp.where(lower, pltpu.roll(real, LANES // 2, axis), imag),
    )


def packed_times(high, low, value):
    rows = high.shape[1]
    both = product(high, low, *split(value))
    lower = lax.broadcasted_iota(jnp.int32, (rows, LANES), 1) < LANES // 2
    blocks = []
    for at in range(0, value.shape[1], LANES):
        turned = pltpu.roll(both[rows:, at:at + LANES], LANES // 2, 1)
        blocks.append(both[:rows, at:at + LANES] + jnp.where(lower, -turned, turned))
    return blocks


def encode(value):
    peak = jnp.max(jnp.abs(value), axis=0, keepdims=True)
    level = jnp.ceil(jnp.log2(jnp.maximum(peak * 1.0001, 1e-30)))
    levels = jnp.broadcast_to(level, (EXTRA, value.shape[1]))
    code = jnp.concatenate([jnp.round(value * jnp.exp2(15.0 - level)), levels], axis=0)
    return code.astype(jnp.int32).astype(jnp.int16)


def decode(code):
    value = code.astype(jnp.int32).astype(jnp.float32)
    rows = code.shape[0] - EXTRA
    return value[:rows] * jnp.exp2(value[rows:rows + 1] - 15.0)


def kernel(
    moms_hbm, counts_hbm, weights_hbm, vertex_hbm, source_hbm, inverse_hbm, coupling_hbm,
    solved_out, sigma_out,
    moms, counts, weights, vertex, source, inverse, coupling, left_high, left_low, own_high, own_low, pair_high, pair_low, step_high, step_low,
    driven, lent, wire, entering, greens,
    outbox, inbox, wide, formed, returned,
    load_sem, pair_send, pair_recv, lend_send, lend_recv, pass_send, hop_send, hop_recv, in_send, in_recv, out_send, out_recv,
):
    n_mom, n_tm = lax.axis_size("mom"), lax.axis_size("tm")
    me, turn = lax.axis_index("mom"), lax.axis_index("tm")
    rows, chunks = driven.shape[1], driven.shape[0] // 2
    share = rows // n_mom
    slots = moms.shape[1]
    core, plane, planes = lax.rem(turn, 2), turn // 2, n_tm // 2
    partner = turn + 1 - 2 * core
    first, behind = plane == 0, planes - 1 - plane

    def is_handed(chunk):
        from_last = (behind == 0) & (chunk == 0)
        return from_last | ((behind == 1) & (chunk == 1))

    def handed_from(slot):
        return lax.rem(slot, 2), slot // 2 + lax.rem(slot, 2)

    def slot_of(chunk):
        return chunks + behind + 2 * chunk * (1 - behind)


    loads = [
        pltpu.make_async_copy(here, there, load_sem.at[place])
        for place, (here, there) in enumerate((
            (inverse_hbm.at[:, 0, 0], inverse),
            (source_hbm.at[:, 0], source),
            (coupling_hbm.at[:, 0, 0], coupling),
            (moms_hbm, moms),
            (counts_hbm, counts),
            (weights_hbm, weights),
            (vertex_hbm, vertex),
        ))
    ]
    for load in loads:
        load.start()

    barrier = pltpu.get_barrier_semaphore()

    def greet(step, carry):
        other = lax.rem(me + step, n_mom)
        pl.semaphore_signal(barrier, inc=1, device_id={"mom": other, "tm": turn}, device_id_type=MESH)
        return carry

    lax.fori_loop(1, n_mom, greet, 0)

    for other in (partner, lax.rem(turn + 2, n_tm), lax.rem(turn + n_tm - 2, n_tm)):
        pl.semaphore_signal(barrier, inc=1, device_id={"mom": me, "tm": other}, device_id_type=MESH)

    def drive(chunk):
        columns = pl.ds(pl.multiple_of(chunk * LANES, LANES), LANES)
        forcing = jnp.concatenate([source[0, :, columns], source[1, :, columns]], axis=1)
        for half, value in enumerate(pack(*complex_times(left_high[...], left_low[...], forcing))):
            driven[2 * chunk + half] = value

    loads[0].wait()
    for part in range(2):
        high, low = split(inverse[part])
        left_high[part * rows:(part + 1) * rows, :] = high
        left_low[part * rows:(part + 1) * rows, :] = low
    loads[1].wait()
    drive(0)
    loads[2].wait()

    def keep_matrix(high_ref, low_ref, matrix):
        for part in range(2):
            high, low = split(matrix[part])
            high_ref[part * rows:(part + 1) * rows, :] = high
            low_ref[part * rows:(part + 1) * rows, :] = low

    @pl.when((plane > 0) | (core == 1))
    def _():
        keep_matrix(own_high, own_low, complex_times(
            left_high[...], left_low[...], jnp.concatenate([coupling[0], coupling[1]], axis=1)
        ))

    for load in loads[3:]:
        load.wait()

    pl.semaphore_wait(barrier, n_mom + 2)

    def to(other, src, dst, send_sem, recv_sem):
        return pltpu.make_async_remote_copy(
            src_ref=src, dst_ref=dst, send_sem=send_sem, recv_sem=recv_sem,
            device_id={"mom": me, "tm": other}, device_id_type=MESH,
        )

    def lend(piece):
        return to(partner, driven.at[piece], lent.at[piece], lend_send.at[piece], lend_recv.at[piece])

    def hop(piece):
        return to(
            lax.rem(turn + 2, n_tm), wire.at[piece], entering.at[piece], hop_send.at[piece], hop_recv.at[piece]
        )

    def forward(piece):
        return to(partner, entering.at[piece], entering.at[piece], pass_send.at[piece], hop_recv.at[piece])

    pairs = (
        to(partner, own_high, pair_high, pair_send.at[0], pair_recv.at[0]),
        to(partner, own_low, pair_low, pair_send.at[1], pair_recv.at[1]),
    )

    @pl.when(core == 0)
    def _():
        for half in range(2):
            lend(half).start()

        @pl.when(plane > 0)
        def _():
            for pair in pairs:
                pair.start()
            step_high[...] = own_high[...]
            step_low[...] = own_low[...]

        def drive_and_lend(chunk, carry):
            drive(chunk)
            for half in range(2):
                lend(2 * chunk + half).start()
            return carry

        lax.fori_loop(1, chunks, drive_and_lend, 0)

    @pl.when(core == 1)
    def _():
        def drive_rest(chunk, carry):
            drive(chunk)
            return carry

        lax.fori_loop(1, chunks, drive_rest, 0)

    @pl.when((core == 1) & (plane > 0))
    def _():
        for pair in pairs:
            pair.wait_recv()
        both = product(
            own_high[...], own_low[...],
            jnp.concatenate([pair_high[:rows, :], pair_high[rows:, :]], axis=1),
            jnp.concatenate([pair_low[:rows, :], pair_low[rows:, :]], axis=1),
        )
        keep_matrix(step_high, step_low, join(both))

    def compose(chunk):
        for half in range(2):
            lend(2 * chunk + half).wait_recv()
        value = jnp.concatenate([lent[2 * chunk], lent[2 * chunk + 1]], axis=1)
        for half, block in enumerate(packed_times(own_high[...], own_low[...], value)):
            driven[2 * chunk + half] = driven[2 * chunk + half] + block

    def send(src, dst, send_sem, recv_sem, other, there):
        pltpu.make_async_remote_copy(
            src_ref=src, dst_ref=dst, send_sem=send_sem, recv_sem=recv_sem,
            device_id={"mom": other, "tm": there}, device_id_type=MESH,
        ).start()

    def settle(block, sem):
        pltpu.make_async_copy(block, block, sem).wait()

    def others(body):
        def one(step, carry):
            body(lax.rem(me + step, n_mom))
            return carry

        return one

    def span(chunk):
        return pl.ds(pl.multiple_of(chunk * LANES, LANES), LANES)

    def advance(piece, carry):
        @pl.when(plane == 0)
        def _():
            greens[piece] = driven[piece]

        @pl.when(plane > 0)
        def _():
            hop(piece).wait_recv()

            @pl.when(core == 1)
            def _():
                forward(piece).start()

            [block] = packed_times(step_high[...], step_low[...], decode(entering[piece]))
            greens[piece] = driven[piece] + block

        @pl.when((core == 1) & (plane < planes - 1))
        def _():
            wire[piece] = encode(greens[piece])
            hop(piece).start()

        chunk, half = piece // 2, lax.rem(piece, 2)
        outbox[chunk, :, half] = greens[piece].reshape(n_mom, share, LANES).astype(jnp.bfloat16)
        given = is_handed(chunk)

        @pl.when(jnp.logical_not(given))
        def _():
            inbox[chunk, me, half] = outbox[chunk, me, half]

        def spread(part):
            @pl.when(jnp.logical_not(given))
            def _():
                for step in range(1, n_mom):
                    other = lax.rem(me + step, n_mom)
                    send(
                        outbox.at[(chunk, other, *part)], inbox.at[(chunk, me, *part)],
                        in_send.at[chunk], in_recv.at[chunk], other, turn,
                    )

            @pl.when(given)
            def _():
                slot = slot_of(chunk)
                lax.fori_loop(0, n_mom, others(lambda other: send(
                    outbox.at[(chunk, other, *part)], inbox.at[(slot, me, *part)],
                    in_send.at[chunk], in_recv.at[slot], other, core,
                )), 0)

        spread((half,))
        return carry

    def keep(chunk):
        for part, value in enumerate(pack(greens[2 * chunk], greens[2 * chunk + 1])):
            solved_out[part, :, span(chunk)] = value.astype(jnp.bfloat16)

    def form(chunk, handed):
        if handed:
            settle(inbox.at[chunk], in_recv.at[chunk])
        else:
            settle(inbox.at[chunk, pl.ds(0, n_mom - 1)], in_recv.at[chunk])

        for part, value in enumerate(pack(*(inbox[chunk, :, half].astype(jnp.float32) for half in range(2)))):
            wide[:, part * share:(part + 1) * share] = value

        def one(step, carry):
            mom = lax.rem(me + step, n_mom)
            live = counts[mom]
            total_real = jnp.zeros((share, LANES), jnp.float32)
            total_imag = jnp.zeros((share, LANES), jnp.float32)
            for slot in range(slots):
                first, second, third = (wide[moms[place, slot, mom]] for place in range(3))
                factor = jnp.where(slot < live, vertex[weights[slot, mom]], 0.0)
                ar, ai = first[:share], first[share:]
                br, bi = second[:share], second[share:]
                cr, ci = third[:share], third[share:]
                prod_real = ar * br - ai * bi
                prod_imag = ar * bi + ai * br
                total_real = total_real + factor * (prod_real * cr + prod_imag * ci)
                total_imag = total_imag + factor * (prod_imag * cr - prod_real * ci)
            formed[chunk, mom] = jnp.concatenate([total_real, total_imag], axis=0).astype(jnp.bfloat16)

            if handed:
                back, which = handed_from(chunk - chunks)
                send(
                    formed.at[chunk, mom], returned.at[which, me], out_send.at[chunk],
                    out_recv.at[which], mom, turn + 2 * (planes - 1 - back),
                )
            else:
                @pl.when(step < n_mom)
                def _():
                    send(
                        formed.at[chunk, mom], returned.at[chunk, me], out_send.at[chunk], out_recv.at[chunk], mom, turn
                    )

            return carry

        lax.fori_loop(1, n_mom + 1, one, 0)
        if not handed:
            returned[chunk, me] = formed[chunk, me]

    def finish(chunk):
        given = is_handed(chunk)

        @pl.when(given)
        def _():
            settle(returned.at[chunk], out_recv.at[chunk])

        @pl.when(jnp.logical_not(given))
        def _():
            settle(returned.at[chunk, pl.ds(0, n_mom - 1)], out_recv.at[chunk])

        value = returned[chunk].astype(jnp.float32)
        sigma_out[0, :, span(chunk)] = value[:, :share].reshape(rows, LANES)
        sigma_out[1, :, span(chunk)] = value[:, share:].reshape(rows, LANES)

    def solve(chunk, carry):
        @pl.when((core == 1) & (chunk > plane))
        def _():
            compose(chunk)

        lax.fori_loop(2 * chunk, 2 * chunk + 2, advance, 0)
        keep(chunk)
        return carry

    def form_own(chunk, carry):
        @pl.when(jnp.logical_not(is_handed(chunk)))
        def _():
            form(chunk, False)

        return carry

    def finish_own(chunk, carry):
        finish(lax.rem(chunk + (2 * plane // planes) * 2, chunks))
        return carry

    @pl.when(core == 1)
    def _():
        def compose_early(chunk, carry):
            compose(chunk)
            return carry

        lax.fori_loop(0, lax.min(chunks, plane + 1), compose_early, 0)

    lax.fori_loop(0, chunks, solve, 0)
    lax.fori_loop(0, chunks, form_own, 0)

    @pl.when(first)
    def _():
        def form_other(place, carry):
            form(chunks + place, True)
            return carry

        lax.fori_loop(0, HANDED, form_other, 0)

    lax.fori_loop(0, chunks, finish_own, 0)

    def close_piece(piece, carry):
        @pl.when(core == 0)
        def _():
            lend(piece).wait_send()

        @pl.when((core == 1) & (plane > 0))
        def _():
            forward(piece).wait_send()

        @pl.when((core == 1) & (plane < planes - 1))
        def _():
            hop(piece).wait_send()

        return carry

    lax.fori_loop(0, 2 * chunks, close_piece, 0)

    @pl.when((core == 0) & (plane > 0))
    def _():
        for pair in pairs:
            pair.wait_send()

    def close(chunk, carry):
        given = is_handed(chunk)

        @pl.when(jnp.logical_not(given))
        def _():
            settle(outbox.at[chunk, pl.ds(0, n_mom - 1)], in_send.at[chunk])

        @pl.when(given)
        def _():
            settle(outbox.at[chunk], in_send.at[chunk])

        @pl.when(jnp.logical_not(given))
        def _():
            settle(formed.at[chunk, pl.ds(0, n_mom - 1)], out_send.at[chunk])
        return carry

    lax.fori_loop(0, chunks, close, 0)

    @pl.when(first)
    def _():
        def close_other(slot, carry):
            settle(formed.at[slot], out_send.at[slot])
            return carry

        lax.fori_loop(chunks, chunks + HANDED, close_other, 0)


def write_out(solved, sigma, solved_out, sigma_out, sem):
    blocks = sem.shape[2]
    height = solved.shape[1] // blocks
    copies = []
    for place, (src, dst) in enumerate(((sigma, sigma_out), (solved, solved_out))):
        for part in range(2):
            for block in range(blocks):
                span = pl.ds(block * height, height)
                copies.append(pltpu.make_async_copy(src.at[part, span], dst.at[part, 0, span], sem.at[place, part, block]))
    for copy in copies:
        copy.start()
    for copy in copies:
        copy.wait()


def local(source, inverse_diag, coupling, pair_moms, pair_count, pair_weight, vertex):
    rows, columns = source.shape[2], source.shape[3]
    n_mom = lax.axis_size("mom")
    chunks, share = columns // LANES, rows // n_mom
    f32, bf16 = jnp.float32, jnp.bfloat16
    hbm, vmem = pl.BlockSpec(memory_space=pltpu.HBM), pl.BlockSpec(memory_space=pltpu.VMEM)
    piece = (chunks, n_mom, 2 * share, LANES)
    twice = pltpu.SemaphoreType.DMA((2 * chunks,))
    results = pl.pallas_call(
        kernel,
        out_shape=(
            pltpu.VMEM((2, rows, columns), bf16),
            pltpu.VMEM((2, rows, columns), f32),
        ),
        in_specs=[hbm] * 7,
        out_specs=(vmem, vmem),
        scratch_shapes=[
            pltpu.SMEM(pair_moms.shape[::-1], jnp.int32),
            pltpu.SMEM(pair_count.shape, jnp.int32),
            pltpu.SMEM(pair_weight.shape[::-1], jnp.int32),
            pltpu.SMEM(vertex.shape, f32),
            pltpu.VMEM((2, rows, columns), f32),
            pltpu.VMEM((2, rows, rows), f32),
            pltpu.VMEM((2, rows, rows), f32),
            *[pltpu.VMEM((2 * rows, rows), bf16) for _ in range(8)],
            pltpu.VMEM((2 * chunks, rows, LANES), f32),
            pltpu.VMEM((2 * chunks, rows, LANES), f32),
            pltpu.VMEM((2 * chunks, rows + EXTRA, LANES), jnp.int16),
            pltpu.VMEM((2 * chunks, rows + EXTRA, LANES), jnp.int16),
            pltpu.VMEM((2 * chunks, rows, LANES), f32),
            pltpu.VMEM((chunks, n_mom, 2, share, LANES), bf16),
            pltpu.VMEM((chunks + HANDED, n_mom, 2, share, LANES), bf16),
            pltpu.VMEM(piece[1:], f32),
            pltpu.VMEM((chunks + HANDED, *piece[1:]), bf16),
            pltpu.VMEM(piece, bf16),
            pltpu.SemaphoreType.DMA((7,)),
            pltpu.SemaphoreType.DMA((2,)),
            pltpu.SemaphoreType.DMA((2,)),
            twice, twice, twice, twice, twice,
            *[pltpu.SemaphoreType.DMA((chunks + extra,)) for extra in (0, HANDED, HANDED, 0)],
        ],
        compiler_params=pltpu.CompilerParams(
            collective_id=0, has_side_effects=True, vmem_limit_bytes=58 << 20
        ),
    )(
        jnp.transpose(pair_moms, (2, 1, 0)), pair_count, jnp.transpose(pair_weight, (1, 0)), vertex,
        source, inverse_diag, coupling,
    )
    return pl.pallas_call(
        write_out,
        out_shape=[jax.ShapeDtypeStruct(source.shape, dtype) for dtype in (bf16, f32)],
        in_specs=[vmem] * 2,
        out_specs=[hbm] * 2,
        scratch_shapes=[pltpu.SemaphoreType.DMA((2, 2, 4))],
        compiler_params=pltpu.CompilerParams(vmem_limit_bytes=32 << 20),
    )(*results)


def solution(mesh):
    return jax.shard_map(
        local,
        mesh=mesh,
        in_specs=(
            P(None, "mom", "tm", None),
            P(None, "mom", "tm", None, None),
            P(None, "mom", "tm", None, None),
            P(),
            P(),
            P(),
            P(),
        ),
        out_specs=(P(None, "mom", "tm", None), P(None, "mom", "tm", None)),
        check_vma=False,
    )
```

```python
import jax
import jax.numpy as jnp
from jax import lax
from jax.experimental import pallas as pl
from jax.experimental.pallas import tpu as pltpu
from jax.sharding import PartitionSpec as P

MESH = pl.DeviceIdType.MESH
LANES = 128
EXTRA = 16
HANDED = 2


def split(value):
    high = value.astype(jnp.bfloat16)
    return high, (value - high.astype(jnp.float32)).astype(jnp.bfloat16)


def dot(left, right):
    return jnp.dot(left, right, preferred_element_type=jnp.float32)


def product(high, low, value_high, value_low):
    return dot(high, value_high) + (dot(high, value_low) + dot(low, value_high))


def join(both):
    rows, width = both.shape[0] // 2, both.shape[1] // 2
    real = both[:rows, :width] - both[rows:, width:]
    imag = both[:rows, width:] + both[rows:, :width]
    return real, imag


def complex_times(high, low, value):
    return join(product(high, low, *split(value)))


def pack(real, imag):
    axis = real.ndim - 1
    lower = lax.broadcasted_iota(jnp.int32, real.shape, axis) < LANES // 2
    return (
        jnp.where(lower, real, pltpu.roll(imag, LANES // 2, axis)),
        jnp.where(lower, pltpu.roll(real, LANES // 2, axis), imag),
    )


def packed_times(high, low, value):
    rows = high.shape[1]
    both = product(high, low, *split(value))
    lower = lax.broadcasted_iota(jnp.int32, (rows, LANES), 1) < LANES // 2
    blocks = []
    for at in range(0, value.shape[1], LANES):
        turned = pltpu.roll(both[rows:, at:at + LANES], LANES // 2, 1)
        blocks.append(both[:rows, at:at + LANES] + jnp.where(lower, -turned, turned))
    return blocks


def encode(value):
    peak = jnp.max(jnp.abs(value), axis=0, keepdims=True)
    level = jnp.ceil(jnp.log2(jnp.maximum(peak * 1.0001, 1e-30)))
    levels = jnp.broadcast_to(level, (EXTRA, value.shape[1]))
    code = jnp.concatenate([jnp.round(value * jnp.exp2(15.0 - level)), levels], axis=0)
    return code.astype(jnp.int32).astype(jnp.int16)


def decode(code):
    value = code.astype(jnp.int32).astype(jnp.float32)
    rows = code.shape[0] - EXTRA
    return value[:rows] * jnp.exp2(value[rows:rows + 1] - 15.0)


def kernel(
    moms_hbm, counts_hbm, weights_hbm, vertex_hbm, source_hbm, inverse_hbm, coupling_hbm,
    solved_out, sigma_out,
    moms, counts, weights, vertex, source, inverse, coupling, left_high, left_low, own_high, own_low, pair_high, pair_low, step_high, step_low,
    driven, lent, wire, entering, greens,
    outbox, inbox, wide, formed, returned,
    load_sem, pair_send, pair_recv, lend_send, lend_recv, pass_send, hop_send, hop_recv, in_send, in_recv, out_send, out_recv,
):
    n_mom, n_tm = lax.axis_size("mom"), lax.axis_size("tm")
    me, turn = lax.axis_index("mom"), lax.axis_index("tm")
    rows, chunks = driven.shape[1], driven.shape[0] // 2
    share = rows // n_mom
    slots = moms.shape[1]
    core, plane, planes = lax.rem(turn, 2), turn // 2, n_tm // 2
    partner = turn + 1 - 2 * core
    first, behind = plane == 0, planes - 1 - plane

    def is_handed(chunk):
        from_last = (behind == 0) & (chunk == 0)
        return from_last | ((behind == 1) & (chunk == 1))

    def handed_from(slot):
        return lax.rem(slot, 2), slot // 2 + lax.rem(slot, 2)

    def slot_of(chunk):
        return chunks + behind + 2 * chunk * (1 - behind)


    loads = [
        pltpu.make_async_copy(here, there, load_sem.at[place])
        for place, (here, there) in enumerate((
            (inverse_hbm.at[:, 0, 0], inverse),
            (source_hbm.at[:, 0], source),
            (coupling_hbm.at[:, 0, 0], coupling),
            (moms_hbm, moms),
            (counts_hbm, counts),
            (weights_hbm, weights),
            (vertex_hbm, vertex),
        ))
    ]
    for load in loads:
        load.start()

    barrier = pltpu.get_barrier_semaphore()

    def greet(step, carry):
        other = lax.rem(me + step, n_mom)
        pl.semaphore_signal(barrier, inc=1, device_id={"mom": other, "tm": turn}, device_id_type=MESH)
        return carry

    lax.fori_loop(1, n_mom, greet, 0)

    for other in (partner, lax.rem(turn + 2, n_tm), lax.rem(turn + n_tm - 2, n_tm)):
        pl.semaphore_signal(barrier, inc=1, device_id={"mom": me, "tm": other}, device_id_type=MESH)

    def drive(chunk):
        columns = pl.ds(pl.multiple_of(chunk * LANES, LANES), LANES)
        forcing = jnp.concatenate([source[0, :, columns], source[1, :, columns]], axis=1)
        for half, value in enumerate(pack(*complex_times(left_high[...], left_low[...], forcing))):
            driven[2 * chunk + half] = value

    loads[0].wait()
    for part in range(2):
        high, low = split(inverse[part])
        left_high[part * rows:(part + 1) * rows, :] = high
        left_low[part * rows:(part + 1) * rows, :] = low
    loads[1].wait()
    drive(0)
    loads[2].wait()

    def keep_matrix(high_ref, low_ref, matrix):
        for part in range(2):
            high, low = split(matrix[part])
            high_ref[part * rows:(part + 1) * rows, :] = high
            low_ref[part * rows:(part + 1) * rows, :] = low

    @pl.when((plane > 0) | (core == 1))
    def _():
        keep_matrix(own_high, own_low, complex_times(
            left_high[...], left_low[...], jnp.concatenate([coupling[0], coupling[1]], axis=1)
        ))

    for load in loads[3:]:
        load.wait()

    pl.semaphore_wait(barrier, n_mom + 2)

    def to(other, src, dst, send_sem, recv_sem):
        return pltpu.make_async_remote_copy(
            src_ref=src, dst_ref=dst, send_sem=send_sem, recv_sem=recv_sem,
            device_id={"mom": me, "tm": other}, device_id_type=MESH,
        )

    def lend(piece):
        return to(partner, driven.at[piece], lent.at[piece], lend_send.at[piece], lend_recv.at[piece])

    def hop(piece):
        return to(
            lax.rem(turn + 2, n_tm), wire.at[piece], entering.at[piece], hop_send.at[piece], hop_recv.at[piece]
        )

    def forward(piece):
        return to(partner, entering.at[piece], entering.at[piece], pass_send.at[piece], hop_recv.at[piece])

    pairs = (
        to(partner, own_high, pair_high, pair_send.at[0], pair_recv.at[0]),
        to(partner, own_low, pair_low, pair_send.at[1], pair_recv.at[1]),
    )

    @pl.when(core == 0)
    def _():
        for half in range(2):
            lend(half).start()

        @pl.when(plane > 0)
        def _():
            for pair in pairs:
                pair.start()
            step_high[...] = own_high[...]
            step_low[...] = own_low[...]

        def drive_and_lend(chunk, carry):
            drive(chunk)
            for half in range(2):
                lend(2 * chunk + half).start()
            return carry

        lax.fori_loop(1, chunks, drive_and_lend, 0)

    @pl.when(core == 1)
    def _():
        def drive_rest(chunk, carry):
            drive(chunk)
            return carry

        lax.fori_loop(1, chunks, drive_rest, 0)

    @pl.when((core == 1) & (plane > 0))
    def _():
        for pair in pairs:
            pair.wait_recv()
        both = product(
            own_high[...], own_low[...],
            jnp.concatenate([pair_high[:rows, :], pair_high[rows:, :]], axis=1),
            jnp.concatenate([pair_low[:rows, :], pair_low[rows:, :]], axis=1),
        )
        keep_matrix(step_high, step_low, join(both))

    def compose(chunk):
        for half in range(2):
            lend(2 * chunk + half).wait_recv()
        value = jnp.concatenate([lent[2 * chunk], lent[2 * chunk + 1]], axis=1)
        for half, block in enumerate(packed_times(own_high[...], own_low[...], value)):
            driven[2 * chunk + half] = driven[2 * chunk + half] + block

    def send(src, dst, send_sem, recv_sem, other, there):
        pltpu.make_async_remote_copy(
            src_ref=src, dst_ref=dst, send_sem=send_sem, recv_sem=recv_sem,
            device_id={"mom": other, "tm": there}, device_id_type=MESH,
        ).start()

    def settle(block, sem):
        pltpu.make_async_copy(block, block, sem).wait()

    def span(chunk):
        return pl.ds(pl.multiple_of(chunk * LANES, LANES), LANES)

    def advance(piece, carry):
        @pl.when(plane == 0)
        def _():
            greens[piece] = driven[piece]

        @pl.when(plane > 0)
        def _():
            hop(piece).wait_recv()

            @pl.when(core == 1)
            def _():
                forward(piece).start()

            [block] = packed_times(step_high[...], step_low[...], decode(entering[piece]))
            greens[piece] = driven[piece] + block

        @pl.when((core == 1) & (plane < planes - 1))
        def _():
            wire[piece] = encode(greens[piece])
            hop(piece).start()

        chunk, half = piece // 2, lax.rem(piece, 2)
        outbox[chunk, :, half] = greens[piece].reshape(n_mom, share, LANES).astype(jnp.bfloat16)
        given = is_handed(chunk)

        @pl.when(jnp.logical_not(given))
        def _():
            inbox[chunk, me, half] = outbox[chunk, me, half]

        def spread(part):
            @pl.when(jnp.logical_not(given))
            def _():
                for step in range(1, n_mom):
                    other = lax.rem(me + step, n_mom)
                    send(
                        outbox.at[(chunk, other, *part)], inbox.at[(chunk, me, *part)],
                        in_send.at[chunk], in_recv.at[chunk], other, turn,
                    )

            @pl.when(given)
            def _():
                slot = slot_of(chunk)
                for step in range(n_mom):
                    other = lax.rem(me + step, n_mom)
                    send(
                        outbox.at[(chunk, other, *part)], inbox.at[(slot, me, *part)],
                        in_send.at[chunk], in_recv.at[slot], other, core,
                    )

        spread((half,))
        return carry

    def keep(chunk):
        for part, value in enumerate(pack(greens[2 * chunk], greens[2 * chunk + 1])):
            solved_out[part, :, span(chunk)] = value.astype(jnp.bfloat16)

    def form(chunk, handed):
        if handed:
            settle(inbox.at[chunk], in_recv.at[chunk])
        else:
            settle(inbox.at[chunk, pl.ds(0, n_mom - 1)], in_recv.at[chunk])

        for part, value in enumerate(pack(*(inbox[chunk, :, half].astype(jnp.float32) for half in range(2)))):
            wide[:, part * share:(part + 1) * share] = value

        def one(step, carry):
            mom = lax.rem(me + step, n_mom)
            live = counts[mom]
            total_real = jnp.zeros((share, LANES), jnp.float32)
            total_imag = jnp.zeros((share, LANES), jnp.float32)
            for slot in range(slots):
                first, second, third = (wide[moms[place, slot, mom]] for place in range(3))
                factor = jnp.where(slot < live, vertex[weights[slot, mom]], 0.0)
                ar, ai = first[:share], first[share:]
                br, bi = second[:share], second[share:]
                cr, ci = third[:share], third[share:]
                prod_real = ar * br - ai * bi
                prod_imag = ar * bi + ai * br
                total_real = total_real + factor * (prod_real * cr + prod_imag * ci)
                total_imag = total_imag + factor * (prod_imag * cr - prod_real * ci)
            formed[chunk, mom] = jnp.concatenate([total_real, total_imag], axis=0).astype(jnp.bfloat16)

            if handed:
                back, which = handed_from(chunk - chunks)
                send(
                    formed.at[chunk, mom], returned.at[which, me], out_send.at[chunk],
                    out_recv.at[which], mom, turn + 2 * (planes - 1 - back),
                )
            else:
                @pl.when(step < n_mom)
                def _():
                    send(
                        formed.at[chunk, mom], returned.at[chunk, me], out_send.at[chunk], out_recv.at[chunk], mom, turn
                    )

            return carry

        lax.fori_loop(1, n_mom + 1, one, 0)
        if not handed:
            returned[chunk, me] = formed[chunk, me]

    def finish(chunk):
        given = is_handed(chunk)

        @pl.when(given)
        def _():
            settle(returned.at[chunk], out_recv.at[chunk])

        @pl.when(jnp.logical_not(given))
        def _():
            settle(returned.at[chunk, pl.ds(0, n_mom - 1)], out_recv.at[chunk])

        value = returned[chunk].astype(jnp.float32)
        sigma_out[0, :, span(chunk)] = value[:, :share].reshape(rows, LANES)
        sigma_out[1, :, span(chunk)] = value[:, share:].reshape(rows, LANES)

    def solve(chunk, carry):
        @pl.when((core == 1) & (chunk > plane))
        def _():
            compose(chunk)

        lax.fori_loop(2 * chunk, 2 * chunk + 2, advance, 0)
        keep(chunk)
        return carry

    def form_own(chunk, carry):
        @pl.when(jnp.logical_not(is_handed(chunk)))
        def _():
            form(chunk, False)

        return carry

    def finish_own(chunk, carry):
        finish(lax.rem(chunk + (2 * plane // planes) * 2, chunks))
        return carry

    @pl.when(core == 1)
    def _():
        def compose_early(chunk, carry):
            compose(chunk)
            return carry

        lax.fori_loop(0, lax.min(chunks, plane + 1), compose_early, 0)

    lax.fori_loop(0, chunks, solve, 0)
    lax.fori_loop(0, chunks, form_own, 0)

    @pl.when(first)
    def _():
        def form_other(place, carry):
            form(chunks + place, True)
            return carry

        lax.fori_loop(0, HANDED, form_other, 0)

    lax.fori_loop(0, chunks, finish_own, 0)

    def close_piece(piece, carry):
        @pl.when(core == 0)
        def _():
            lend(piece).wait_send()

        @pl.when((core == 1) & (plane > 0))
        def _():
            forward(piece).wait_send()

        @pl.when((core == 1) & (plane < planes - 1))
        def _():
            hop(piece).wait_send()

        return carry

    lax.fori_loop(0, 2 * chunks, close_piece, 0)

    @pl.when((core == 0) & (plane > 0))
    def _():
        for pair in pairs:
            pair.wait_send()

    def close(chunk, carry):
        given = is_handed(chunk)

        @pl.when(jnp.logical_not(given))
        def _():
            settle(outbox.at[chunk, pl.ds(0, n_mom - 1)], in_send.at[chunk])

        @pl.when(given)
        def _():
            settle(outbox.at[chunk], in_send.at[chunk])

        @pl.when(jnp.logical_not(given))
        def _():
            settle(formed.at[chunk, pl.ds(0, n_mom - 1)], out_send.at[chunk])
        return carry

    lax.fori_loop(0, chunks, close, 0)

    @pl.when(first)
    def _():
        def close_other(slot, carry):
            settle(formed.at[slot], out_send.at[slot])
            return carry

        lax.fori_loop(chunks, chunks + HANDED, close_other, 0)


def write_out(solved, sigma, solved_out, sigma_out, sem):
    blocks = sem.shape[2]
    height = solved.shape[1] // blocks
    copies = []
    for place, (src, dst) in enumerate(((sigma, sigma_out), (solved, solved_out))):
        for part in range(2):
            for block in range(blocks):
                span = pl.ds(block * height, height)
                copies.append(pltpu.make_async_copy(src.at[part, span], dst.at[part, 0, span], sem.at[place, part, block]))
    for copy in copies:
        copy.start()
    for copy in copies:
        copy.wait()


def local(source, inverse_diag, coupling, pair_moms, pair_count, pair_weight, vertex):
    rows, columns = source.shape[2], source.shape[3]
    n_mom = lax.axis_size("mom")
    chunks, share = columns // LANES, rows // n_mom
    f32, bf16 = jnp.float32, jnp.bfloat16
    hbm, vmem = pl.BlockSpec(memory_space=pltpu.HBM), pl.BlockSpec(memory_space=pltpu.VMEM)
    piece = (chunks, n_mom, 2 * share, LANES)
    twice = pltpu.SemaphoreType.DMA((2 * chunks,))
    results = pl.pallas_call(
        kernel,
        out_shape=(
            pltpu.VMEM((2, rows, columns), bf16),
            pltpu.VMEM((2, rows, columns), f32),
        ),
        in_specs=[hbm] * 7,
        out_specs=(vmem, vmem),
        scratch_shapes=[
            pltpu.SMEM(pair_moms.shape[::-1], jnp.int32),
            pltpu.SMEM(pair_count.shape, jnp.int32),
            pltpu.SMEM(pair_weight.shape[::-1], jnp.int32),
            pltpu.SMEM(vertex.shape, f32),
            pltpu.VMEM((2, rows, columns), f32),
            pltpu.VMEM((2, rows, rows), f32),
            pltpu.VMEM((2, rows, rows), f32),
            *[pltpu.VMEM((2 * rows, rows), bf16) for _ in range(8)],
            pltpu.VMEM((2 * chunks, rows, LANES), f32),
            pltpu.VMEM((2 * chunks, rows, LANES), f32),
            pltpu.VMEM((2 * chunks, rows + EXTRA, LANES), jnp.int16),
            pltpu.VMEM((2 * chunks, rows + EXTRA, LANES), jnp.int16),
            pltpu.VMEM((2 * chunks, rows, LANES), f32),
            pltpu.VMEM((chunks, n_mom, 2, share, LANES), bf16),
            pltpu.VMEM((chunks + HANDED, n_mom, 2, share, LANES), bf16),
            pltpu.VMEM(piece[1:], f32),
            pltpu.VMEM((chunks + HANDED, *piece[1:]), bf16),
            pltpu.VMEM(piece, bf16),
            pltpu.SemaphoreType.DMA((7,)),
            pltpu.SemaphoreType.DMA((2,)),
            pltpu.SemaphoreType.DMA((2,)),
            twice, twice, twice, twice, twice,
            *[pltpu.SemaphoreType.DMA((chunks + extra,)) for extra in (0, HANDED, HANDED, 0)],
        ],
        compiler_params=pltpu.CompilerParams(
            collective_id=0, has_side_effects=True, vmem_limit_bytes=58 << 20
        ),
    )(
        jnp.transpose(pair_moms, (2, 1, 0)), pair_count, jnp.transpose(pair_weight, (1, 0)), vertex,
        source, inverse_diag, coupling,
    )
    return pl.pallas_call(
        write_out,
        out_shape=[jax.ShapeDtypeStruct(source.shape, dtype) for dtype in (bf16, f32)],
        in_specs=[vmem] * 2,
        out_specs=[hbm] * 2,
        scratch_shapes=[pltpu.SemaphoreType.DMA((2, 2, 4))],
        compiler_params=pltpu.CompilerParams(vmem_limit_bytes=32 << 20),
    )(*results)


def solution(mesh):
    return jax.shard_map(
        local,
        mesh=mesh,
        in_specs=(
            P(None, "mom", "tm", None),
            P(None, "mom", "tm", None, None),
            P(None, "mom", "tm", None, None),
            P(),
            P(),
            P(),
            P(),
        ),
        out_specs=(P(None, "mom", "tm", None), P(None, "mom", "tm", None)),
        check_vma=False,
    )
```
